256 devices in a mesh: grp: 4 (over x), dev: 64 (over z, y, core).
Axes of the slice: x: 4, y: 4, z: 8, core: 2. Of those that a mesh axis runs over, the one named last changes fastest.
Arguments:
- token_ids: int32 [1024, 128], P(('grp', 'dev')), may hold values from 0 to 128255, as said below
- sensitivity: bfloat16 [1024, 128, 4096], P(('grp', 'dev')), may hold values from -6 to 6
- last_hidden: bfloat16 [1024, 4096], P(('grp', 'dev')), may hold values from -6 to 6
- lengths: int32 [1024], P(('grp', 'dev')), may hold values from 97 to 128
- norm_gain: float32 [4096], replicated, may hold values from 0.25 to 1.75
- reward_head: float32 [4096], replicated, may hold values from -0.09375 to 0.09375
- chosen_index: int32 [512], replicated, may hold values from 0 to 1023, as said below
- rejected_index: int32 [512], replicated, may hold values from 0 to 1023, as said below
- shard_owner: int32 [256], replicated, may hold values from 0 to 255, each once
Outputs:
- owned_grad: bfloat16 [128256, 4096], P(('grp', 'dev'))
- head_grad: float32 [4096], P(('grp', 'dev'))
The draws below stay inside these ranges and needn't reach their ends.
Inputs may be any that keep to these rules, and one draw needn't show every extreme that they name: `token_ids`: within the token slots of one device, at most 4 ids fall in any one vocabulary shard of 501 rows, and on every device some shard gets exactly 4. chosen_index and rejected_index together name every response exactly once. `rejected_index`: see chosen_index.
All inputs are finite; a program needn't handle non-finite values.
Results may differ from the reference program's by a relative error of at most 0.0042.
Values may be sent and summed in bfloat16 or wider, within the bound.
No kernel may reach another device: no remote copies, remote signals or barrier semaphores. Data moves between devices by JAX's collectives and lax.ppermute only.
A program may use at most 64 MiB of HBM per device.

```python
import jax
import jax.numpy as jnp
from jax import lax

D = 4096
VOCAB = 128256
BLOCK = 128
RESP_DEV = 4
TOK_DEV = 512
RESPONSES = 1024
PAIRS = 512
SHARD = 501
CAP = 4
DEVICES = 256


def pair_split(key):
    order = jax.random.permutation(jax.random.fold_in(key, 7), RESPONSES).astype(jnp.int32)
    return (order[:PAIRS], order[PAIRS:])


def draw_chosen_index(key, part):
    return pair_split(key)[0]


def draw_rejected_index(key, part):
    return pair_split(key)[1]


def draw_token_ids(key, part):
    total = DEVICES * CAP

    def one_device(dev_key):
        key_first, key_order, key_shuffle, key_offset = jax.random.split(dev_key, 4)
        labels = jnp.arange(total, dtype=jnp.int32) // CAP
        within = jnp.arange(total, dtype=jnp.int32) % CAP
        first = jax.random.randint(key_first, (), 0, DEVICES, dtype=jnp.int32)
        order = jax.random.permutation(key_order, total).astype(jnp.int32)
        score = jnp.where(labels == first, within - CAP, order)
        picked = jnp.argsort(score, stable=True)[:TOK_DEV]
        shards = jax.random.permutation(key_shuffle, labels[picked])
        offset = jax.random.randint(key_offset, (TOK_DEV,), 0, SHARD, dtype=jnp.int32)
        return (shards * SHARD + offset).astype(jnp.int32)
    keys = jax.random.split(jax.random.fold_in(key, 11), DEVICES)
    return jax.vmap(one_device)(keys).reshape(RESPONSES, BLOCK)


def set_ends(drawn, stream_key, low, top_value):
    longest = drawn.shape.index(max(drawn.shape))
    spots = []
    for shift in (0, 1):
        where = [jax.random.randint(jax.random.fold_in(stream_key, axis), (), 0, length) for axis, length in enumerate(drawn.shape)]
        where[longest] = (where[longest] + shift) % drawn.shape[longest]
        spots.append(tuple(where))
    return drawn.at[spots[0]].set(low).at[spots[1]].set(top_value)


def level_of(own_key, extent, cuts, smallest, largest):
    loudness = 1.0
    for axis_at, parts in cuts:
        draws = jax.random.uniform(jax.random.fold_in(jax.random.fold_in(own_key, 6), axis_at), (parts,), jnp.float32, smallest / len(cuts), largest / len(cuts))
        loudness = loudness * jnp.repeat(jnp.exp(draws), extent[axis_at] // parts).reshape((-1,) + (1,) * (len(extent) - 1 - axis_at))
    return loudness


def normal_values(rng, dims, width, limit, cuts=(), held_as=jnp.bfloat16):
    result = jax.random.normal(rng, dims, jnp.float32) * width
    if len(cuts) > 0:
        result = level_of(rng, dims, cuts, -0.22, 0.18) * result
    return jnp.clip(result, min=-limit, max=limit).astype(held_as)


def setup_inputs(seed: int = 0) -> dict:
    arg_keys = jax.random.split(jax.random.key(seed), 10)
    token_ids = draw_token_ids(jax.random.fold_in(arg_keys[9], 71), 0)
    sensitivity = normal_values(arg_keys[1], (RESPONSES, BLOCK, D), 1.0, 6.0, ((0, 256),))
    last_hidden = normal_values(arg_keys[2], (RESPONSES, D), 1.0, 6.0, ((0, 256),))
    lengths = set_ends(jax.random.randint(arg_keys[3], (RESPONSES,), BLOCK - BLOCK // 4 + 1, BLOCK + 1), jax.random.fold_in(arg_keys[3], 1), BLOCK - BLOCK // 4 + 1, BLOCK).astype(jnp.int32)
    norm_gain = jnp.clip(1.0 + 0.15 * jax.random.normal(arg_keys[4], (D,), jnp.float32), 0.25, 1.75)
    reward_head = normal_values(arg_keys[5], (D,), D ** -0.5, 0.09375, (), jnp.float32)
    chosen_index = draw_chosen_index(jax.random.fold_in(arg_keys[9], 71), 0)
    rejected_index = draw_rejected_index(jax.random.fold_in(arg_keys[9], 71), 0)
    shard_owner = jax.random.permutation(arg_keys[8], DEVICES).astype(jnp.int32)
    return {"token_ids": token_ids, "sensitivity": sensitivity, "last_hidden": last_hidden, "lengths": lengths, "norm_gain": norm_gain, "reward_head": reward_head, "chosen_index": chosen_index, "rejected_index": rejected_index, "shard_owner": shard_owner}


def reference(token_ids, sensitivity, last_hidden, lengths, norm_gain, reward_head, chosen_index, rejected_index, shard_owner):
    hidden = last_hidden.astype(jnp.float32)
    normed = hidden / jnp.sqrt(lax.optimization_barrier(jnp.mean(hidden * hidden, axis=-1, keepdims=True)) + 1e-05) * norm_gain
    reward = lax.optimization_barrier(jnp.sum(normed * reward_head, axis=-1))
    margin = reward[chosen_index] - reward[rejected_index]
    push = -jax.nn.sigmoid(-margin)
    reward_grad = jnp.zeros((RESPONSES,), jnp.float32).at[chosen_index].add(push).at[rejected_index].add(-push)
    head_grad = lax.optimization_barrier(jnp.sum(reward_grad[:, None] * normed, axis=0))
    slots = jnp.arange(BLOCK, dtype=jnp.int32)
    live = slots[None, :] < lengths[:, None]
    scale_all = jnp.where(live, reward_grad[:, None], jnp.float32(0.0))
    ids_dev = token_ids.reshape(DEVICES, RESP_DEV * BLOCK)
    sens_dev = sensitivity.reshape(DEVICES, RESP_DEV * BLOCK, D)
    scale_dev = scale_all.reshape(DEVICES, RESP_DEV * BLOCK)

    def accumulate(table, items):
        ids, sens, scale = items
        rows = (scale[:, None] * sens.astype(jnp.float32)).astype(jnp.bfloat16)
        return (table.at[ids].add(rows.astype(jnp.float32)), None)
    table = jnp.zeros((VOCAB, D), jnp.float32)
    table, _ = lax.scan(accumulate, table, (ids_dev, sens_dev, scale_dev))
    inverse = jnp.argsort(shard_owner).astype(jnp.int32)
    owned = table.reshape(DEVICES, SHARD, D)[inverse].reshape(VOCAB, D)
    return (owned.astype(jnp.bfloat16), head_grad)
```

```python
import jax
import jax.numpy as jnp
from jax import lax
from jax.experimental import pallas as pl
from jax.experimental.pallas import tpu as pltpu
from jax.sharding import Mesh
from jax.sharding import PartitionSpec as P

VOCAB = 128256
CAP = 4
GRP_DEV = ("grp", "dev_0", "dev_1", "dev_2")


def pack_kernel(slot_ref, rows_ref, out_ref):
    slots, cap, width = out_ref.shape
    tokens = slot_ref.shape[1]
    hot = jax.lax.broadcasted_iota(jnp.int32, (slots * cap, tokens), 0) == slot_ref[...]
    picked = jnp.dot(
        hot.astype(jnp.bfloat16), rows_ref[...], preferred_element_type=jnp.float32
    )
    out_ref[...] = picked.reshape(slots, cap, width).astype(jnp.bfloat16)


def packed_rows(slot, rows, devices, block):
    tokens, width = rows.shape
    return pl.pallas_call(
        pack_kernel,
        out_shape=jax.ShapeDtypeStruct((devices, CAP, width), jnp.bfloat16),
        grid=(width // block,),
        in_specs=[
            pl.BlockSpec((1, tokens), lambda j: (0, 0)),
            pl.BlockSpec((tokens, block), lambda j: (0, j)),
        ],
        out_specs=pl.BlockSpec((devices, CAP, block), lambda j: (0, 0, j)),
        compiler_params=pltpu.CompilerParams(vmem_limit_bytes=48 << 20),
        cost_estimate=pl.CostEstimate(
            flops=2 * devices * CAP * tokens * width,
            bytes_accessed=2 * (tokens + devices * CAP) * width,
            transcendentals=0,
        ),
    )(slot, rows)


def place_kernel(target_ref, scale_ref, rows_ref, out_ref):
    slots, cap, width = rows_ref.shape
    rows = rows_ref[...].astype(jnp.float32).reshape(slots * cap, width)
    scaled = (scale_ref[...] * rows).astype(jnp.bfloat16)
    hot = jax.lax.broadcasted_iota(jnp.int32, (out_ref.shape[0], slots * cap), 0) == target_ref[...]
    out_ref[...] = jnp.dot(
        hot.astype(jnp.bfloat16), scaled, preferred_element_type=jnp.float32
    ).astype(jnp.bfloat16)


def placed_rows(target, scale, rows, shard_rows, block):
    devices, cap, width = rows.shape
    return pl.pallas_call(
        place_kernel,
        out_shape=jax.ShapeDtypeStruct((shard_rows, width), jnp.bfloat16),
        grid=(width // block,),
        in_specs=[
            pl.BlockSpec((1, devices * cap), lambda j: (0, 0)),
            pl.BlockSpec((devices * cap, 1), lambda j: (0, 0)),
            pl.BlockSpec((devices, cap, block), lambda j: (0, 0, j)),
        ],
        out_specs=pl.BlockSpec((shard_rows, block), lambda j: (0, j)),
        compiler_params=pltpu.CompilerParams(vmem_limit_bytes=48 << 20),
        cost_estimate=pl.CostEstimate(
            flops=2 * shard_rows * devices * cap * width,
            bytes_accessed=2 * (shard_rows + devices * cap) * width,
            transcendentals=0,
        ),
    )(target, scale, rows)


def local(
    token_ids,
    sensitivity,
    last_hidden,
    lengths,
    norm_gain,
    reward_head,
    chosen_index,
    rejected_index,
    shard_owner,
):
    resp_local, block_len = token_ids.shape
    width = sensitivity.shape[2]
    tok_local = resp_local * block_len
    devices = shard_owner.shape[0]
    shard_rows = VOCAB // devices
    responses = devices * resp_local

    own_place = lax.axis_index(GRP_DEV)
    cols = width // devices

    ids = token_ids.reshape(tok_local)
    shard_of = ids // shard_rows
    offset = ids - shard_of * shard_rows
    shard_hot = shard_of[:, None] == jnp.arange(devices, dtype=jnp.int32)[None, :]
    owner = jnp.sum(jnp.where(shard_hot, shard_owner[None, :], 0), axis=1)
    token_pos = jnp.arange(tok_local, dtype=jnp.int32)
    earlier = (token_pos[None, :] < token_pos[:, None]) & (shard_of[None, :] == shard_of[:, None])
    rank = jnp.sum(earlier.astype(jnp.int32), axis=1)
    slot = owner * CAP + rank

    live = (jnp.arange(block_len, dtype=jnp.int32)[None, :] < lengths[:, None]).reshape(tok_local)
    code = jnp.where(live, (offset + 1) * resp_local + token_pos // block_len, 0)
    hidden = last_hidden.astype(jnp.float32)
    norm = jnp.sqrt(jnp.mean(hidden * hidden, axis=-1, keepdims=True) + 1e-05)
    own_reward = jnp.sum(hidden / norm * norm_gain * reward_head, axis=-1)
    slot_match = slot[None, :] == jnp.arange(devices * CAP, dtype=jnp.int32)[:, None]
    codes = jnp.sum(jnp.where(slot_match, code[None, :], 0), axis=1).reshape(devices, CAP)
    own_facts = jnp.concatenate([own_reward, norm[:, 0], jnp.zeros((52,), jnp.float32)])
    message = jnp.concatenate(
        [
            codes.astype(jnp.float32),
            jnp.broadcast_to(own_facts[None, :], (devices, 60)),
            hidden.reshape(resp_local, devices, cols).swapaxes(0, 1).reshape(devices, -1),
        ],
        axis=1,
    )
    heard = lax.all_to_all(message, GRP_DEV, split_axis=0, concat_axis=0, tiled=True)
    outgoing = packed_rows(slot[None, :], sensitivity.reshape(tok_local, width), devices, 512)
    arrived = lax.all_to_all(outgoing, GRP_DEV, split_axis=0, concat_axis=0, tiled=True)

    arrived_code = heard[:, :CAP].astype(jnp.int32)
    reward = heard[:, 4:8].reshape(responses)
    margin = reward[chosen_index] - reward[rejected_index]
    push = -jax.nn.sigmoid(-margin)
    every = jnp.arange(responses, dtype=jnp.int32)
    sign_table = (chosen_index[None, :] == every[:, None]).astype(jnp.float32) - (
        rejected_index[None, :] == every[:, None]
    ).astype(jnp.float32)
    reward_grad = jnp.sum(sign_table * push[None, :], axis=1).reshape(devices, resp_local)
    own_gain = lax.dynamic_slice(norm_gain, (own_place * cols,), (cols,))
    head_grad = jnp.zeros((cols,), jnp.float32)
    for r in range(resp_local):
        normed = heard[:, 64 + r * cols : 64 + (r + 1) * cols] / heard[:, 8 + r : 9 + r] * own_gain
        head_grad += jnp.sum(reward_grad[:, r : r + 1] * normed, axis=0)

    response_in = arrived_code % resp_local
    scale = jnp.zeros(arrived_code.shape, jnp.float32)
    for r in range(resp_local):
        scale = jnp.where(response_in == r, reward_grad[:, r : r + 1], scale)
    target = arrived_code // resp_local - 1
    scale = jnp.where(target >= 0, scale, 0.0)
    owned = placed_rows(
        target.reshape(1, devices * CAP), scale.reshape(devices * CAP, 1), arrived, shard_rows, 512
    )
    return (owned, head_grad)


def solution(mesh):
    torus = Mesh(
        mesh.devices.reshape(mesh.shape["grp"], 8, 4, 2), ("grp", "dev_0", "dev_1", "dev_2")
    )
    placed = (
        P(GRP_DEV, None),
        P(GRP_DEV, None, None),
        P(GRP_DEV, None),
        P(GRP_DEV),
        P(),
        P(),
        P(),
        P(),
        P(),
    )
    return jax.shard_map(
        local,
        mesh=torus,
        in_specs=placed,
        out_specs=(P(GRP_DEV, None), P(GRP_DEV)),
        check_vma=False,
    )
```

```python
import functools

import jax
import jax.numpy as jnp
from jax import lax
from jax.experimental import pallas as pl
from jax.experimental.pallas import tpu as pltpu
from jax.sharding import Mesh
from jax.sharding import PartitionSpec as P

VOCAB = 128256
CAP = 4
GRP_DEV = ("grp", "dev_0", "dev_1", "dev_2")
PLANE = ("grp", "dev_1", "dev_2")
RING = 8
COLUMNS = 32
ROWS = 88
BLOCK = 512
VMEM = pltpu.CompilerParams(vmem_limit_bytes=48 << 20)
NT = (((1,), (1,)), ((), ()))


def cost(contractions, elements):
    return pl.CostEstimate(flops=2 * contractions, bytes_accessed=2 * elements, transcendentals=0)


def rows_of(shape):
    return lax.broadcasted_iota(jnp.int32, shape, 0)


def whole(shape):
    return pl.BlockSpec(shape, lambda j: (0,) * len(shape))


def pack_kernel(slot_ref, rows_ref, out_ref):
    hot = rows_of((out_ref.shape[0], slot_ref.shape[1])) == slot_ref[...]
    out_ref[...] = jnp.dot(
        hot.astype(jnp.bfloat16), rows_ref[...], preferred_element_type=jnp.float32
    ).astype(jnp.bfloat16)


def packed_rows(slot, rows, slots, first, width):
    tokens = rows.shape[0]
    skip = first // BLOCK
    return pl.pallas_call(
        pack_kernel,
        out_shape=jax.ShapeDtypeStruct((slots, width), jnp.bfloat16),
        grid=(width // BLOCK,),
        in_specs=[
            whole((1, tokens)),
            pl.BlockSpec((tokens, BLOCK), lambda j: (0, skip + j)),
        ],
        out_specs=pl.BlockSpec((slots, BLOCK), lambda j: (0, j)),
        compiler_params=VMEM,
        cost_estimate=cost(slots * tokens * width, (slots + tokens) * width),
    )(slot, rows)


def compact_tables(ring, place, code, hot_ref, note_ref):
    count = ring.shape[1]
    row = jnp.where(ring >= 0, ring * ROWS + place, -1)
    hot_ref[...] = (rows_of((RING * ROWS, count)) == row).astype(jnp.bfloat16)
    codes = jnp.broadcast_to(code, (8, count)).astype(jnp.bfloat16)
    for k in range(RING):
        mine = rows_of((128, count)) == jnp.where(ring == k, place, -1)
        note_ref[8 * k : 8 * k + 8, :] = lax.dot_general(
            codes, mine.astype(jnp.bfloat16), NT, preferred_element_type=jnp.float32
        )


def write_compact(rows, hot_ref, note_ref, out_refs):
    picked = jnp.dot(hot_ref[...], rows, preferred_element_type=jnp.float32)
    for k in range(RING):
        out_refs[k][...] = picked[k * ROWS : (k + 1) * ROWS].astype(jnp.bfloat16)

    @pl.when(pl.program_id(0) == 0)
    def _():
        for k in range(RING):
            tail = picked[(k + 1) * ROWS - 8 : (k + 1) * ROWS, :128]
            note = jnp.where(rows_of((8, 128)) == 7, note_ref[8 * k : 8 * k + 8, :], 0.0)
            out_refs[k][ROWS - 8 : ROWS, 0:128] = (tail + note).astype(jnp.bfloat16)


def ring_pack_kernel(ring_ref, place_ref, code_ref, rows_ref, *refs):
    outs, (hot_ref, note_ref) = refs[:RING], refs[RING:]

    @pl.when(pl.program_id(0) == 0)
    def _():
        compact_tables(ring_ref[...], place_ref[...], code_ref[...], hot_ref, note_ref)

    write_compact(rows_ref[...], hot_ref, note_ref, outs)


def ring_packed(ring, place, code, rows, width):
    tokens = rows.shape[0]
    return pl.pallas_call(
        ring_pack_kernel,
        out_shape=[jax.ShapeDtypeStruct((ROWS, width), jnp.bfloat16)] * RING,
        grid=(width // BLOCK,),
        in_specs=[whole((1, tokens))] * 3 + [pl.BlockSpec((tokens, BLOCK), lambda j: (0, j))],
        out_specs=[pl.BlockSpec((ROWS, BLOCK), lambda j: (0, j))] * RING,
        scratch_shapes=[
            pltpu.VMEM((RING * ROWS, tokens), jnp.bfloat16),
            pltpu.VMEM((8 * RING, 128), jnp.float32),
        ],
        compiler_params=VMEM,
        cost_estimate=cost(RING * ROWS * tokens * width, (RING * ROWS + tokens) * width),
    )(ring, place, code, rows)


def ring_repack_kernel(z_ref, rows_ref, *refs):
    outs, flag_ref = refs[:RING], refs[RING]
    hot_ref, note_ref, sum_ref, place_ref = refs[RING + 1 :]
    slots, width = rows_ref.shape
    step = pl.program_id(0)

    @pl.when(step == 0)
    def _():
        for r in range(0, slots, 256):
            total = jnp.zeros((256, 128), jnp.float32)
            for c in range(0, width, 128):
                total += jnp.abs(rows_ref[r : r + 256, c : c + 128].astype(jnp.float32))
            sum_ref[r : r + 256, :] = (total > 0).astype(jnp.bfloat16)
        seen = lax.dot_general(
            jnp.ones((8, 128), jnp.bfloat16), sum_ref[...], NT, preferred_element_type=jnp.float32
        )
        used = seen > 0
        used_bf16 = used.astype(jnp.bfloat16)
        for c in range(0, slots, 256):
            before = rows_of((slots, 256))
            slot = lax.broadcasted_iota(jnp.int32, (slots, 256), 1) + c
            ahead = (before < slot) & (((before ^ slot) & 28) == 0)
            place_ref[:, c : c + 256] = jnp.dot(
                used_bf16, ahead.astype(jnp.bfloat16), preferred_element_type=jnp.float32
            )
        place = place_ref[...].astype(jnp.int32)
        slot = lax.broadcasted_iota(jnp.int32, (8, slots), 1)
        over = jnp.where(used & (place >= ROWS - 1), 1.0, 0.0)
        flag_ref[...] = jnp.broadcast_to(jnp.max(over, axis=1, keepdims=True), (8, 128))
        ring = jnp.where(used & (place < ROWS - 1), (((slot >> 2) & 7) - z_ref[0]) & 7, -1)
        code = (((slot >> 5) << 2) + (slot & 3) + 1).astype(jnp.float32)
        compact_tables(ring[0:1, :], place[0:1, :], code[0:1, :], hot_ref, note_ref)

    start = pl.multiple_of(step * BLOCK, BLOCK)
    write_compact(rows_ref[:, pl.ds(start, BLOCK)], hot_ref, note_ref, outs)


def ring_repacked(z, rows):
    slots, width = rows.shape
    out = pl.pallas_call(
        ring_repack_kernel,
        out_shape=[jax.ShapeDtypeStruct((ROWS, width), jnp.bfloat16)] * RING
        + [jax.ShapeDtypeStruct((8, 128), jnp.float32)],
        grid=(width // BLOCK,),
        in_specs=[pl.BlockSpec(memory_space=pltpu.SMEM), whole((slots, width))],
        out_specs=[pl.BlockSpec((ROWS, BLOCK), lambda j: (0, j))] * RING + [whole((8, 128))],
        scratch_shapes=[
            pltpu.VMEM((RING * ROWS, slots), jnp.bfloat16),
            pltpu.VMEM((8 * RING, 128), jnp.float32),
            pltpu.VMEM((slots, 128), jnp.bfloat16),
            pltpu.VMEM((8, slots), jnp.float32),
        ],
        compiler_params=VMEM,
        cost_estimate=cost(RING * ROWS * slots * width, (RING * ROWS + slots) * width),
    )(z, rows)
    return out[:RING], out[RING]


def spread(z_ref, in_refs, hot_ref, held_ref):
    slots = hot_ref.shape[0]

    @pl.when(pl.program_id(0) == 0)
    def _():
        held_ref[...] = jnp.zeros_like(held_ref)
        for k in range(RING):
            code = in_refs[k][ROWS - 8 : ROWS, 0:128].astype(jnp.float32)[7:8, :].astype(jnp.int32)
            where = code - 1
            plane = (z_ref[0] - k) & 7
            slot = jnp.where(code > 0, ((where >> 2) << 5) + (plane << 2) + (where & 3), -1)
            hot_ref[:, 128 * k : 128 * k + 128] = (rows_of((slots, 128)) == slot).astype(
                jnp.bfloat16
            )

    for k in range(RING):
        held_ref[128 * k : 128 * k + ROWS, :] = in_refs[k][...]
    return jnp.dot(hot_ref[...], held_ref[...], preferred_element_type=jnp.float32)


def ring_spread_kernel(z_ref, *refs):
    ins, (out_ref, hot_ref, held_ref) = refs[:RING], refs[RING:]
    out_ref[...] = spread(z_ref, ins, hot_ref, held_ref).astype(jnp.bfloat16)


def ring_specs():
    return [pl.BlockSpec(memory_space=pltpu.SMEM)] + [
        pl.BlockSpec((ROWS, BLOCK), lambda j: (0, j))
    ] * RING


def ring_spread(z, parts, slots):
    width = parts[0].shape[1]
    return pl.pallas_call(
        ring_spread_kernel,
        out_shape=jax.ShapeDtypeStruct((slots, width), jnp.bfloat16),
        grid=(width // BLOCK,),
        in_specs=ring_specs(),
        out_specs=pl.BlockSpec((slots, BLOCK), lambda j: (0, j)),
        scratch_shapes=[
            pltpu.VMEM((slots, 128 * RING), jnp.bfloat16),
            pltpu.VMEM((128 * RING, BLOCK), jnp.bfloat16),
        ],
        compiler_params=VMEM,
        cost_estimate=cost(slots * 128 * RING * width, (slots + ROWS * RING) * width),
    )(z, *parts)


def placed(target, scale, rows, out_ref):
    scaled = (scale * rows).astype(jnp.bfloat16)
    hot = rows_of((out_ref.shape[0], target.shape[1])) == target
    out_ref[...] = jnp.dot(
        hot.astype(jnp.bfloat16), scaled, preferred_element_type=jnp.float32
    ).astype(jnp.bfloat16)


def place_kernel(target_ref, scale_ref, rows_ref, out_ref):
    placed(target_ref[...], scale_ref[...], rows_ref[...].astype(jnp.float32), out_ref)


def placed_rows(target, scale, rows, shard_rows, out_width):
    slots, width = rows.shape
    return pl.pallas_call(
        place_kernel,
        out_shape=jax.ShapeDtypeStruct((shard_rows, out_width), jnp.bfloat16),
        grid=(width // BLOCK,),
        in_specs=[
            whole((1, slots)),
            whole((slots, 1)),
            pl.BlockSpec((slots, BLOCK), lambda j: (0, j)),
        ],
        out_specs=pl.BlockSpec((shard_rows, BLOCK), lambda j: (0, j)),
        compiler_params=VMEM,
        cost_estimate=cost(shard_rows * slots * width, (shard_rows + slots) * width),
    )(target, scale, rows)


def ring_place_kernel(target_ref, scale_ref, z_ref, *refs):
    ins, (_, out_ref, hot_ref, held_ref) = refs[:RING], refs[RING:]
    placed(target_ref[...], scale_ref[...], spread(z_ref, ins, hot_ref, held_ref), out_ref)


def ring_placed(target, scale, z, parts, half_done):
    shard_rows, out_width = half_done.shape
    slots = target.shape[1]
    width = parts[0].shape[1]
    skip = (out_width - width) // BLOCK
    return pl.pallas_call(
        ring_place_kernel,
        out_shape=jax.ShapeDtypeStruct(half_done.shape, jnp.bfloat16),
        grid=(width // BLOCK,),
        in_specs=[whole((1, slots)), whole((slots, 1))]
        + ring_specs()
        + [pl.BlockSpec(memory_space=pl.ANY)],
        out_specs=pl.BlockSpec((shard_rows, BLOCK), lambda j: (0, skip + j)),
        scratch_shapes=[
            pltpu.VMEM((slots, 128 * RING), jnp.bfloat16),
            pltpu.VMEM((128 * RING, BLOCK), jnp.bfloat16),
        ],
        input_output_aliases={3 + RING: 0},
        compiler_params=VMEM,
        cost_estimate=cost((shard_rows + 1024) * slots * width, (shard_rows + slots) * width),
    )(target, scale, z, *parts, half_done)


def ring_shifted(parts):
    moved = [parts[0]]
    for k in range(1, RING):
        moved.append(lax.ppermute(parts[k], "dev_0", [(i, (i + k) % RING) for i in range(RING)]))
    return moved


def in_plane(rows):
    slots, width = rows.shape
    parts = rows.reshape(COLUMNS, slots // COLUMNS, width)
    return lax.all_to_all(parts, PLANE, split_axis=0, concat_axis=0, tiled=True).reshape(
        slots, width
    )


def slot_order(table):
    return table.reshape(4, RING, 8, CAP).swapaxes(1, 2).reshape(-1)


def count_earlier(key, counts):
    pos = jnp.arange(key.shape[0], dtype=jnp.int32)
    earlier = (pos[None, :] < pos[:, None]) & (key[None, :] == key[:, None]) & counts[None, :]
    return jnp.sum(earlier.astype(jnp.int32), axis=1)


def local(
    token_ids,
    sensitivity,
    last_hidden,
    lengths,
    norm_gain,
    reward_head,
    chosen_index,
    rejected_index,
    shard_owner,
):
    resp_local, block_len = token_ids.shape
    width = sensitivity.shape[2]
    half = width // 2
    tok_local = resp_local * block_len
    devices = shard_owner.shape[0]
    slots = devices * CAP
    shard_rows = VOCAB // devices
    responses = devices * resp_local
    cols = width // devices
    own_place = lax.axis_index(GRP_DEV)
    z = lax.axis_index("dev_0")[None]
    rows = sensitivity.reshape(tok_local, width)

    ids = token_ids.reshape(tok_local)
    shard_of = ids // shard_rows
    offset = ids - shard_of * shard_rows
    shard_hot = shard_of[:, None] == jnp.arange(devices, dtype=jnp.int32)[None, :]
    owner = jnp.sum(jnp.where(shard_hot, shard_owner[None, :], 0), axis=1)
    token_pos = jnp.arange(tok_local, dtype=jnp.int32)
    live = (jnp.arange(block_len, dtype=jnp.int32)[None, :] < lengths[:, None]).reshape(tok_local)
    rank = count_earlier(shard_of, jnp.ones_like(live))
    plane = (owner >> 3) & 7
    column = ((owner >> 6) << 3) + (owner & 7)
    place = count_earlier(plane, live)
    fits = live & (place < ROWS - 1)
    over_here = jnp.any(live & ~fits).astype(jnp.float32)
    ring = jnp.where(fits, (plane - z) & 7, -1)

    first = ring_packed(
        ring[None, :],
        place[None, :],
        (column * CAP + rank + 1).astype(jnp.float32)[None, :],
        rows,
        half,
    )
    first = ring_shifted(first)
    second_slot = jnp.where(live, (column << 5) + (plane << 2) + rank, -1)
    second = in_plane(packed_rows(second_slot[None, :], rows, slots, half, half))
    second, over_there = ring_repacked(z, second)
    second = ring_shifted(second)

    code = jnp.where(live, (offset + 1) * resp_local + token_pos // block_len, 0)
    direct_slot = owner * CAP + rank
    hidden = last_hidden.astype(jnp.float32)
    norm = jnp.sqrt(jnp.mean(hidden * hidden, axis=-1, keepdims=True) + 1e-05)
    own_reward = jnp.sum(hidden / norm * norm_gain * reward_head, axis=-1)
    slot_match = direct_slot[None, :] == jnp.arange(slots, dtype=jnp.int32)[:, None]
    codes = jnp.sum(jnp.where(slot_match, code[None, :], 0), axis=1).reshape(devices, CAP)
    over = jnp.maximum(over_here, over_there[0, 0])
    own_facts = jnp.concatenate(
        [own_reward, norm[:, 0], over[None], jnp.zeros((51,), jnp.float32)]
    )
    message = jnp.concatenate(
        [
            codes.astype(jnp.float32),
            jnp.broadcast_to(own_facts[None, :], (devices, 60)),
            hidden.reshape(resp_local, devices, cols).swapaxes(0, 1).reshape(devices, -1),
        ],
        axis=1,
    )
    heard = lax.all_to_all(message, GRP_DEV, split_axis=0, concat_axis=0, tiled=True)

    first = in_plane(ring_spread(z, first, slots))

    arrived_code = heard[:, :CAP].astype(jnp.int32)
    reward = heard[:, 4:8].reshape(responses)
    any_over = jnp.max(heard[:, 12]) > 0
    margin = reward[chosen_index] - reward[rejected_index]
    push = -jax.nn.sigmoid(-margin)
    every = jnp.arange(responses, dtype=jnp.int32)
    sign_table = (chosen_index[None, :] == every[:, None]).astype(jnp.float32) - (
        rejected_index[None, :] == every[:, None]
    ).astype(jnp.float32)
    reward_grad = jnp.sum(sign_table * push[None, :], axis=1).reshape(devices, resp_local)
    own_gain = lax.dynamic_slice(norm_gain, (own_place * cols,), (cols,))
    head_grad = jnp.zeros((cols,), jnp.float32)
    for r in range(resp_local):
        normed = heard[:, 64 + r * cols : 64 + (r + 1) * cols] / heard[:, 8 + r : 9 + r] * own_gain
        head_grad += jnp.sum(reward_grad[:, r : r + 1] * normed, axis=0)

    response_in = arrived_code % resp_local
    scale = jnp.zeros(arrived_code.shape, jnp.float32)
    for r in range(resp_local):
        scale = jnp.where(response_in == r, reward_grad[:, r : r + 1], scale)
    target = arrived_code // resp_local - 1
    scale = jnp.where(target >= 0, scale, 0.0)
    target_row = slot_order(target)[None, :]
    scale_column = slot_order(scale)[:, None]
    half_done = placed_rows(target_row, scale_column, first, shard_rows, width)

    def by_ring():
        return ring_placed(target_row, scale_column, z, second, half_done)

    def direct():
        sent = packed_rows(
            jnp.where(live, direct_slot, -1)[None, :], rows, slots, 0, width
        ).reshape(devices, CAP, width)
        arrived = lax.all_to_all(sent, GRP_DEV, split_axis=0, concat_axis=0, tiled=True)
        return placed_rows(
            target.reshape(1, slots),
            scale.reshape(slots, 1),
            arrived.reshape(slots, width),
            shard_rows,
            width,
        )

    return (lax.cond(any_over, direct, by_ring), head_grad)


def solution(mesh):
    torus = Mesh(
        mesh.devices.reshape(mesh.shape["grp"], 8, 4, 2), ("grp", "dev_0", "dev_1", "dev_2")
    )
    placed_as = (
        P(GRP_DEV, None),
        P(GRP_DEV, None, None),
        P(GRP_DEV, None),
        P(GRP_DEV),
        P(),
        P(),
        P(),
        P(),
        P(),
    )
    return jax.shard_map(
        local,
        mesh=torus,
        in_specs=placed_as,
        out_specs=(P(GRP_DEV, None), P(GRP_DEV)),
        check_vma=False,
    )
```

```python
import functools

import jax
import jax.numpy as jnp
from jax import lax
from jax.experimental import pallas as pl
from jax.experimental.pallas import tpu as pltpu
from jax.sharding import Mesh
from jax.sharding import PartitionSpec as P

VOCAB = 128256
CAP = 4
GRP_DEV = ("grp", "dev_0", "dev_1", "dev_2")
PLANE = ("grp", "dev_1", "dev_2")
RING = 8
COLUMNS = 32
ROWS = 88
BLOCK = 512
VMEM = pltpu.CompilerParams(vmem_limit_bytes=48 << 20)
NT = (((1,), (1,)), ((), ()))


def cost(contractions, elements):
    return pl.CostEstimate(flops=2 * contractions, bytes_accessed=2 * elements, transcendentals=0)


def rows_of(shape):
    return lax.broadcasted_iota(jnp.int32, shape, 0)


def whole(shape):
    return pl.BlockSpec(shape, lambda j: (0,) * len(shape))


def pack_kernel(slot_ref, rows_ref, out_ref):
    hot = rows_of((out_ref.shape[0], slot_ref.shape[1])) == slot_ref[...]
    out_ref[...] = jnp.dot(
        hot.astype(jnp.bfloat16), rows_ref[...], preferred_element_type=jnp.float32
    ).astype(jnp.bfloat16)


def packed_rows(slot, rows, slots, first, width):
    tokens = rows.shape[0]
    skip = first // BLOCK
    return pl.pallas_call(
        pack_kernel,
        out_shape=jax.ShapeDtypeStruct((slots, width), jnp.bfloat16),
        grid=(width // BLOCK,),
        in_specs=[
            whole((1, tokens)),
            pl.BlockSpec((tokens, BLOCK), lambda j: (0, skip + j)),
        ],
        out_specs=pl.BlockSpec((slots, BLOCK), lambda j: (0, j)),
        compiler_params=VMEM,
        cost_estimate=cost(slots * tokens * width, (slots + tokens) * width),
    )(slot, rows)


def compact_tables(ring, place, code, hot_ref, note_ref):
    count = ring.shape[1]
    row = jnp.where(ring >= 0, ring * ROWS + place, -1)
    hot_ref[...] = (rows_of((RING * ROWS, count)) == row).astype(jnp.bfloat16)
    codes = jnp.broadcast_to(code, (8, count)).astype(jnp.bfloat16)
    for k in range(RING):
        mine = rows_of((128, count)) == jnp.where(ring == k, place, -1)
        note_ref[8 * k : 8 * k + 8, :] = lax.dot_general(
            codes, mine.astype(jnp.bfloat16), NT, preferred_element_type=jnp.float32
        )


def write_compact(rows, hot_ref, note_ref, out_refs):
    picked = jnp.dot(hot_ref[...], rows, preferred_element_type=jnp.float32)
    for k in range(RING):
        out_refs[k][...] = picked[k * ROWS : (k + 1) * ROWS].astype(jnp.bfloat16)

    @pl.when(pl.program_id(0) == 0)
    def _():
        for k in range(RING):
            tail = picked[(k + 1) * ROWS - 8 : (k + 1) * ROWS, :128]
            note = jnp.where(rows_of((8, 128)) == 7, note_ref[8 * k : 8 * k + 8, :], 0.0)
            out_refs[k][ROWS - 8 : ROWS, 0:128] = (tail + note).astype(jnp.bfloat16)


def ring_pack_kernel(ring_ref, place_ref, code_ref, rows_ref, *refs):
    outs, (hot_ref, note_ref) = refs[:RING], refs[RING:]

    @pl.when(pl.program_id(0) == 0)
    def _():
        compact_tables(ring_ref[...], place_ref[...], code_ref[...], hot_ref, note_ref)

    write_compact(rows_ref[...], hot_ref, note_ref, outs)


def ring_packed(ring, place, code, rows, width):
    tokens = rows.shape[0]
    return pl.pallas_call(
        ring_pack_kernel,
        out_shape=[jax.ShapeDtypeStruct((ROWS, width), jnp.bfloat16)] * RING,
        grid=(width // BLOCK,),
        in_specs=[whole((1, tokens))] * 3 + [pl.BlockSpec((tokens, BLOCK), lambda j: (0, j))],
        out_specs=[pl.BlockSpec((ROWS, BLOCK), lambda j: (0, j))] * RING,
        scratch_shapes=[
            pltpu.VMEM((RING * ROWS, tokens), jnp.bfloat16),
            pltpu.VMEM((8 * RING, 128), jnp.float32),
        ],
        compiler_params=VMEM,
        cost_estimate=cost(RING * ROWS * tokens * width, (RING * ROWS + tokens) * width),
    )(ring, place, code, rows)


def ring_repack_kernel(z_ref, rows_ref, *refs):
    outs, flag_ref = refs[:RING], refs[RING]
    hot_ref, note_ref, sum_ref, place_ref = refs[RING + 1 :]
    slots, width = rows_ref.shape
    step = pl.program_id(0)

    @pl.when(step == 0)
    def _():
        for r in range(0, slots, 256):
            total = jnp.zeros((256, 128), jnp.float32)
            for c in range(0, width, 128):
                total += jnp.abs(rows_ref[r : r + 256, c : c + 128].astype(jnp.float32))
            sum_ref[r : r + 256, :] = (total > 0).astype(jnp.bfloat16)
        seen = lax.dot_general(
            jnp.ones((8, 128), jnp.bfloat16), sum_ref[...], NT, preferred_element_type=jnp.float32
        )
        used = seen > 0
        used_bf16 = used.astype(jnp.bfloat16)
        for c in range(0, slots, 256):
            before = rows_of((slots, 256))
            slot = lax.broadcasted_iota(jnp.int32, (slots, 256), 1) + c
            ahead = (before < slot) & (((before ^ slot) & 28) == 0)
            place_ref[:, c : c + 256] = jnp.dot(
                used_bf16, ahead.astype(jnp.bfloat16), preferred_element_type=jnp.float32
            )
        place = place_ref[...].astype(jnp.int32)
        slot = lax.broadcasted_iota(jnp.int32, (8, slots), 1)
        over = jnp.where(used & (place >= ROWS - 1), 1.0, 0.0)
        flag_ref[...] = jnp.broadcast_to(jnp.max(over, axis=1, keepdims=True), (8, 128))
        ring = jnp.where(used & (place < ROWS - 1), (((slot >> 2) & 7) - z_ref[0]) & 7, -1)
        code = (((slot >> 5) << 2) + (slot & 3) + 1).astype(jnp.float32)
        compact_tables(ring[0:1, :], place[0:1, :], code[0:1, :], hot_ref, note_ref)

    start = pl.multiple_of(step * BLOCK, BLOCK)
    write_compact(rows_ref[:, pl.ds(start, BLOCK)], hot_ref, note_ref, outs)


def ring_repacked(z, rows):
    slots, width = rows.shape
    out = pl.pallas_call(
        ring_repack_kernel,
        out_shape=[jax.ShapeDtypeStruct((ROWS, width), jnp.bfloat16)] * RING
        + [jax.ShapeDtypeStruct((8, 128), jnp.float32)],
        grid=(width // BLOCK,),
        in_specs=[pl.BlockSpec(memory_space=pltpu.SMEM), whole((slots, width))],
        out_specs=[pl.BlockSpec((ROWS, BLOCK), lambda j: (0, j))] * RING + [whole((8, 128))],
        scratch_shapes=[
            pltpu.VMEM((RING * ROWS, slots), jnp.bfloat16),
            pltpu.VMEM((8 * RING, 128), jnp.float32),
            pltpu.VMEM((slots, 128), jnp.bfloat16),
            pltpu.VMEM((8, slots), jnp.float32),
        ],
        compiler_params=VMEM,
        cost_estimate=cost(RING * ROWS * slots * width, (RING * ROWS + slots) * width),
    )(z, rows)
    return out[:RING], out[RING]


def spread(z_ref, in_refs, hot_ref, held_ref):
    slots = hot_ref.shape[0]

    @pl.when(pl.program_id(0) == 0)
    def _():
        held_ref[...] = jnp.zeros_like(held_ref)
        for k in range(RING):
            code = in_refs[k][ROWS - 8 : ROWS, 0:128].astype(jnp.float32)[7:8, :].astype(jnp.int32)
            where = code - 1
            plane = (z_ref[0] - k) & 7
            slot = jnp.where(code > 0, ((where >> 2) << 5) + (plane << 2) + (where & 3), -1)
            hot_ref[:, 128 * k : 128 * k + 128] = (rows_of((slots, 128)) == slot).astype(
                jnp.bfloat16
            )

    for k in range(RING):
        held_ref[128 * k : 128 * k + ROWS, :] = in_refs[k][...]
    return jnp.dot(hot_ref[...], held_ref[...], preferred_element_type=jnp.float32)


def ring_spread_kernel(z_ref, *refs):
    ins, (out_ref, hot_ref, held_ref) = refs[:RING], refs[RING:]
    out_ref[...] = spread(z_ref, ins, hot_ref, held_ref).astype(jnp.bfloat16)


def ring_specs():
    return [pl.BlockSpec(memory_space=pltpu.SMEM)] + [
        pl.BlockSpec((ROWS, BLOCK), lambda j: (0, j))
    ] * RING


def ring_spread(z, parts, slots):
    width = parts[0].shape[1]
    return pl.pallas_call(
        ring_spread_kernel,
        out_shape=jax.ShapeDtypeStruct((slots, width), jnp.bfloat16),
        grid=(width // BLOCK,),
        in_specs=ring_specs(),
        out_specs=pl.BlockSpec((slots, BLOCK), lambda j: (0, j)),
        scratch_shapes=[
            pltpu.VMEM((slots, 128 * RING), jnp.bfloat16),
            pltpu.VMEM((128 * RING, BLOCK), jnp.bfloat16),
        ],
        compiler_params=VMEM,
        cost_estimate=cost(slots * 128 * RING * width, (slots + ROWS * RING) * width),
    )(z, *parts)


def placed(target, scale, rows, out_ref):
    scaled = (scale * rows).astype(jnp.bfloat16)
    hot = rows_of((out_ref.shape[0], target.shape[1])) == target
    out_ref[...] = jnp.dot(
        hot.astype(jnp.bfloat16), scaled, preferred_element_type=jnp.float32
    ).astype(jnp.bfloat16)


def place_kernel(target_ref, scale_ref, rows_ref, out_ref):
    placed(target_ref[...], scale_ref[...], rows_ref[...].astype(jnp.float32), out_ref)


def placed_rows(target, scale, rows, shard_rows, out_width):
    slots, width = rows.shape
    return pl.pallas_call(
        place_kernel,
        out_shape=jax.ShapeDtypeStruct((shard_rows, out_width), jnp.bfloat16),
        grid=(width // BLOCK,),
        in_specs=[
            whole((1, slots)),
            whole((slots, 1)),
            pl.BlockSpec((slots, BLOCK), lambda j: (0, j)),
        ],
        out_specs=pl.BlockSpec((shard_rows, BLOCK), lambda j: (0, j)),
        compiler_params=VMEM,
        cost_estimate=cost(shard_rows * slots * width, (shard_rows + slots) * width),
    )(target, scale, rows)


def ring_place_kernel(target_ref, scale_ref, z_ref, *refs):
    ins, (_, out_ref, hot_ref, held_ref) = refs[:RING], refs[RING:]
    placed(target_ref[...], scale_ref[...], spread(z_ref, ins, hot_ref, held_ref), out_ref)


def ring_placed(target, scale, z, parts, half_done):
    shard_rows, out_width = half_done.shape
    slots = target.shape[1]
    width = parts[0].shape[1]
    skip = (out_width - width) // BLOCK
    return pl.pallas_call(
        ring_place_kernel,
        out_shape=jax.ShapeDtypeStruct(half_done.shape, jnp.bfloat16),
        grid=(width // BLOCK,),
        in_specs=[whole((1, slots)), whole((slots, 1))]
        + ring_specs()
        + [pl.BlockSpec(memory_space=pl.ANY)],
        out_specs=pl.BlockSpec((shard_rows, BLOCK), lambda j: (0, skip + j)),
        scratch_shapes=[
            pltpu.VMEM((slots, 128 * RING), jnp.bfloat16),
            pltpu.VMEM((128 * RING, BLOCK), jnp.bfloat16),
        ],
        input_output_aliases={3 + RING: 0},
        compiler_params=VMEM,
        cost_estimate=cost((shard_rows + 1024) * slots * width, (shard_rows + slots) * width),
    )(target, scale, z, *parts, half_done)


def ring_shifted(parts):
    moved = [parts[0]]
    for k in range(1, RING):
        moved.append(lax.ppermute(parts[k], "dev_0", [(i, (i + k) % RING) for i in range(RING)]))
    return moved


def in_plane(rows):
    slots, width = rows.shape
    parts = rows.reshape(COLUMNS, slots // COLUMNS, width)
    return lax.all_to_all(parts, PLANE, split_axis=0, concat_axis=0, tiled=True).reshape(
        slots, width
    )


def slot_order(table):
    return table.reshape(4, RING, 8, CAP).swapaxes(1, 2).reshape(-1)


def count_earlier(key, counts):
    pos = jnp.arange(key.shape[0], dtype=jnp.int32)
    earlier = (pos[None, :] < pos[:, None]) & (key[None, :] == key[:, None]) & counts[None, :]
    return jnp.sum(earlier.astype(jnp.int32), axis=1)


def local(
    token_ids,
    sensitivity,
    last_hidden,
    lengths,
    norm_gain,
    reward_head,
    chosen_index,
    rejected_index,
    shard_owner,
):
    resp_local, block_len = token_ids.shape
    width = sensitivity.shape[2]
    half = width // 2
    tok_local = resp_local * block_len
    devices = shard_owner.shape[0]
    slots = devices * CAP
    shard_rows = VOCAB // devices
    responses = devices * resp_local
    cols = width // devices
    own_place = lax.axis_index(GRP_DEV)
    z = lax.axis_index("dev_0")[None]
    rows = sensitivity.reshape(tok_local, width)

    ids = token_ids.reshape(tok_local)
    shard_of = ids // shard_rows
    offset = ids - shard_of * shard_rows
    shard_hot = shard_of[:, None] == jnp.arange(devices, dtype=jnp.int32)[None, :]
    owner = jnp.sum(jnp.where(shard_hot, shard_owner[None, :], 0), axis=1)
    token_pos = jnp.arange(tok_local, dtype=jnp.int32)
    live = (jnp.arange(block_len, dtype=jnp.int32)[None, :] < lengths[:, None]).reshape(tok_local)
    rank = count_earlier(shard_of, jnp.ones_like(live))
    plane = (owner >> 3) & 7
    column = ((owner >> 6) << 3) + (owner & 7)
    place = count_earlier(plane, live)
    fits = live & (place < ROWS - 1)
    over_here = jnp.any(live & ~fits).astype(jnp.float32)
    ring = jnp.where(fits, (plane - z) & 7, -1)

    first = ring_packed(
        ring[None, :],
        place[None, :],
        (column * CAP + rank + 1).astype(jnp.float32)[None, :],
        rows,
        half,
    )
    first = ring_shifted(first)
    second_slot = jnp.where(live, (column << 5) + (plane << 2) + rank, -1)
    second = in_plane(packed_rows(second_slot[None, :], rows, slots, half, half))
    first[1], first[2], second = lax.optimization_barrier((first[1], first[2], second))
    second, over_there = ring_repacked(z, second)
    second = ring_shifted(second)

    code = jnp.where(live, (offset + 1) * resp_local + token_pos // block_len, 0)
    direct_slot = owner * CAP + rank
    hidden = last_hidden.astype(jnp.float32)
    norm = jnp.sqrt(jnp.mean(hidden * hidden, axis=-1, keepdims=True) + 1e-05)
    own_reward = jnp.sum(hidden / norm * norm_gain * reward_head, axis=-1)
    slot_match = direct_slot[None, :] == jnp.arange(slots, dtype=jnp.int32)[:, None]
    codes = jnp.sum(jnp.where(slot_match, code[None, :], 0), axis=1).reshape(devices, CAP)
    over = jnp.maximum(over_here, over_there[0, 0])
    own_facts = jnp.concatenate(
        [own_reward, norm[:, 0], over[None], jnp.zeros((51,), jnp.float32)]
    )
    message = jnp.concatenate(
        [
            codes.astype(jnp.float32),
            jnp.broadcast_to(own_facts[None, :], (devices, 60)),
            hidden.reshape(resp_local, devices, cols).swapaxes(0, 1).reshape(devices, -1),
        ],
        axis=1,
    )
    heard = lax.all_to_all(message, GRP_DEV, split_axis=0, concat_axis=0, tiled=True)

    arrived_code = heard[:, :CAP].astype(jnp.int32)
    reward = heard[:, 4:8].reshape(responses)
    any_over = jnp.max(heard[:, 12]) > 0
    margin = reward[chosen_index] - reward[rejected_index]
    push = -jax.nn.sigmoid(-margin)
    every = jnp.arange(responses, dtype=jnp.int32)
    sign_table = (chosen_index[None, :] == every[:, None]).astype(jnp.float32) - (
        rejected_index[None, :] == every[:, None]
    ).astype(jnp.float32)
    reward_grad = jnp.sum(sign_table * push[None, :], axis=1).reshape(devices, resp_local)
    own_gain = lax.dynamic_slice(norm_gain, (own_place * cols,), (cols,))
    head_grad = jnp.zeros((cols,), jnp.float32)
    for r in range(resp_local):
        normed = heard[:, 64 + r * cols : 64 + (r + 1) * cols] / heard[:, 8 + r : 9 + r] * own_gain
        head_grad += jnp.sum(reward_grad[:, r : r + 1] * normed, axis=0)

    response_in = arrived_code % resp_local
    scale = jnp.zeros(arrived_code.shape, jnp.float32)
    for r in range(resp_local):
        scale = jnp.where(response_in == r, reward_grad[:, r : r + 1], scale)
    target = arrived_code // resp_local - 1
    scale = jnp.where(target >= 0, scale, 0.0)
    target_row = slot_order(target)[None, :]
    scale_column = slot_order(scale)[:, None]
    target_row, scale_column, first = lax.optimization_barrier((target_row, scale_column, first))
    first = ring_spread(z, first, slots)
    first, second[1], second[7] = lax.optimization_barrier((first, second[1], second[7]))
    first = in_plane(first)
    half_done = placed_rows(target_row, scale_column, first, shard_rows, width)

    def by_ring():
        return ring_placed(target_row, scale_column, z, second, half_done)

    def direct():
        sent = packed_rows(
            jnp.where(live, direct_slot, -1)[None, :], rows, slots, 0, width
        ).reshape(devices, CAP, width)
        arrived = lax.all_to_all(sent, GRP_DEV, split_axis=0, concat_axis=0, tiled=True)
        return placed_rows(
            target.reshape(1, slots),
            scale.reshape(slots, 1),
            arrived.reshape(slots, width),
            shard_rows,
            width,
        )

    return (lax.cond(any_over, direct, by_ring), head_grad)


def solution(mesh):
    torus = Mesh(
        mesh.devices.reshape(mesh.shape["grp"], 8, 4, 2), ("grp", "dev_0", "dev_1", "dev_2")
    )
    placed_as = (
        P(GRP_DEV, None),
        P(GRP_DEV, None, None),
        P(GRP_DEV, None),
        P(GRP_DEV),
        P(),
        P(),
        P(),
        P(),
        P(),
    )
    return jax.shard_map(
        local,
        mesh=torus,
        in_specs=placed_as,
        out_specs=(P(GRP_DEV, None), P(GRP_DEV)),
        check_vma=False,
    )
```

```python
import functools

import jax
import jax.numpy as jnp
from jax import lax
from jax.experimental import pallas as pl
from jax.experimental.pallas import tpu as pltpu
from jax.sharding import Mesh
from jax.sharding import PartitionSpec as P

VOCAB = 128256
CAP = 4
GRP_DEV = ("grp", "dev_0", "dev_1", "dev_2")
PLANE = ("grp", "dev_1", "dev_2")
RING = 8
COLUMNS = 32
ROWS = 88
BLOCK = 512
VMEM = pltpu.CompilerParams(vmem_limit_bytes=48 << 20)
NT = (((1,), (1,)), ((), ()))


def cost(contractions, elements):
    return pl.CostEstimate(flops=2 * contractions, bytes_accessed=2 * elements, transcendentals=0)


def rows_of(shape):
    return lax.broadcasted_iota(jnp.int32, shape, 0)


def whole(shape):
    return pl.BlockSpec(shape, lambda j: (0,) * len(shape))


def pack_kernel(slot_ref, rows_ref, out_ref):
    hot = rows_of((out_ref.shape[0], slot_ref.shape[1])) == slot_ref[...]
    out_ref[...] = jnp.dot(
        hot.astype(jnp.bfloat16), rows_ref[...], preferred_element_type=jnp.float32
    ).astype(jnp.bfloat16)


def packed_rows(slot, rows, slots, first, width):
    tokens = rows.shape[0]
    skip = first // BLOCK
    return pl.pallas_call(
        pack_kernel,
        out_shape=jax.ShapeDtypeStruct((slots, width), jnp.bfloat16),
        grid=(width // BLOCK,),
        in_specs=[
            whole((1, tokens)),
            pl.BlockSpec((tokens, BLOCK), lambda j: (0, skip + j)),
        ],
        out_specs=pl.BlockSpec((slots, BLOCK), lambda j: (0, j)),
        compiler_params=VMEM,
        cost_estimate=cost(slots * tokens * width, (slots + tokens) * width),
    )(slot, rows)


def compact_tables(ring, place, code, hot_ref, note_ref):
    count = ring.shape[1]
    row = jnp.where(ring >= 0, ring * ROWS + place, -1)
    hot_ref[...] = (rows_of((RING * ROWS, count)) == row).astype(jnp.bfloat16)
    codes = jnp.broadcast_to(code, (8, count)).astype(jnp.bfloat16)
    for k in range(RING):
        mine = rows_of((128, count)) == jnp.where(ring == k, place, -1)
        note_ref[8 * k : 8 * k + 8, :] = lax.dot_general(
            codes, mine.astype(jnp.bfloat16), NT, preferred_element_type=jnp.float32
        )


def write_compact(rows, hot_ref, note_ref, out_refs):
    picked = jnp.dot(hot_ref[...], rows, preferred_element_type=jnp.float32)
    for k in range(RING):
        out_refs[k][...] = picked[k * ROWS : (k + 1) * ROWS].astype(jnp.bfloat16)

    @pl.when(pl.program_id(0) == 0)
    def _():
        for k in range(RING):
            tail = picked[(k + 1) * ROWS - 8 : (k + 1) * ROWS, :128]
            note = jnp.where(rows_of((8, 128)) == 7, note_ref[8 * k : 8 * k + 8, :], 0.0)
            out_refs[k][ROWS - 8 : ROWS, 0:128] = (tail + note).astype(jnp.bfloat16)


def ring_pack_kernel(ring_ref, place_ref, code_ref, rows_ref, *refs):
    outs, (hot_ref, note_ref) = refs[:RING], refs[RING:]

    @pl.when(pl.program_id(0) == 0)
    def _():
        compact_tables(ring_ref[...], place_ref[...], code_ref[...], hot_ref, note_ref)

    write_compact(rows_ref[...], hot_ref, note_ref, outs)


def ring_packed(ring, place, code, rows, width):
    tokens = rows.shape[0]
    return pl.pallas_call(
        ring_pack_kernel,
        out_shape=[jax.ShapeDtypeStruct((ROWS, width), jnp.bfloat16)] * RING,
        grid=(width // BLOCK,),
        in_specs=[whole((1, tokens))] * 3 + [pl.BlockSpec((tokens, BLOCK), lambda j: (0, j))],
        out_specs=[pl.BlockSpec((ROWS, BLOCK), lambda j: (0, j))] * RING,
        scratch_shapes=[
            pltpu.VMEM((RING * ROWS, tokens), jnp.bfloat16),
            pltpu.VMEM((8 * RING, 128), jnp.float32),
        ],
        compiler_params=VMEM,
        cost_estimate=cost(RING * ROWS * tokens * width, (RING * ROWS + tokens) * width),
    )(ring, place, code, rows)


def ring_repack_kernel(z_ref, rows_ref, *refs):
    outs, flag_ref = refs[:RING], refs[RING]
    hot_ref, note_ref, sum_ref, place_ref = refs[RING + 1 :]
    slots, width = rows_ref.shape
    step = pl.program_id(0)

    @pl.when(step == 0)
    def _():
        for r in range(0, slots, 256):
            total = jnp.zeros((256, 128), jnp.float32)
            for c in range(0, width, 128):
                total += jnp.abs(rows_ref[r : r + 256, c : c + 128].astype(jnp.float32))
            sum_ref[r : r + 256, :] = (total > 0).astype(jnp.bfloat16)
        seen = lax.dot_general(
            jnp.ones((8, 128), jnp.bfloat16), sum_ref[...], NT, preferred_element_type=jnp.float32
        )
        used = seen > 0
        used_bf16 = used.astype(jnp.bfloat16)
        for c in range(0, slots, 256):
            before = rows_of((slots, 256))
            slot = lax.broadcasted_iota(jnp.int32, (slots, 256), 1) + c
            ahead = (before < slot) & (((before ^ slot) & 28) == 0)
            place_ref[:, c : c + 256] = jnp.dot(
                used_bf16, ahead.astype(jnp.bfloat16), preferred_element_type=jnp.float32
            )
        place = place_ref[...].astype(jnp.int32)
        slot = lax.broadcasted_iota(jnp.int32, (8, slots), 1)
        over = jnp.where(used & (place >= ROWS - 1), 1.0, 0.0)
        flag_ref[...] = jnp.broadcast_to(jnp.max(over, axis=1, keepdims=True), (8, 128))
        ring = jnp.where(used & (place < ROWS - 1), (((slot >> 2) & 7) - z_ref[0]) & 7, -1)
        code = (((slot >> 5) << 2) + (slot & 3) + 1).astype(jnp.float32)
        compact_tables(ring[0:1, :], place[0:1, :], code[0:1, :], hot_ref, note_ref)

    start = pl.multiple_of(step * BLOCK, BLOCK)
    write_compact(rows_ref[:, pl.ds(start, BLOCK)], hot_ref, note_ref, outs)


def ring_repacked(z, rows):
    slots, width = rows.shape
    out = pl.pallas_call(
        ring_repack_kernel,
        out_shape=[jax.ShapeDtypeStruct((ROWS, width), jnp.bfloat16)] * RING
        + [jax.ShapeDtypeStruct((8, 128), jnp.float32)],
        grid=(width // BLOCK,),
        in_specs=[pl.BlockSpec(memory_space=pltpu.SMEM), whole((slots, width))],
        out_specs=[pl.BlockSpec((ROWS, BLOCK), lambda j: (0, j))] * RING + [whole((8, 128))],
        scratch_shapes=[
            pltpu.VMEM((RING * ROWS, slots), jnp.bfloat16),
            pltpu.VMEM((8 * RING, 128), jnp.float32),
            pltpu.VMEM((slots, 128), jnp.bfloat16),
            pltpu.VMEM((8, slots), jnp.float32),
        ],
        compiler_params=VMEM,
        cost_estimate=cost(RING * ROWS * slots * width, (RING * ROWS + slots) * width),
    )(z, rows)
    return out[:RING], out[RING]


def spread(z_ref, in_refs, hot_ref, held_ref):
    slots = hot_ref.shape[0]

    @pl.when(pl.program_id(0) == 0)
    def _():
        held_ref[...] = jnp.zeros_like(held_ref)
        for k in range(RING):
            code = in_refs[k][ROWS - 8 : ROWS, 0:128].astype(jnp.float32)[7:8, :].astype(jnp.int32)
            where = code - 1
            plane = (z_ref[0] - k) & 7
            slot = jnp.where(code > 0, ((where >> 2) << 5) + (plane << 2) + (where & 3), -1)
            hot_ref[:, 128 * k : 128 * k + 128] = (rows_of((slots, 128)) == slot).astype(
                jnp.bfloat16
            )

    for k in range(RING):
        held_ref[128 * k : 128 * k + ROWS, :] = in_refs[k][...]
    return jnp.dot(hot_ref[...], held_ref[...], preferred_element_type=jnp.float32)


def ring_spread_kernel(z_ref, *refs):
    ins, (out_ref, hot_ref, held_ref) = refs[:RING], refs[RING:]
    out_ref[...] = spread(z_ref, ins, hot_ref, held_ref).astype(jnp.bfloat16)


def ring_specs():
    return [pl.BlockSpec(memory_space=pltpu.SMEM)] + [
        pl.BlockSpec((ROWS, BLOCK), lambda j: (0, j))
    ] * RING


def ring_spread(z, parts, slots):
    width = parts[0].shape[1]
    return pl.pallas_call(
        ring_spread_kernel,
        out_shape=jax.ShapeDtypeStruct((slots, width), jnp.bfloat16),
        grid=(width // BLOCK,),
        in_specs=ring_specs(),
        out_specs=pl.BlockSpec((slots, BLOCK), lambda j: (0, j)),
        scratch_shapes=[
            pltpu.VMEM((slots, 128 * RING), jnp.bfloat16),
            pltpu.VMEM((128 * RING, BLOCK), jnp.bfloat16),
        ],
        compiler_params=VMEM,
        cost_estimate=cost(slots * 128 * RING * width, (slots + ROWS * RING) * width),
    )(z, *parts)


def place_kernel(target_ref, scale_ref, rows_ref, out_ref, hot_ref, held_ref):
    @pl.when(pl.program_id(0) == 0)
    def _():
        hot_ref[...] = (rows_of(hot_ref.shape) == target_ref[...]).astype(jnp.bfloat16)
        held_ref[...] = jnp.broadcast_to(scale_ref[...], held_ref.shape)

    scale = jnp.concatenate([held_ref[...]] * (BLOCK // 128), axis=1)
    scaled = (scale * rows_ref[...].astype(jnp.float32)).astype(jnp.bfloat16)
    out_ref[...] = jnp.dot(
        hot_ref[...], scaled, preferred_element_type=jnp.float32
    ).astype(jnp.bfloat16)


def placed_rows(target, scale, rows, shard_rows, out_width):
    slots, width = rows.shape
    return pl.pallas_call(
        place_kernel,
        out_shape=jax.ShapeDtypeStruct((shard_rows, out_width), jnp.bfloat16),
        grid=(width // BLOCK,),
        in_specs=[
            whole((1, slots)),
            whole((slots, 1)),
            pl.BlockSpec((slots, BLOCK), lambda j: (0, j)),
        ],
        out_specs=pl.BlockSpec((shard_rows, BLOCK), lambda j: (0, j)),
        scratch_shapes=[
            pltpu.VMEM((shard_rows, slots), jnp.bfloat16),
            pltpu.VMEM((slots, 128), jnp.float32),
        ],
        compiler_params=VMEM,
        cost_estimate=cost(shard_rows * slots * width, (shard_rows + slots) * width),
    )(target, scale, rows)


def rounded(x):
    return x.astype(jnp.bfloat16).astype(jnp.float32)


def ring_place_kernel(z_ref, target_ref, scale_ref, *refs):
    ins, (_, out_ref, hot_ref, held_ref, scaled_ref) = refs[:RING], refs[RING:]

    @pl.when(pl.program_id(0) == 0)
    def _():
        scaled_ref[...] = jnp.zeros_like(scaled_ref)
        row = rows_of((8, 128))
        for k in range(RING):
            code = ins[k][ROWS - 8 : ROWS, 0:128].astype(jnp.float32)[7:8, :].astype(jnp.int32)
            plane = (z_ref[0] - k) & 7
            listed = (rows_of((128, 128)) == code - 1).astype(jnp.bfloat16)
            target = target_ref[pl.ds(plane, 1), :] + 1
            scale = scale_ref[pl.ds(plane, 1), :]
            high = rounded(scale)
            middle = rounded(scale - high)
            low = scale - high - middle
            parts = [(target >> 4).astype(jnp.float32), (target & 15).astype(jnp.float32)]
            parts += [high, middle, low]
            table = jnp.zeros((8, 128), jnp.float32)
            for r, part in enumerate(parts):
                table = jnp.where(row == r, part, table)
            found = jnp.dot(
                table.astype(jnp.bfloat16), listed, preferred_element_type=jnp.float32
            )
            place = (found[0:1, :] * 16 + found[1:2, :]).astype(jnp.int32) - 1
            hot_ref[:, 128 * k : 128 * k + 128] = (
                rows_of((out_ref.shape[0], 128)) == place
            ).astype(jnp.bfloat16)
            weight = found[2:3, :] + found[3:4, :] + found[4:5, :]
            held_ref[128 * k : 128 * k + 128, :] = jnp.broadcast_to(weight, (128, 128)).T

    for k in range(RING):
        scale = held_ref[128 * k : 128 * k + ROWS, :]
        for c in range(0, BLOCK, 128):
            rows = ins[k][:, c : c + 128].astype(jnp.float32)
            scaled_ref[128 * k : 128 * k + ROWS, c : c + 128] = (scale * rows).astype(jnp.bfloat16)
    out_ref[...] = jnp.dot(
        hot_ref[...], scaled_ref[...], preferred_element_type=jnp.float32
    ).astype(jnp.bfloat16)


def ring_placed(z, target, scale, parts, half_done):
    shard_rows, out_width = half_done.shape
    width = parts[0].shape[1]
    skip = (out_width - width) // BLOCK
    return pl.pallas_call(
        ring_place_kernel,
        out_shape=jax.ShapeDtypeStruct(half_done.shape, jnp.bfloat16),
        grid=(width // BLOCK,),
        in_specs=[pl.BlockSpec(memory_space=pltpu.SMEM)]
        + [whole((RING, 128))] * 2
        + [pl.BlockSpec((ROWS, BLOCK), lambda j: (0, j))] * RING
        + [pl.BlockSpec(memory_space=pl.ANY)],
        out_specs=pl.BlockSpec((shard_rows, BLOCK), lambda j: (0, skip + j)),
        scratch_shapes=[
            pltpu.VMEM((shard_rows, 128 * RING), jnp.bfloat16),
            pltpu.VMEM((128 * RING, 128), jnp.float32),
            pltpu.VMEM((128 * RING, BLOCK), jnp.bfloat16),
        ],
        input_output_aliases={3 + RING: 0},
        compiler_params=VMEM,
        cost_estimate=cost(shard_rows * 1024 * width, (shard_rows + 704) * width),
    )(z, target, scale, *parts, half_done)


def ring_shifted(parts):
    moved = [parts[0]]
    for k in range(1, RING):
        moved.append(lax.ppermute(parts[k], "dev_0", [(i, (i + k) % RING) for i in range(RING)]))
    return moved


def in_plane(rows):
    slots, width = rows.shape
    parts = rows.reshape(COLUMNS, slots // COLUMNS, width)
    return lax.all_to_all(parts, PLANE, split_axis=0, concat_axis=0, tiled=True).reshape(
        slots, width
    )


def slot_order(table):
    return table.reshape(4, RING, 8, CAP).swapaxes(1, 2).reshape(-1)


def ring_order(table):
    return table.reshape(4, RING, 8, CAP).swapaxes(0, 1).reshape(RING, -1)


def count_earlier(key, counts):
    pos = jnp.arange(key.shape[0], dtype=jnp.int32)
    earlier = (pos[None, :] < pos[:, None]) & (key[None, :] == key[:, None]) & counts[None, :]
    return jnp.sum(earlier.astype(jnp.int32), axis=1)


def local(
    token_ids,
    sensitivity,
    last_hidden,
    lengths,
    norm_gain,
    reward_head,
    chosen_index,
    rejected_index,
    shard_owner,
):
    resp_local, block_len = token_ids.shape
    width = sensitivity.shape[2]
    half = width // 2
    tok_local = resp_local * block_len
    devices = shard_owner.shape[0]
    slots = devices * CAP
    shard_rows = VOCAB // devices
    responses = devices * resp_local
    cols = width // devices
    own_place = lax.axis_index(GRP_DEV)
    z = lax.axis_index("dev_0")[None]
    rows = sensitivity.reshape(tok_local, width)

    ids = token_ids.reshape(tok_local)
    shard_of = ids // shard_rows
    offset = ids - shard_of * shard_rows
    shard_hot = shard_of[:, None] == jnp.arange(devices, dtype=jnp.int32)[None, :]
    owner = jnp.sum(jnp.where(shard_hot, shard_owner[None, :], 0), axis=1)
    token_pos = jnp.arange(tok_local, dtype=jnp.int32)
    live = (jnp.arange(block_len, dtype=jnp.int32)[None, :] < lengths[:, None]).reshape(tok_local)
    rank = count_earlier(shard_of, jnp.ones_like(live))
    plane = (owner >> 3) & 7
    column = ((owner >> 6) << 3) + (owner & 7)
    place = count_earlier(plane, live)
    fits = live & (place < ROWS - 1)
    over_here = jnp.any(live & ~fits).astype(jnp.float32)
    ring = jnp.where(fits, (plane - z) & 7, -1)

    first = ring_packed(
        ring[None, :],
        place[None, :],
        (column * CAP + rank + 1).astype(jnp.float32)[None, :],
        rows,
        half,
    )
    first = ring_shifted(first)
    second_slot = jnp.where(live, (column << 5) + (plane << 2) + rank, -1)
    second = in_plane(packed_rows(second_slot[None, :], rows, slots, half, half))
    first[1], first[2], second = lax.optimization_barrier((first[1], first[2], second))
    second, over_there = ring_repacked(z, second)
    second = ring_shifted(second)

    code = jnp.where(live, (offset + 1) * resp_local + token_pos // block_len, 0)
    direct_slot = owner * CAP + rank
    hidden = last_hidden.astype(jnp.float32)
    norm = jnp.sqrt(jnp.mean(hidden * hidden, axis=-1, keepdims=True) + 1e-05)
    own_reward = jnp.sum(hidden / norm * norm_gain * reward_head, axis=-1)
    slot_match = direct_slot[None, :] == jnp.arange(slots, dtype=jnp.int32)[:, None]
    codes = jnp.sum(jnp.where(slot_match, code[None, :], 0), axis=1).reshape(devices, CAP)
    over = jnp.maximum(over_here, over_there[0, 0])
    own_facts = jnp.concatenate(
        [own_reward, norm[:, 0], over[None], jnp.zeros((51,), jnp.float32)]
    )
    message = jnp.concatenate(
        [
            codes.astype(jnp.float32),
            jnp.broadcast_to(own_facts[None, :], (devices, 60)),
            hidden.reshape(resp_local, devices, cols).swapaxes(0, 1).reshape(devices, -1),
        ],
        axis=1,
    )
    heard = lax.all_to_all(message, GRP_DEV, split_axis=0, concat_axis=0, tiled=True)

    first = ring_spread(z, first, slots)
    first, second[1], second[7] = lax.optimization_barrier((first, second[1], second[7]))
    first = in_plane(first)

    arrived_code = heard[:, :CAP].astype(jnp.int32)
    reward = heard[:, 4:8].reshape(responses)
    any_over = jnp.max(heard[:, 12]) > 0
    margin = reward[chosen_index] - reward[rejected_index]
    push = -jax.nn.sigmoid(-margin)
    every = jnp.arange(responses, dtype=jnp.int32)
    sign_table = (chosen_index[None, :] == every[:, None]).astype(jnp.float32) - (
        rejected_index[None, :] == every[:, None]
    ).astype(jnp.float32)
    reward_grad = jnp.sum(sign_table * push[None, :], axis=1).reshape(devices, resp_local)
    own_gain = lax.dynamic_slice(norm_gain, (own_place * cols,), (cols,))
    head_grad = jnp.zeros((cols,), jnp.float32)
    for r in range(resp_local):
        normed = heard[:, 64 + r * cols : 64 + (r + 1) * cols] / heard[:, 8 + r : 9 + r] * own_gain
        head_grad += jnp.sum(reward_grad[:, r : r + 1] * normed, axis=0)

    response_in = arrived_code % resp_local
    scale = jnp.zeros(arrived_code.shape, jnp.float32)
    for r in range(resp_local):
        scale = jnp.where(response_in == r, reward_grad[:, r : r + 1], scale)
    target = arrived_code // resp_local - 1
    scale = jnp.where(target >= 0, scale, 0.0)
    target_row = slot_order(target)[None, :]
    scale_column = slot_order(scale)[:, None]
    half_done = placed_rows(target_row, scale_column, first, shard_rows, width)

    def by_ring():
        return ring_placed(z, ring_order(target), ring_order(scale), second, half_done)

    def direct():
        sent = packed_rows(
            jnp.where(live, direct_slot, -1)[None, :], rows, slots, 0, width
        ).reshape(devices, CAP, width)
        arrived = lax.all_to_all(sent, GRP_DEV, split_axis=0, concat_axis=0, tiled=True)
        return placed_rows(
            target.reshape(1, slots),
            scale.reshape(slots, 1),
            arrived.reshape(slots, width),
            shard_rows,
            width,
        )

    return (lax.cond(any_over, direct, by_ring), head_grad)


def solution(mesh):
    torus = Mesh(
        mesh.devices.reshape(mesh.shape["grp"], 8, 4, 2), ("grp", "dev_0", "dev_1", "dev_2")
    )
    placed_as = (
        P(GRP_DEV, None),
        P(GRP_DEV, None, None),
        P(GRP_DEV, None),
        P(GRP_DEV),
        P(),
        P(),
        P(),
        P(),
        P(),
    )
    return jax.shard_map(
        local,
        mesh=torus,
        in_specs=placed_as,
        out_specs=(P(GRP_DEV, None), P(GRP_DEV)),
        check_vma=False,
    )
```

```python
import functools

import jax
import jax.numpy as jnp
from jax import lax
from jax.experimental import pallas as pl
from jax.experimental.pallas import tpu as pltpu
from jax.sharding import Mesh
from jax.sharding import PartitionSpec as P

VOCAB = 128256
CAP = 4
GRP_DEV = ("grp", "dev_0", "dev_1", "dev_2")
PLANE = ("grp", "dev_1", "dev_2")
RING = 8
COLUMNS = 32
ROWS = 88
BLOCK = 512
VMEM = pltpu.CompilerParams(vmem_limit_bytes=48 << 20)
NT = (((1,), (1,)), ((), ()))


def cost(contractions, elements):
    return pl.CostEstimate(flops=2 * contractions, bytes_accessed=2 * elements, transcendentals=0)


def rows_of(shape):
    return lax.broadcasted_iota(jnp.int32, shape, 0)


def whole(shape):
    return pl.BlockSpec(shape, lambda j: (0,) * len(shape))


def pack_kernel(slot_ref, rows_ref, out_ref, hot_ref):
    @pl.when(pl.program_id(0) == 0)
    def _():
        hot_ref[...] = (rows_of(hot_ref.shape) == slot_ref[...]).astype(jnp.bfloat16)

    out_ref[...] = jnp.dot(
        hot_ref[...], rows_ref[...], preferred_element_type=jnp.float32
    ).astype(jnp.bfloat16)


def packed_rows(slot, rows, slots, first, width):
    tokens = rows.shape[0]
    skip = first // BLOCK
    return pl.pallas_call(
        pack_kernel,
        out_shape=jax.ShapeDtypeStruct((slots, width), jnp.bfloat16),
        grid=(width // BLOCK,),
        in_specs=[
            whole((1, tokens)),
            pl.BlockSpec((tokens, BLOCK), lambda j: (0, skip + j)),
        ],
        out_specs=pl.BlockSpec((slots, BLOCK), lambda j: (0, j)),
        scratch_shapes=[pltpu.VMEM((slots, tokens), jnp.bfloat16)],
        compiler_params=VMEM,
        cost_estimate=cost(slots * tokens * width, (slots + tokens) * width),
    )(slot, rows)


def compact_tables(ring, place, code, hot_ref, note_ref):
    count = ring.shape[1]
    row = jnp.where(ring >= 0, ring * ROWS + place, -1)
    hot_ref[...] = (rows_of((RING * ROWS, count)) == row).astype(jnp.bfloat16)
    codes = jnp.broadcast_to(code, (8, count)).astype(jnp.bfloat16)
    for k in range(RING):
        mine = rows_of((128, count)) == jnp.where(ring == k, place, -1)
        note_ref[8 * k : 8 * k + 8, :] = lax.dot_general(
            codes, mine.astype(jnp.bfloat16), NT, preferred_element_type=jnp.float32
        )


def write_compact(rows, hot_ref, note_ref, out_refs):
    picked = jnp.dot(hot_ref[...], rows, preferred_element_type=jnp.float32)
    for k in range(RING):
        out_refs[k][...] = picked[k * ROWS : (k + 1) * ROWS].astype(jnp.bfloat16)

    @pl.when(pl.program_id(0) == 0)
    def _():
        for k in range(RING):
            tail = picked[(k + 1) * ROWS - 8 : (k + 1) * ROWS, :128]
            note = jnp.where(rows_of((8, 128)) == 7, note_ref[8 * k : 8 * k + 8, :], 0.0)
            out_refs[k][ROWS - 8 : ROWS, 0:128] = (tail + note).astype(jnp.bfloat16)


def ring_pack_kernel(ring_ref, place_ref, code_ref, rows_ref, *refs):
    outs, (hot_ref, note_ref) = refs[:RING], refs[RING:]

    @pl.when(pl.program_id(0) == 0)
    def _():
        compact_tables(ring_ref[...], place_ref[...], code_ref[...], hot_ref, note_ref)

    write_compact(rows_ref[...], hot_ref, note_ref, outs)


def ring_packed(ring, place, code, rows, width):
    tokens = rows.shape[0]
    return pl.pallas_call(
        ring_pack_kernel,
        out_shape=[jax.ShapeDtypeStruct((ROWS, width), jnp.bfloat16)] * RING,
        grid=(width // BLOCK,),
        in_specs=[whole((1, tokens))] * 3 + [pl.BlockSpec((tokens, BLOCK), lambda j: (0, j))],
        out_specs=[pl.BlockSpec((ROWS, BLOCK), lambda j: (0, j))] * RING,
        scratch_shapes=[
            pltpu.VMEM((RING * ROWS, tokens), jnp.bfloat16),
            pltpu.VMEM((8 * RING, 128), jnp.float32),
        ],
        compiler_params=VMEM,
        cost_estimate=cost(RING * ROWS * tokens * width, (RING * ROWS + tokens) * width),
    )(ring, place, code, rows)


def ring_repack_kernel(z_ref, rows_ref, *refs):
    outs, flag_ref = refs[:RING], refs[RING]
    hot_ref, note_ref, place_ref, held_ref = refs[RING + 1 :]
    width = rows_ref.shape[2]
    step = pl.program_id(0)

    @pl.when(step == 0)
    def _():
        lane = lax.broadcasted_iota(jnp.int32, (8, 256), 1)
        before = rows_of((256, 256))
        slot = lax.broadcasted_iota(jnp.int32, (256, 256), 1)
        ahead = ((before < slot) & (((before ^ slot) & 4) == 0)).astype(jnp.bfloat16)
        over = jnp.zeros((8, 256), jnp.float32)
        for q in range(RING // 2):
            total = jnp.zeros((COLUMNS, 8, 128), jnp.float32)
            for c in range(0, width, 128):
                total += jnp.abs(
                    rows_ref[:, 8 * q : 8 * q + 8, c : c + 128].astype(jnp.float32)
                )
            filled = (total.reshape(256, 128) > 0).astype(jnp.bfloat16)
            seen = lax.dot_general(
                jnp.ones((8, 128), jnp.bfloat16), filled, NT, preferred_element_type=jnp.float32
            )
            used = seen > 0
            place = jnp.dot(
                used.astype(jnp.bfloat16), ahead, preferred_element_type=jnp.float32
            )
            over = jnp.maximum(over, jnp.where(used & (place >= ROWS - 1), 1.0, 0.0))
            place_ref[8 * q : 8 * q + 8, :] = jnp.where(
                used & (place < ROWS - 1), place, -1.0
            ).astype(jnp.int32)
        flag_ref[...] = jnp.broadcast_to(jnp.max(over, axis=1, keepdims=True), (8, 128))
        codes = (((lane >> 3) << 2) + (lane & 3) + 1).astype(jnp.float32).astype(jnp.bfloat16)
        for k in range(RING):
            plane = (z_ref[0] + k) & 7
            start = pl.multiple_of((plane >> 1) * 8, 8)
            mine = ((lane >> 2) & 1) == (plane & 1)
            place = jnp.where(mine, place_ref[pl.ds(start, 8), :], -1)[0:1, :]
            hot_ref[k] = (rows_of((ROWS, 256)) == place).astype(jnp.bfloat16)
            note_ref[8 * k : 8 * k + 8, :] = lax.dot_general(
                codes,
                (rows_of((128, 256)) == place).astype(jnp.bfloat16),
                NT,
                preferred_element_type=jnp.float32,
            )

    first = pl.multiple_of(step * BLOCK, BLOCK)
    for q in range(RING // 2):
        rows = rows_ref[:, 8 * q : 8 * q + 8, pl.ds(first, BLOCK)].astype(jnp.float32)
        held_ref[256 * q : 256 * q + 256, :] = rows.reshape(256, BLOCK).astype(jnp.bfloat16)
    for k in range(RING):
        start = pl.multiple_of((((z_ref[0] + k) & 7) >> 1) * 256, 256)
        picked = jnp.dot(
            hot_ref[k], held_ref[pl.ds(start, 256), :], preferred_element_type=jnp.float32
        )
        outs[k][...] = picked.astype(jnp.bfloat16)

        @pl.when(step == 0)
        def _():
            note = jnp.where(rows_of((8, 128)) == 7, note_ref[8 * k : 8 * k + 8, :], 0.0)
            outs[k][ROWS - 8 : ROWS, 0:128] = (picked[ROWS - 8 :, :128] + note).astype(
                jnp.bfloat16
            )


def ring_repacked(z, rows):
    width = rows.shape[2]
    out = pl.pallas_call(
        ring_repack_kernel,
        out_shape=[jax.ShapeDtypeStruct((ROWS, width), jnp.bfloat16)] * RING
        + [jax.ShapeDtypeStruct((8, 128), jnp.float32)],
        grid=(width // BLOCK,),
        in_specs=[pl.BlockSpec(memory_space=pltpu.SMEM), whole(rows.shape)],
        out_specs=[pl.BlockSpec((ROWS, BLOCK), lambda j: (0, j))] * RING + [whole((8, 128))],
        scratch_shapes=[
            pltpu.VMEM((RING, ROWS, 256), jnp.bfloat16),
            pltpu.VMEM((8 * RING, 128), jnp.float32),
            pltpu.VMEM((4 * RING, 256), jnp.int32),
            pltpu.VMEM((128 * RING, BLOCK), jnp.bfloat16),
        ],
        compiler_params=VMEM,
        cost_estimate=cost(RING * ROWS * 256 * width, (RING * ROWS + 1024) * width),
    )(z, rows)
    return out[:RING], out[RING]


def ring_spread_kernel(z_ref, *refs):
    ins, (out_ref, hot_ref, held_ref) = refs[:RING], refs[RING:]

    @pl.when(pl.program_id(0) == 0)
    def _():
        held_ref[...] = jnp.zeros_like(held_ref)
        for k in range(RING):
            code = ins[k][ROWS - 8 : ROWS, 0:128].astype(jnp.float32)[7:8, :].astype(jnp.int32)
            where = code - 1
            plane = (z_ref[0] - k) & 7
            slot = ((where >> 2) << 3) + ((plane & 1) << 2) + (where & 3)
            hot_ref[plane] = (rows_of((256, 128)) == jnp.where(code > 0, slot, -1)).astype(
                jnp.bfloat16
            )

    for k in range(RING):
        start = pl.multiple_of(((z_ref[0] - k) & 7) * 128, 128)
        held_ref[pl.ds(start, ROWS), :] = ins[k][...]
    for q in range(RING // 2):
        hot = jnp.concatenate([hot_ref[2 * q], hot_ref[2 * q + 1]], axis=1)
        picked = jnp.dot(
            hot, held_ref[256 * q : 256 * q + 256, :], preferred_element_type=jnp.float32
        )
        out_ref[:, 8 * q : 8 * q + 8, :] = picked.reshape(COLUMNS, 8, BLOCK).astype(jnp.bfloat16)


def ring_spread(z, parts):
    width = parts[0].shape[1]
    return pl.pallas_call(
        ring_spread_kernel,
        out_shape=jax.ShapeDtypeStruct((COLUMNS, CAP * RING, width), jnp.bfloat16),
        grid=(width // BLOCK,),
        in_specs=[pl.BlockSpec(memory_space=pltpu.SMEM)]
        + [pl.BlockSpec((ROWS, BLOCK), lambda j: (0, j))] * RING,
        out_specs=pl.BlockSpec((COLUMNS, CAP * RING, BLOCK), lambda j: (0, 0, j)),
        scratch_shapes=[
            pltpu.VMEM((RING, 256, 128), jnp.bfloat16),
            pltpu.VMEM((128 * RING, BLOCK), jnp.bfloat16),
        ],
        compiler_params=VMEM,
        cost_estimate=cost(1024 * 256 * width, (1024 + ROWS * RING) * width),
    )(z, *parts)


def place_kernel(target_ref, scale_ref, rows_ref, out_ref, hot_ref, held_ref):
    @pl.when(pl.program_id(0) == 0)
    def _():
        hot_ref[...] = (rows_of(hot_ref.shape) == target_ref[...]).astype(jnp.bfloat16)
        held_ref[...] = jnp.broadcast_to(scale_ref[...], held_ref.shape)

    scale = jnp.concatenate([held_ref[...]] * (BLOCK // 128), axis=1)
    scaled = (scale * rows_ref[...].astype(jnp.float32)).astype(jnp.bfloat16)
    out_ref[...] = jnp.dot(
        hot_ref[...], scaled, preferred_element_type=jnp.float32
    ).astype(jnp.bfloat16)


def placed_rows(target, scale, rows, shard_rows, out_width):
    slots, width = rows.shape
    return pl.pallas_call(
        place_kernel,
        out_shape=jax.ShapeDtypeStruct((shard_rows, out_width), jnp.bfloat16),
        grid=(width // BLOCK,),
        in_specs=[
            whole((1, slots)),
            whole((slots, 1)),
            pl.BlockSpec((slots, BLOCK), lambda j: (0, j)),
        ],
        out_specs=pl.BlockSpec((shard_rows, BLOCK), lambda j: (0, j)),
        scratch_shapes=[
            pltpu.VMEM((shard_rows, slots), jnp.bfloat16),
            pltpu.VMEM((slots, 128), jnp.float32),
        ],
        compiler_params=VMEM,
        cost_estimate=cost(shard_rows * slots * width, (shard_rows + slots) * width),
    )(target, scale, rows)


def rounded(x):
    return x.astype(jnp.bfloat16).astype(jnp.float32)


def ring_place_kernel(z_ref, target_ref, scale_ref, *refs):
    ins, (_, out_ref, hot_ref, held_ref, scaled_ref) = refs[:RING], refs[RING:]

    @pl.when(pl.program_id(0) == 0)
    def _():
        scaled_ref[...] = jnp.zeros_like(scaled_ref)
        row = rows_of((8, 128))
        for k in range(RING):
            code = ins[k][ROWS - 8 : ROWS, 0:128].astype(jnp.float32)[7:8, :].astype(jnp.int32)
            plane = (z_ref[0] - k) & 7
            listed = (rows_of((128, 128)) == code - 1).astype(jnp.bfloat16)
            target = target_ref[pl.ds(plane, 1), :] + 1
            scale = scale_ref[pl.ds(plane, 1), :]
            high = rounded(scale)
            middle = rounded(scale - high)
            low = scale - high - middle
            parts = [(target >> 4).astype(jnp.float32), (target & 15).astype(jnp.float32)]
            parts += [high, middle, low]
            table = jnp.zeros((8, 128), jnp.float32)
            for r, part in enumerate(parts):
                table = jnp.where(row == r, part, table)
            found = jnp.dot(
                table.astype(jnp.bfloat16), listed, preferred_element_type=jnp.float32
            )
            place = (found[0:1, :] * 16 + found[1:2, :]).astype(jnp.int32) - 1
            hot_ref[:, 128 * k : 128 * k + 128] = (
                rows_of((out_ref.shape[0], 128)) == place
            ).astype(jnp.bfloat16)
            weight = found[2:3, :] + found[3:4, :] + found[4:5, :]
            held_ref[128 * k : 128 * k + 128, :] = jnp.broadcast_to(weight, (128, 128)).T

    for k in range(RING):
        scale = held_ref[128 * k : 128 * k + ROWS, :]
        for c in range(0, BLOCK, 128):
            rows = ins[k][:, c : c + 128].astype(jnp.float32)
            scaled_ref[128 * k : 128 * k + ROWS, c : c + 128] = (scale * rows).astype(jnp.bfloat16)
    out_ref[...] = jnp.dot(
        hot_ref[...], scaled_ref[...], preferred_element_type=jnp.float32
    ).astype(jnp.bfloat16)


def ring_placed(z, target, scale, parts, half_done):
    shard_rows, out_width = half_done.shape
    width = parts[0].shape[1]
    skip = (out_width - width) // BLOCK
    return pl.pallas_call(
        ring_place_kernel,
        out_shape=jax.ShapeDtypeStruct(half_done.shape, jnp.bfloat16),
        grid=(width // BLOCK,),
        in_specs=[pl.BlockSpec(memory_space=pltpu.SMEM)]
        + [whole((RING, 128))] * 2
        + [pl.BlockSpec((ROWS, BLOCK), lambda j: (0, j))] * RING
        + [pl.BlockSpec(memory_space=pl.ANY)],
        out_specs=pl.BlockSpec((shard_rows, BLOCK), lambda j: (0, skip + j)),
        scratch_shapes=[
            pltpu.VMEM((shard_rows, 128 * RING), jnp.bfloat16),
            pltpu.VMEM((128 * RING, 128), jnp.float32),
            pltpu.VMEM((128 * RING, BLOCK), jnp.bfloat16),
        ],
        input_output_aliases={3 + RING: 0},
        compiler_params=VMEM,
        cost_estimate=cost(shard_rows * 1024 * width, (shard_rows + 704) * width),
    )(z, target, scale, *parts, half_done)


def ring_shifted(parts):
    moved = [parts[0]]
    for k in range(1, RING):
        moved.append(lax.ppermute(parts[k], "dev_0", [(i, (i + k) % RING) for i in range(RING)]))
    return moved


def in_plane(parts):
    return lax.all_to_all(parts, PLANE, split_axis=0, concat_axis=0, tiled=True)


def by_device(table):
    rest = table.shape[1:]
    return table.reshape(4, 8, RING, *rest).swapaxes(1, 2).reshape(-1, *rest)


def by_column(table):
    rest = table.shape[1:]
    return table.reshape(4, RING, 8, *rest).swapaxes(1, 2).reshape(-1, *rest)


def count_earlier(key, counts):
    pos = jnp.arange(key.shape[0], dtype=jnp.int32)
    earlier = (pos[None, :] < pos[:, None]) & (key[None, :] == key[:, None]) & counts[None, :]
    return jnp.sum(earlier.astype(jnp.int32), axis=1)


def local(
    token_ids,
    sensitivity,
    last_hidden,
    lengths,
    norm_gain,
    reward_head,
    chosen_index,
    rejected_index,
    shard_owner,
):
    resp_local, block_len = token_ids.shape
    width = sensitivity.shape[2]
    half = width // 2
    tok_local = resp_local * block_len
    devices = shard_owner.shape[0]
    slots = devices * CAP
    shard_rows = VOCAB // devices
    responses = devices * resp_local
    cols = width // devices
    own_place = lax.axis_index(GRP_DEV)
    z = lax.axis_index("dev_0")[None]
    rows = sensitivity.reshape(tok_local, width)

    ids = token_ids.reshape(tok_local)
    shard_of = ids // shard_rows
    offset = ids - shard_of * shard_rows
    shard_hot = shard_of[:, None] == jnp.arange(devices, dtype=jnp.int32)[None, :]
    owner = jnp.sum(jnp.where(shard_hot, shard_owner[None, :], 0), axis=1)
    token_pos = jnp.arange(tok_local, dtype=jnp.int32)
    live = (jnp.arange(block_len, dtype=jnp.int32)[None, :] < lengths[:, None]).reshape(tok_local)
    rank = count_earlier(shard_of, jnp.ones_like(live))
    plane = (owner >> 3) & 7
    column = ((owner >> 6) << 3) + (owner & 7)
    place = count_earlier(plane, live)
    fits = live & (place < ROWS - 1)
    over_here = jnp.any(live & ~fits).astype(jnp.float32)
    ring = jnp.where(fits, (plane - z) & 7, -1)

    first = ring_packed(
        ring[None, :],
        place[None, :],
        (column * CAP + rank + 1).astype(jnp.float32)[None, :],
        rows,
        half,
    )
    first = ring_shifted(first)
    second_slot = jnp.where(live, (column << 5) + (plane << 2) + rank, -1)
    second = packed_rows(second_slot[None, :], rows, slots, half, half)
    second = in_plane(second.reshape(COLUMNS, CAP * RING, half))
    first[1], first[2], second = lax.optimization_barrier((first[1], first[2], second))
    second, over_there = ring_repacked(z, second)
    second = ring_shifted(second)

    code = jnp.where(live, (offset + 1) * resp_local + token_pos // block_len, 0)
    note_slot = (plane * COLUMNS + column) * CAP + rank
    hidden = last_hidden.astype(jnp.float32)
    norm = jnp.sqrt(jnp.mean(hidden * hidden, axis=-1, keepdims=True) + 1e-05)
    own_reward = jnp.sum(hidden / norm * norm_gain * reward_head, axis=-1)
    slot_match = note_slot[None, :] == jnp.arange(slots, dtype=jnp.int32)[:, None]
    codes = jnp.sum(jnp.where(slot_match, code[None, :], 0), axis=1).reshape(devices, CAP)
    hidden_cols = hidden.reshape(resp_local, 4, RING, 8, cols).transpose(2, 1, 3, 0, 4)
    own_facts = jnp.concatenate([own_reward, norm[:, 0], over_here[None]])
    ready = jnp.concatenate(
        [
            codes.astype(jnp.float32),
            jnp.broadcast_to(own_facts[None, :], (devices, 9)),
            jnp.zeros((devices, 51), jnp.float32),
            hidden_cols.reshape(devices, resp_local * cols),
        ],
        axis=1,
    )
    lane = jnp.arange(128, dtype=jnp.int32)
    message = jnp.where(lane[None, :] == 13, over_there[0, 0], ready)
    message = message.reshape(RING, COLUMNS, 128)
    message = lax.all_to_all(message, "dev_0", split_axis=0, concat_axis=0, tiled=True)
    heard = in_plane(message.swapaxes(0, 1)).reshape(devices, 128)

    first = ring_spread(z, first)
    first, second[1], second[7] = lax.optimization_barrier((first, second[1], second[7]))
    first = in_plane(first)

    arrived_code = heard[:, :CAP].astype(jnp.int32)
    reward = by_device(heard[:, 4:8]).reshape(responses)
    any_over = jnp.max(heard[:, 12:14]) > 0
    margin = reward[chosen_index] - reward[rejected_index]
    push = -jax.nn.sigmoid(-margin)
    every = jnp.arange(responses, dtype=jnp.int32)
    sign_table = (chosen_index[None, :] == every[:, None]).astype(jnp.float32) - (
        rejected_index[None, :] == every[:, None]
    ).astype(jnp.float32)
    reward_grad = jnp.sum(sign_table * push[None, :], axis=1).reshape(devices, resp_local)
    reward_grad = by_column(reward_grad)
    own_gain = lax.dynamic_slice(norm_gain, (own_place * cols,), (cols,))
    head_grad = jnp.zeros((cols,), jnp.float32)
    for r in range(resp_local):
        normed = heard[:, 64 + r * cols : 64 + (r + 1) * cols] / heard[:, 8 + r : 9 + r] * own_gain
        head_grad += jnp.sum(reward_grad[:, r : r + 1] * normed, axis=0)

    response_in = arrived_code % resp_local
    scale = jnp.zeros(arrived_code.shape, jnp.float32)
    for r in range(resp_local):
        scale = jnp.where(response_in == r, reward_grad[:, r : r + 1], scale)
    target = arrived_code // resp_local - 1
    scale = jnp.where(target >= 0, scale, 0.0)
    half_done = placed_rows(
        target.reshape(1, slots),
        scale.reshape(slots, 1),
        first.reshape(slots, half),
        shard_rows,
        width,
    )

    def by_plane(table):
        return table.reshape(COLUMNS, RING, CAP).swapaxes(0, 1).reshape(RING, -1)

    def by_ring():
        return ring_placed(z, by_plane(target), by_plane(scale), second, half_done)

    def direct():
        sent = packed_rows(
            jnp.where(live, owner * CAP + rank, -1)[None, :], rows, slots, 0, width
        ).reshape(devices, CAP, width)
        arrived = lax.all_to_all(sent, GRP_DEV, split_axis=0, concat_axis=0, tiled=True)
        return placed_rows(
            by_device(target).reshape(1, slots),
            by_device(scale).reshape(slots, 1),
            arrived.reshape(slots, width),
            shard_rows,
            width,
        )

    return (lax.cond(any_over, direct, by_ring), head_grad)


def solution(mesh):
    torus = Mesh(
        mesh.devices.reshape(mesh.shape["grp"], 8, 4, 2), ("grp", "dev_0", "dev_1", "dev_2")
    )
    placed_as = (
        P(GRP_DEV, None),
        P(GRP_DEV, None, None),
        P(GRP_DEV, None),
        P(GRP_DEV),
        P(),
        P(),
        P(),
        P(),
        P(),
    )
    return jax.shard_map(
        local,
        mesh=torus,
        in_specs=placed_as,
        out_specs=(P(GRP_DEV, None), P(GRP_DEV)),
        check_vma=False,
    )
```

```python
import functools

import jax
import jax.numpy as jnp
from jax import lax
from jax.experimental import pallas as pl
from jax.experimental.pallas import tpu as pltpu
from jax.sharding import Mesh
from jax.sharding import PartitionSpec as P

VOCAB = 128256
CAP = 4
GRP_DEV = ("grp", "dev_0", "dev_1", "dev_2")
PLANE = ("grp", "dev_1", "dev_2")
RING = 8
COLUMNS = 32
ROWS = 88
BLOCK = 512
VMEM = pltpu.CompilerParams(vmem_limit_bytes=48 << 20)
NT = (((1,), (1,)), ((), ()))


def cost(contractions, elements):
    return pl.CostEstimate(flops=2 * contractions, bytes_accessed=2 * elements, transcendentals=0)


def rows_of(shape):
    return lax.broadcasted_iota(jnp.int32, shape, 0)


def whole(shape):
    return pl.BlockSpec(shape, lambda j: (0,) * len(shape))


def pack_kernel(slot_ref, rows_ref, out_ref, hot_ref):
    @pl.when(pl.program_id(0) == 0)
    def _():
        hot_ref[...] = (rows_of(hot_ref.shape) == slot_ref[...]).astype(jnp.bfloat16)

    out_ref[...] = jnp.dot(
        hot_ref[...], rows_ref[...], preferred_element_type=jnp.float32
    ).astype(jnp.bfloat16)


def packed_rows(slot, rows, slots, first, width):
    tokens = rows.shape[0]
    skip = first // BLOCK
    return pl.pallas_call(
        pack_kernel,
        out_shape=jax.ShapeDtypeStruct((slots, width), jnp.bfloat16),
        grid=(width // BLOCK,),
        in_specs=[
            whole((1, tokens)),
            pl.BlockSpec((tokens, BLOCK), lambda j: (0, skip + j)),
        ],
        out_specs=pl.BlockSpec((slots, BLOCK), lambda j: (0, j)),
        scratch_shapes=[pltpu.VMEM((slots, tokens), jnp.bfloat16)],
        compiler_params=VMEM,
        cost_estimate=cost(slots * tokens * width, (slots + tokens) * width),
    )(slot, rows)


def compact_tables(ring, place, code, hot_ref, note_ref):
    count = ring.shape[1]
    row = jnp.where(ring >= 0, ring * ROWS + place, -1)
    hot_ref[...] = (rows_of((RING * ROWS, count)) == row).astype(jnp.bfloat16)
    codes = jnp.broadcast_to(code, (8, count)).astype(jnp.bfloat16)
    for k in range(RING):
        mine = rows_of((128, count)) == jnp.where(ring == k, place, -1)
        note_ref[8 * k : 8 * k + 8, :] = lax.dot_general(
            codes, mine.astype(jnp.bfloat16), NT, preferred_element_type=jnp.float32
        )


def write_compact(rows, hot_ref, note_ref, out_refs):
    picked = jnp.dot(hot_ref[...], rows, preferred_element_type=jnp.float32)
    for k in range(RING):
        out_refs[k][...] = picked[k * ROWS : (k + 1) * ROWS].astype(jnp.bfloat16)

    @pl.when(pl.program_id(0) == 0)
    def _():
        for k in range(RING):
            tail = picked[(k + 1) * ROWS - 8 : (k + 1) * ROWS, :128]
            note = jnp.where(rows_of((8, 128)) == 7, note_ref[8 * k : 8 * k + 8, :], 0.0)
            out_refs[k][ROWS - 8 : ROWS, 0:128] = (tail + note).astype(jnp.bfloat16)


def both_pack_kernel(ring_ref, place_ref, code_ref, slot_ref, first_ref, second_ref, *refs):
    outs, (second_out_ref, hot_ref, note_ref, slot_hot_ref) = refs[:RING], refs[RING:]

    @pl.when(pl.program_id(0) == 0)
    def _():
        compact_tables(ring_ref[...], place_ref[...], code_ref[...], hot_ref, note_ref)
        slot_hot_ref[...] = (rows_of(slot_hot_ref.shape) == slot_ref[...]).astype(jnp.bfloat16)

    write_compact(first_ref[...], hot_ref, note_ref, outs)
    second_out_ref[...] = jnp.dot(
        slot_hot_ref[...], second_ref[...], preferred_element_type=jnp.float32
    ).astype(jnp.bfloat16)


def both_packed(ring, place, code, slot, rows, slots, half):
    tokens = rows.shape[0]
    steps = half // BLOCK
    out = pl.pallas_call(
        both_pack_kernel,
        out_shape=[jax.ShapeDtypeStruct((ROWS, half), jnp.bfloat16)] * RING
        + [jax.ShapeDtypeStruct((slots, half), jnp.bfloat16)],
        grid=(steps,),
        in_specs=[whole((1, tokens))] * 4
        + [
            pl.BlockSpec((tokens, BLOCK), lambda j: (0, j)),
            pl.BlockSpec((tokens, BLOCK), lambda j: (0, steps + j)),
        ],
        out_specs=[pl.BlockSpec((ROWS, BLOCK), lambda j: (0, j))] * RING
        + [pl.BlockSpec((slots, BLOCK), lambda j: (0, j))],
        scratch_shapes=[
            pltpu.VMEM((RING * ROWS, tokens), jnp.bfloat16),
            pltpu.VMEM((8 * RING, 128), jnp.float32),
            pltpu.VMEM((slots, tokens), jnp.bfloat16),
        ],
        compiler_params=VMEM,
        cost_estimate=cost(
            (RING * ROWS + slots) * tokens * half, (RING * ROWS + slots + 2 * tokens) * half
        ),
    )(ring, place, code, slot, rows, rows)
    return out[:RING], out[RING]


def ring_repack_kernel(z_ref, rows_ref, *refs):
    outs, flag_ref = refs[:RING], refs[RING]
    hot_ref, note_ref, place_ref, held_ref, sent_ref = refs[RING + 1 :]
    width = rows_ref.shape[2]
    step = pl.program_id(0)

    @pl.when(step == 0)
    def _():
        lane = lax.broadcasted_iota(jnp.int32, (8, 256), 1)
        before = rows_of((256, 256))
        slot = lax.broadcasted_iota(jnp.int32, (256, 256), 1)
        ahead = ((before < slot) & (((before ^ slot) & 4) == 0)).astype(jnp.bfloat16)
        over = jnp.zeros((8, 256), jnp.float32)
        for q in range(RING // 2):
            total = jnp.zeros((COLUMNS, 8, 128), jnp.float32)
            for c in range(0, width, 128):
                total += jnp.abs(
                    rows_ref[:, 8 * q : 8 * q + 8, c : c + 128].astype(jnp.float32)
                )
            filled = (total.reshape(256, 128) > 0).astype(jnp.bfloat16)
            seen = lax.dot_general(
                jnp.ones((8, 128), jnp.bfloat16), filled, NT, preferred_element_type=jnp.float32
            )
            used = seen > 0
            place = jnp.dot(
                used.astype(jnp.bfloat16), ahead, preferred_element_type=jnp.float32
            )
            over = jnp.maximum(over, jnp.where(used & (place >= ROWS - 1), 1.0, 0.0))
            place_ref[8 * q : 8 * q + 8, :] = jnp.where(
                used & (place < ROWS - 1), place, -1.0
            ).astype(jnp.int32)
        flag_ref[...] = jnp.broadcast_to(jnp.max(over, axis=1, keepdims=True), (8, 128))
        codes = (((lane >> 3) << 2) + (lane & 3) + 1).astype(jnp.float32).astype(jnp.bfloat16)
        for k in range(RING):
            plane = (z_ref[0] + k) & 7
            start = pl.multiple_of((plane >> 1) * 8, 8)
            mine = ((lane >> 2) & 1) == (plane & 1)
            place = jnp.where(mine, place_ref[pl.ds(start, 8), :], -1)[0:1, :]
            hot_ref[plane] = (rows_of((ROWS, 256)) == place).astype(jnp.bfloat16)
            note_ref[8 * k : 8 * k + 8, :] = lax.dot_general(
                codes,
                (rows_of((128, 256)) == place).astype(jnp.bfloat16),
                NT,
                preferred_element_type=jnp.float32,
            )

    first = pl.multiple_of(step * BLOCK, BLOCK)
    for q in range(RING // 2):
        rows = rows_ref[:, 8 * q : 8 * q + 8, pl.ds(first, BLOCK)].astype(jnp.float32)
        held_ref[256 * q : 256 * q + 256, :] = rows.reshape(256, BLOCK).astype(jnp.bfloat16)
    for q in range(RING // 2):
        hot = jnp.concatenate([hot_ref[2 * q], hot_ref[2 * q + 1]], axis=0)
        picked = jnp.dot(
            hot, held_ref[256 * q : 256 * q + 256, :], preferred_element_type=jnp.float32
        )
        for half in (0, 1):
            k = (2 * q + half - z_ref[0]) & 7
            sent_ref[k] = picked[half * ROWS : (half + 1) * ROWS].astype(jnp.bfloat16)
    for k in range(RING):
        outs[k][...] = sent_ref[k]

    @pl.when(step == 0)
    def _():
        for k in range(RING):
            tail = sent_ref[k, ROWS - 8 : ROWS, 0:128].astype(jnp.float32)
            note = jnp.where(rows_of((8, 128)) == 7, note_ref[8 * k : 8 * k + 8, :], 0.0)
            outs[k][ROWS - 8 : ROWS, 0:128] = (tail + note).astype(jnp.bfloat16)


def ring_repacked(z, rows):
    width = rows.shape[2]
    out = pl.pallas_call(
        ring_repack_kernel,
        out_shape=[jax.ShapeDtypeStruct((ROWS, width), jnp.bfloat16)] * RING
        + [jax.ShapeDtypeStruct((8, 128), jnp.float32)],
        grid=(width // BLOCK,),
        in_specs=[pl.BlockSpec(memory_space=pltpu.SMEM), whole(rows.shape)],
        out_specs=[pl.BlockSpec((ROWS, BLOCK), lambda j: (0, j))] * RING + [whole((8, 128))],
        scratch_shapes=[
            pltpu.VMEM((RING, ROWS, 256), jnp.bfloat16),
            pltpu.VMEM((8 * RING, 128), jnp.float32),
            pltpu.VMEM((4 * RING, 256), jnp.int32),
            pltpu.VMEM((128 * RING, BLOCK), jnp.bfloat16),
            pltpu.VMEM((RING, ROWS, BLOCK), jnp.bfloat16),
        ],
        compiler_params=VMEM,
        cost_estimate=cost(RING * ROWS * 256 * width, (RING * ROWS + 1024) * width),
    )(z, rows)
    return out[:RING], out[RING]


def ring_spread_kernel(z_ref, *refs):
    ins, (out_ref, hot_ref, held_ref) = refs[:RING], refs[RING:]

    @pl.when(pl.program_id(0) == 0)
    def _():
        held_ref[...] = jnp.zeros_like(held_ref)
        for k in range(RING):
            code = ins[k][ROWS - 8 : ROWS, 0:128].astype(jnp.float32)[7:8, :].astype(jnp.int32)
            where = code - 1
            plane = (z_ref[0] - k) & 7
            slot = ((where >> 2) << 3) + ((plane & 1) << 2) + (where & 3)
            hot_ref[plane] = (rows_of((256, 128)) == jnp.where(code > 0, slot, -1)).astype(
                jnp.bfloat16
            )

    for k in range(RING):
        start = pl.multiple_of(((z_ref[0] - k) & 7) * 128, 128)
        held_ref[pl.ds(start, ROWS), :] = ins[k][...]
    for q in range(RING // 2):
        hot = jnp.concatenate([hot_ref[2 * q], hot_ref[2 * q + 1]], axis=1)
        picked = jnp.dot(
            hot, held_ref[256 * q : 256 * q + 256, :], preferred_element_type=jnp.float32
        )
        out_ref[:, 8 * q : 8 * q + 8, :] = picked.reshape(COLUMNS, 8, BLOCK).astype(jnp.bfloat16)


def ring_spread(z, parts):
    width = parts[0].shape[1]
    return pl.pallas_call(
        ring_spread_kernel,
        out_shape=jax.ShapeDtypeStruct((COLUMNS, CAP * RING, width), jnp.bfloat16),
        grid=(width // BLOCK,),
        in_specs=[pl.BlockSpec(memory_space=pltpu.SMEM)]
        + [pl.BlockSpec((ROWS, BLOCK), lambda j: (0, j))] * RING,
        out_specs=pl.BlockSpec((COLUMNS, CAP * RING, BLOCK), lambda j: (0, 0, j)),
        scratch_shapes=[
            pltpu.VMEM((RING, 256, 128), jnp.bfloat16),
            pltpu.VMEM((128 * RING, BLOCK), jnp.bfloat16),
        ],
        compiler_params=VMEM,
        cost_estimate=cost(1024 * 256 * width, (1024 + ROWS * RING) * width),
    )(z, *parts)


def place_kernel(target_ref, scale_ref, rows_ref, out_ref, hot_ref, held_ref):
    @pl.when(pl.program_id(0) == 0)
    def _():
        hot_ref[...] = (rows_of(hot_ref.shape) == target_ref[...]).astype(jnp.bfloat16)
        held_ref[...] = jnp.broadcast_to(scale_ref[...], held_ref.shape)

    scale = jnp.concatenate([held_ref[...]] * (BLOCK // 128), axis=1)
    scaled = (scale * rows_ref[...].astype(jnp.float32)).astype(jnp.bfloat16)
    out_ref[...] = jnp.dot(
        hot_ref[...], scaled, preferred_element_type=jnp.float32
    ).astype(jnp.bfloat16)


def placed_rows(target, scale, rows, shard_rows, out_width):
    slots, width = rows.shape
    return pl.pallas_call(
        place_kernel,
        out_shape=jax.ShapeDtypeStruct((shard_rows, out_width), jnp.bfloat16),
        grid=(width // BLOCK,),
        in_specs=[
            whole((1, slots)),
            whole((slots, 1)),
            pl.BlockSpec((slots, BLOCK), lambda j: (0, j)),
        ],
        out_specs=pl.BlockSpec((shard_rows, BLOCK), lambda j: (0, j)),
        scratch_shapes=[
            pltpu.VMEM((shard_rows, slots), jnp.bfloat16),
            pltpu.VMEM((slots, 128), jnp.float32),
        ],
        compiler_params=VMEM,
        cost_estimate=cost(shard_rows * slots * width, (shard_rows + slots) * width),
    )(target, scale, rows)


def rounded(x):
    return x.astype(jnp.bfloat16).astype(jnp.float32)


def ring_place_kernel(z_ref, target_ref, scale_ref, *refs):
    ins, (_, out_ref, hot_ref, held_ref, scaled_ref) = refs[:RING], refs[RING:]

    @pl.when(pl.program_id(0) == 0)
    def _():
        scaled_ref[...] = jnp.zeros_like(scaled_ref)
        row = rows_of((8, 128))
        for k in range(RING):
            code = ins[k][ROWS - 8 : ROWS, 0:128].astype(jnp.float32)[7:8, :].astype(jnp.int32)
            plane = (z_ref[0] - k) & 7
            listed = (rows_of((128, 128)) == code - 1).astype(jnp.bfloat16)
            target = target_ref[pl.ds(plane, 1), :] + 1
            scale = scale_ref[pl.ds(plane, 1), :]
            high = rounded(scale)
            middle = rounded(scale - high)
            low = scale - high - middle
            parts = [(target >> 4).astype(jnp.float32), (target & 15).astype(jnp.float32)]
            parts += [high, middle, low]
            table = jnp.zeros((8, 128), jnp.float32)
            for r, part in enumerate(parts):
                table = jnp.where(row == r, part, table)
            found = jnp.dot(
                table.astype(jnp.bfloat16), listed, preferred_element_type=jnp.float32
            )
            place = (found[0:1, :] * 16 + found[1:2, :]).astype(jnp.int32) - 1
            hot_ref[:, 128 * k : 128 * k + 128] = (
                rows_of((out_ref.shape[0], 128)) == place
            ).astype(jnp.bfloat16)
            weight = found[2:3, :] + found[3:4, :] + found[4:5, :]
            held_ref[128 * k : 128 * k + 128, :] = jnp.broadcast_to(weight, (128, 128)).T

    for k in range(RING):
        scale = held_ref[128 * k : 128 * k + ROWS, :]
        for c in range(0, BLOCK, 128):
            rows = ins[k][:, c : c + 128].astype(jnp.float32)
            scaled_ref[128 * k : 128 * k + ROWS, c : c + 128] = (scale * rows).astype(jnp.bfloat16)
    out_ref[...] = jnp.dot(
        hot_ref[...], scaled_ref[...], preferred_element_type=jnp.float32
    ).astype(jnp.bfloat16)


def ring_placed(z, target, scale, parts, half_done):
    shard_rows, out_width = half_done.shape
    width = parts[0].shape[1]
    skip = (out_width - width) // BLOCK
    return pl.pallas_call(
        ring_place_kernel,
        out_shape=jax.ShapeDtypeStruct(half_done.shape, jnp.bfloat16),
        grid=(width // BLOCK,),
        in_specs=[pl.BlockSpec(memory_space=pltpu.SMEM)]
        + [whole((RING, 128))] * 2
        + [pl.BlockSpec((ROWS, BLOCK), lambda j: (0, j))] * RING
        + [pl.BlockSpec(memory_space=pl.ANY)],
        out_specs=pl.BlockSpec((shard_rows, BLOCK), lambda j: (0, skip + j)),
        scratch_shapes=[
            pltpu.VMEM((shard_rows, 128 * RING), jnp.bfloat16),
            pltpu.VMEM((128 * RING, 128), jnp.float32),
            pltpu.VMEM((128 * RING, BLOCK), jnp.bfloat16),
        ],
        input_output_aliases={3 + RING: 0},
        compiler_params=VMEM,
        cost_estimate=cost(shard_rows * 1024 * width, (shard_rows + 704) * width),
    )(z, target, scale, *parts, half_done)


def ring_shifted(parts):
    moved = [parts[0]]
    for k in range(1, RING):
        moved.append(lax.ppermute(parts[k], "dev_0", [(i, (i + k) % RING) for i in range(RING)]))
    return moved


def in_plane(parts):
    return lax.all_to_all(parts, PLANE, split_axis=0, concat_axis=0, tiled=True)


def by_device(table):
    rest = table.shape[1:]
    return table.reshape(4, 8, RING, *rest).swapaxes(1, 2).reshape(-1, *rest)


def by_column(table):
    rest = table.shape[1:]
    return table.reshape(4, RING, 8, *rest).swapaxes(1, 2).reshape(-1, *rest)


def count_earlier(key, counts):
    pos = jnp.arange(key.shape[0], dtype=jnp.int32)
    earlier = (pos[None, :] < pos[:, None]) & (key[None, :] == key[:, None]) & counts[None, :]
    return jnp.sum(earlier.astype(jnp.int32), axis=1)


def local(
    token_ids,
    sensitivity,
    last_hidden,
    lengths,
    norm_gain,
    reward_head,
    chosen_index,
    rejected_index,
    shard_owner,
):
    resp_local, block_len = token_ids.shape
    width = sensitivity.shape[2]
    half = width // 2
    tok_local = resp_local * block_len
    devices = shard_owner.shape[0]
    slots = devices * CAP
    shard_rows = VOCAB // devices
    responses = devices * resp_local
    cols = width // devices
    own_place = lax.axis_index(GRP_DEV)
    z = lax.axis_index("dev_0")[None]
    rows = sensitivity.reshape(tok_local, width)

    ids = token_ids.reshape(tok_local)
    shard_of = ids // shard_rows
    offset = ids - shard_of * shard_rows
    shard_hot = shard_of[:, None] == jnp.arange(devices, dtype=jnp.int32)[None, :]
    owner = jnp.sum(jnp.where(shard_hot, shard_owner[None, :], 0), axis=1)
    token_pos = jnp.arange(tok_local, dtype=jnp.int32)
    live = (jnp.arange(block_len, dtype=jnp.int32)[None, :] < lengths[:, None]).reshape(tok_local)
    rank = count_earlier(shard_of, jnp.ones_like(live))
    plane = (owner >> 3) & 7
    column = ((owner >> 6) << 3) + (owner & 7)
    place = count_earlier(plane, live)
    fits = live & (place < ROWS - 1)
    over_here = jnp.any(live & ~fits).astype(jnp.float32)
    ring = jnp.where(fits, (plane - z) & 7, -1)

    second_slot = jnp.where(live, (column << 5) + (plane << 2) + rank, -1)
    first, second = both_packed(
        ring[None, :],
        place[None, :],
        (column * CAP + rank + 1).astype(jnp.float32)[None, :],
        second_slot[None, :],
        rows,
        slots,
        half,
    )
    first = ring_shifted(first)
    second = in_plane(second.reshape(COLUMNS, CAP * RING, half))
    first[1], first[2], second = lax.optimization_barrier((first[1], first[2], second))
    second, over_there = ring_repacked(z, second)
    second = ring_shifted(second)

    code = jnp.where(live, (offset + 1) * resp_local + token_pos // block_len, 0)
    note_slot = owner * CAP + rank
    hidden = last_hidden.astype(jnp.float32)
    norm = jnp.sqrt(jnp.mean(hidden * hidden, axis=-1, keepdims=True) + 1e-05)
    own_reward = jnp.sum(hidden / norm * norm_gain * reward_head, axis=-1)
    slot_match = note_slot[None, :] == jnp.arange(slots, dtype=jnp.int32)[:, None]
    codes = jnp.sum(jnp.where(slot_match, code[None, :], 0), axis=1).reshape(devices, CAP)
    hidden_cols = hidden.reshape(resp_local, devices, cols).swapaxes(0, 1)
    own_facts = jnp.concatenate([own_reward, norm[:, 0], over_here[None]])
    ready = jnp.concatenate(
        [
            codes.astype(jnp.float32),
            jnp.broadcast_to(own_facts[None, :], (devices, 9)),
            jnp.zeros((devices, 51), jnp.float32),
            hidden_cols.reshape(devices, resp_local * cols),
        ],
        axis=1,
    )
    lane = jnp.arange(128, dtype=jnp.int32)
    message = jnp.where(lane[None, :] == 13, over_there[0, 0], ready)
    heard = lax.all_to_all(message, GRP_DEV, split_axis=0, concat_axis=0, tiled=True)
    heard = by_column(heard)

    first = ring_spread(z, first)
    first, second[1], second[7] = lax.optimization_barrier((first, second[1], second[7]))
    first = in_plane(first)

    arrived_code = heard[:, :CAP].astype(jnp.int32)
    reward = by_device(heard[:, 4:8]).reshape(responses)
    any_over = jnp.max(heard[:, 12:14]) > 0
    margin = reward[chosen_index] - reward[rejected_index]
    push = -jax.nn.sigmoid(-margin)
    every = jnp.arange(responses, dtype=jnp.int32)
    sign_table = (chosen_index[None, :] == every[:, None]).astype(jnp.float32) - (
        rejected_index[None, :] == every[:, None]
    ).astype(jnp.float32)
    reward_grad = jnp.sum(sign_table * push[None, :], axis=1).reshape(devices, resp_local)
    reward_grad = by_column(reward_grad)
    own_gain = lax.dynamic_slice(norm_gain, (own_place * cols,), (cols,))
    head_grad = jnp.zeros((cols,), jnp.float32)
    for r in range(resp_local):
        normed = heard[:, 64 + r * cols : 64 + (r + 1) * cols] / heard[:, 8 + r : 9 + r] * own_gain
        head_grad += jnp.sum(reward_grad[:, r : r + 1] * normed, axis=0)

    response_in = arrived_code % resp_local
    scale = jnp.zeros(arrived_code.shape, jnp.float32)
    for r in range(resp_local):
        scale = jnp.where(response_in == r, reward_grad[:, r : r + 1], scale)
    target = arrived_code // resp_local - 1
    scale = jnp.where(target >= 0, scale, 0.0)
    half_done = placed_rows(
        target.reshape(1, slots),
        scale.reshape(slots, 1),
        first.reshape(slots, half),
        shard_rows,
        width,
    )

    def by_plane(table):
        return table.reshape(COLUMNS, RING, CAP).swapaxes(0, 1).reshape(RING, -1)

    def by_ring():
        return ring_placed(z, by_plane(target), by_plane(scale), second, half_done)

    def direct():
        sent = packed_rows(
            jnp.where(live, owner * CAP + rank, -1)[None, :], rows, slots, 0, width
        ).reshape(devices, CAP, width)
        arrived = lax.all_to_all(sent, GRP_DEV, split_axis=0, concat_axis=0, tiled=True)
        return placed_rows(
            by_device(target).reshape(1, slots),
            by_device(scale).reshape(slots, 1),
            arrived.reshape(slots, width),
            shard_rows,
            width,
        )

    return (lax.cond(any_over, direct, by_ring), head_grad)


def solution(mesh):
    torus = Mesh(
        mesh.devices.reshape(mesh.shape["grp"], 8, 4, 2), ("grp", "dev_0", "dev_1", "dev_2")
    )
    placed_as = (
        P(GRP_DEV, None),
        P(GRP_DEV, None, None),
        P(GRP_DEV, None),
        P(GRP_DEV),
        P(),
        P(),
        P(),
        P(),
        P(),
    )
    return jax.shard_map(
        local,
        mesh=torus,
        in_specs=placed_as,
        out_specs=(P(GRP_DEV, None), P(GRP_DEV)),
        check_vma=False,
    )
```

```python
import functools

import jax
import jax.numpy as jnp
from jax import lax
from jax.experimental import pallas as pl
from jax.experimental.pallas import tpu as pltpu
from jax.sharding import Mesh
from jax.sharding import PartitionSpec as P

VOCAB = 128256
CAP = 4
GRP_DEV = ("grp", "dev_0", "dev_1", "dev_2")
PLANE = ("grp", "dev_1", "dev_2")
RING = 8
COLUMNS = 32
ROWS = 88
BLOCK = 256
FIRST = 2304
VMEM = pltpu.CompilerParams(vmem_limit_bytes=48 << 20)
NT = (((1,), (1,)), ((), ()))


def cost(contractions, elements):
    return pl.CostEstimate(flops=2 * contractions, bytes_accessed=2 * elements, transcendentals=0)


def rows_of(shape):
    return lax.broadcasted_iota(jnp.int32, shape, 0)


def whole(shape):
    return pl.BlockSpec(shape, lambda j: (0,) * len(shape))


def pack_kernel(slot_ref, rows_ref, out_ref, hot_ref):
    @pl.when(pl.program_id(0) == 0)
    def _():
        hot_ref[...] = (rows_of(hot_ref.shape) == slot_ref[...]).astype(jnp.bfloat16)

    out_ref[...] = jnp.dot(
        hot_ref[...], rows_ref[...], preferred_element_type=jnp.float32
    ).astype(jnp.bfloat16)


def packed_rows(slot, rows, slots, first, width):
    tokens = rows.shape[0]
    skip = first // BLOCK
    return pl.pallas_call(
        pack_kernel,
        out_shape=jax.ShapeDtypeStruct((slots, width), jnp.bfloat16),
        grid=(width // BLOCK,),
        in_specs=[
            whole((1, tokens)),
            pl.BlockSpec((tokens, BLOCK), lambda j: (0, skip + j)),
        ],
        out_specs=pl.BlockSpec((slots, BLOCK), lambda j: (0, j)),
        scratch_shapes=[pltpu.VMEM((slots, tokens), jnp.bfloat16)],
        compiler_params=VMEM,
        cost_estimate=cost(slots * tokens * width, (slots + tokens) * width),
    )(slot, rows)


def compact_tables(ring, place, code, hot_ref, note_ref):
    count = ring.shape[1]
    row = jnp.where(ring >= 0, ring * ROWS + place, -1)
    hot_ref[...] = (rows_of((RING * ROWS, count)) == row).astype(jnp.bfloat16)
    codes = jnp.broadcast_to(code, (8, count)).astype(jnp.bfloat16)
    for k in range(RING):
        mine = rows_of((128, count)) == jnp.where(ring == k, place, -1)
        note_ref[8 * k : 8 * k + 8, :] = lax.dot_general(
            codes, mine.astype(jnp.bfloat16), NT, preferred_element_type=jnp.float32
        )


def write_compact(rows, hot_ref, note_ref, out_refs):
    picked = jnp.dot(hot_ref[...], rows, preferred_element_type=jnp.float32)
    for k in range(RING):
        out_refs[k][...] = picked[k * ROWS : (k + 1) * ROWS].astype(jnp.bfloat16)

    @pl.when(pl.program_id(0) == 0)
    def _():
        for k in range(RING):
            tail = picked[(k + 1) * ROWS - 8 : (k + 1) * ROWS, :128]
            note = jnp.where(rows_of((8, 128)) == 7, note_ref[8 * k : 8 * k + 8, :], 0.0)
            out_refs[k][ROWS - 8 : ROWS, 0:128] = (tail + note).astype(jnp.bfloat16)


def ring_pack_kernel(ring_ref, place_ref, code_ref, rows_ref, *refs):
    outs, (hot_ref, note_ref) = refs[:RING], refs[RING:]

    @pl.when(pl.program_id(0) == 0)
    def _():
        compact_tables(ring_ref[...], place_ref[...], code_ref[...], hot_ref, note_ref)

    write_compact(rows_ref[...], hot_ref, note_ref, outs)


def ring_packed(ring, place, code, rows, width):
    tokens = rows.shape[0]
    return pl.pallas_call(
        ring_pack_kernel,
        out_shape=[jax.ShapeDtypeStruct((ROWS, width), jnp.bfloat16)] * RING,
        grid=(width // BLOCK,),
        in_specs=[whole((1, tokens))] * 3 + [pl.BlockSpec((tokens, BLOCK), lambda j: (0, j))],
        out_specs=[pl.BlockSpec((ROWS, BLOCK), lambda j: (0, j))] * RING,
        scratch_shapes=[
            pltpu.VMEM((RING * ROWS, tokens), jnp.bfloat16),
            pltpu.VMEM((8 * RING, 128), jnp.float32),
        ],
        compiler_params=VMEM,
        cost_estimate=cost(RING * ROWS * tokens * width, (RING * ROWS + tokens) * width),
    )(ring, place, code, rows)


def ring_repack_kernel(z_ref, rows_ref, *refs):
    outs = refs[:RING]
    hot_ref, note_ref, place_ref, held_ref, sent_ref = refs[RING:]
    width = rows_ref.shape[2]
    step = pl.program_id(0)

    @pl.when(step == 0)
    def _():
        lane = lax.broadcasted_iota(jnp.int32, (8, 256), 1)
        before = rows_of((256, 256))
        slot = lax.broadcasted_iota(jnp.int32, (256, 256), 1)
        ahead = ((before < slot) & (((before ^ slot) & 4) == 0)).astype(jnp.bfloat16)
        for q in range(RING // 2):
            total = jnp.zeros((COLUMNS, 8, 128), jnp.float32)
            for c in range(0, width, 128):
                total += jnp.abs(
                    rows_ref[:, 8 * q : 8 * q + 8, c : c + 128].astype(jnp.float32)
                )
            filled = (total.reshape(256, 128) > 0).astype(jnp.bfloat16)
            seen = lax.dot_general(
                jnp.ones((8, 128), jnp.bfloat16), filled, NT, preferred_element_type=jnp.float32
            )
            used = seen > 0
            place = jnp.dot(
                used.astype(jnp.bfloat16), ahead, preferred_element_type=jnp.float32
            )
            place_ref[8 * q : 8 * q + 8, :] = jnp.where(
                used & (place < ROWS - 1), place, -1.0
            ).astype(jnp.int32)
        codes = (((lane >> 3) << 2) + (lane & 3) + 1).astype(jnp.float32).astype(jnp.bfloat16)
        for k in range(RING):
            plane = (z_ref[0] + k) & 7
            start = pl.multiple_of((plane >> 1) * 8, 8)
            mine = ((lane >> 2) & 1) == (plane & 1)
            place = jnp.where(mine, place_ref[pl.ds(start, 8), :], -1)[0:1, :]
            hot_ref[plane] = (rows_of((ROWS, 256)) == place).astype(jnp.bfloat16)
            note_ref[8 * k : 8 * k + 8, :] = lax.dot_general(
                codes,
                (rows_of((128, 256)) == place).astype(jnp.bfloat16),
                NT,
                preferred_element_type=jnp.float32,
            )

    first = pl.multiple_of(step * BLOCK, BLOCK)
    for q in range(RING // 2):
        rows = rows_ref[:, 8 * q : 8 * q + 8, pl.ds(first, BLOCK)].astype(jnp.float32)
        held_ref[256 * q : 256 * q + 256, :] = rows.reshape(256, BLOCK).astype(jnp.bfloat16)
    for q in range(RING // 2):
        hot = jnp.concatenate([hot_ref[2 * q], hot_ref[2 * q + 1]], axis=0)
        picked = jnp.dot(
            hot, held_ref[256 * q : 256 * q + 256, :], preferred_element_type=jnp.float32
        )
        for half in (0, 1):
            k = (2 * q + half - z_ref[0]) & 7
            sent_ref[k] = picked[half * ROWS : (half + 1) * ROWS].astype(jnp.bfloat16)
    for k in range(RING):
        outs[k][...] = sent_ref[k]

    @pl.when(step == 0)
    def _():
        for k in range(RING):
            tail = sent_ref[k, ROWS - 8 : ROWS, 0:128].astype(jnp.float32)
            note = jnp.where(rows_of((8, 128)) == 7, note_ref[8 * k : 8 * k + 8, :], 0.0)
            outs[k][ROWS - 8 : ROWS, 0:128] = (tail + note).astype(jnp.bfloat16)


def ring_repacked(z, rows):
    width = rows.shape[2]
    return pl.pallas_call(
        ring_repack_kernel,
        out_shape=[jax.ShapeDtypeStruct((ROWS, width), jnp.bfloat16)] * RING,
        grid=(width // BLOCK,),
        in_specs=[pl.BlockSpec(memory_space=pltpu.SMEM), whole(rows.shape)],
        out_specs=[pl.BlockSpec((ROWS, BLOCK), lambda j: (0, j))] * RING,
        scratch_shapes=[
            pltpu.VMEM((RING, ROWS, 256), jnp.bfloat16),
            pltpu.VMEM((8 * RING, 128), jnp.float32),
            pltpu.VMEM((4 * RING, 256), jnp.int32),
            pltpu.VMEM((128 * RING, BLOCK), jnp.bfloat16),
            pltpu.VMEM((RING, ROWS, BLOCK), jnp.bfloat16),
        ],
        compiler_params=VMEM,
        cost_estimate=cost(RING * ROWS * 256 * width, (RING * ROWS + 1024) * width),
    )(z, rows)


def ring_spread_kernel(z_ref, *refs):
    ins, (out_ref, hot_ref, held_ref) = refs[:RING], refs[RING:]

    @pl.when(pl.program_id(0) == 0)
    def _():
        held_ref[...] = jnp.zeros_like(held_ref)
        for k in range(RING):
            code = ins[k][ROWS - 8 : ROWS, 0:128].astype(jnp.float32)[7:8, :].astype(jnp.int32)
            where = code - 1
            plane = (z_ref[0] - k) & 7
            slot = ((where >> 2) << 3) + ((plane & 1) << 2) + (where & 3)
            hot_ref[plane] = (rows_of((256, 128)) == jnp.where(code > 0, slot, -1)).astype(
                jnp.bfloat16
            )

    for k in range(RING):
        start = pl.multiple_of(((z_ref[0] - k) & 7) * 128, 128)
        held_ref[pl.ds(start, ROWS), :] = ins[k][...]
    for q in range(RING // 2):
        hot = jnp.concatenate([hot_ref[2 * q], hot_ref[2 * q + 1]], axis=1)
        picked = jnp.dot(
            hot, held_ref[256 * q : 256 * q + 256, :], preferred_element_type=jnp.float32
        )
        out_ref[:, 8 * q : 8 * q + 8, :] = picked.reshape(COLUMNS, 8, BLOCK).astype(jnp.bfloat16)


def ring_spread(z, parts):
    width = parts[0].shape[1]
    return pl.pallas_call(
        ring_spread_kernel,
        out_shape=jax.ShapeDtypeStruct((COLUMNS, CAP * RING, width), jnp.bfloat16),
        grid=(width // BLOCK,),
        in_specs=[pl.BlockSpec(memory_space=pltpu.SMEM)]
        + [pl.BlockSpec((ROWS, BLOCK), lambda j: (0, j))] * RING,
        out_specs=pl.BlockSpec((COLUMNS, CAP * RING, BLOCK), lambda j: (0, 0, j)),
        scratch_shapes=[
            pltpu.VMEM((RING, 256, 128), jnp.bfloat16),
            pltpu.VMEM((128 * RING, BLOCK), jnp.bfloat16),
        ],
        compiler_params=VMEM,
        cost_estimate=cost(1024 * 256 * width, (1024 + ROWS * RING) * width),
    )(z, *parts)


def place_kernel(target_ref, scale_ref, rows_ref, out_ref, hot_ref, held_ref):
    @pl.when(pl.program_id(0) == 0)
    def _():
        hot_ref[...] = (rows_of(hot_ref.shape) == target_ref[...]).astype(jnp.bfloat16)
        held_ref[...] = jnp.broadcast_to(scale_ref[...], held_ref.shape)

    scale = jnp.concatenate([held_ref[...]] * (BLOCK // 128), axis=1)
    scaled = (scale * rows_ref[...].astype(jnp.float32)).astype(jnp.bfloat16)
    out_ref[...] = jnp.dot(
        hot_ref[...], scaled, preferred_element_type=jnp.float32
    ).astype(jnp.bfloat16)


def placed_rows(target, scale, rows, shard_rows, out_width):
    slots, width = rows.shape
    return pl.pallas_call(
        place_kernel,
        out_shape=jax.ShapeDtypeStruct((shard_rows, out_width), jnp.bfloat16),
        grid=(width // BLOCK,),
        in_specs=[
            whole((1, slots)),
            whole((slots, 1)),
            pl.BlockSpec((slots, BLOCK), lambda j: (0, j)),
        ],
        out_specs=pl.BlockSpec((shard_rows, BLOCK), lambda j: (0, j)),
        scratch_shapes=[
            pltpu.VMEM((shard_rows, slots), jnp.bfloat16),
            pltpu.VMEM((slots, 128), jnp.float32),
        ],
        compiler_params=VMEM,
        cost_estimate=cost(shard_rows * slots * width, (shard_rows + slots) * width),
    )(target, scale, rows)


def rounded(x):
    return x.astype(jnp.bfloat16).astype(jnp.float32)


def ring_place_kernel(z_ref, target_ref, scale_ref, *refs):
    ins, (_, out_ref, hot_ref, held_ref, scaled_ref) = refs[:RING], refs[RING:]

    @pl.when(pl.program_id(0) == 0)
    def _():
        scaled_ref[...] = jnp.zeros_like(scaled_ref)
        row = rows_of((8, 128))
        for k in range(RING):
            code = ins[k][ROWS - 8 : ROWS, 0:128].astype(jnp.float32)[7:8, :].astype(jnp.int32)
            plane = (z_ref[0] - k) & 7
            listed = (rows_of((128, 128)) == code - 1).astype(jnp.bfloat16)
            target = target_ref[pl.ds(plane, 1), :] + 1
            scale = scale_ref[pl.ds(plane, 1), :]
            high = rounded(scale)
            middle = rounded(scale - high)
            low = scale - high - middle
            parts = [(target >> 4).astype(jnp.float32), (target & 15).astype(jnp.float32)]
            parts += [high, middle, low]
            table = jnp.zeros((8, 128), jnp.float32)
            for r, part in enumerate(parts):
                table = jnp.where(row == r, part, table)
            found = jnp.dot(
                table.astype(jnp.bfloat16), listed, preferred_element_type=jnp.float32
            )
            place = (found[0:1, :] * 16 + found[1:2, :]).astype(jnp.int32) - 1
            hot_ref[:, 128 * k : 128 * k + 128] = (
                rows_of((out_ref.shape[0], 128)) == place
            ).astype(jnp.bfloat16)
            weight = found[2:3, :] + found[3:4, :] + found[4:5, :]
            held_ref[128 * k : 128 * k + 128, :] = jnp.broadcast_to(weight, (128, 128)).T

    for k in range(RING):
        scale = held_ref[128 * k : 128 * k + ROWS, :]
        for c in range(0, BLOCK, 128):
            rows = ins[k][:, c : c + 128].astype(jnp.float32)
            scaled_ref[128 * k : 128 * k + ROWS, c : c + 128] = (scale * rows).astype(jnp.bfloat16)
    out_ref[...] = jnp.dot(
        hot_ref[...], scaled_ref[...], preferred_element_type=jnp.float32
    ).astype(jnp.bfloat16)


def ring_placed(z, target, scale, parts, half_done):
    shard_rows, out_width = half_done.shape
    width = parts[0].shape[1]
    skip = (out_width - width) // BLOCK
    return pl.pallas_call(
        ring_place_kernel,
        out_shape=jax.ShapeDtypeStruct(half_done.shape, jnp.bfloat16),
        grid=(width // BLOCK,),
        in_specs=[pl.BlockSpec(memory_space=pltpu.SMEM)]
        + [whole((RING, 128))] * 2
        + [pl.BlockSpec((ROWS, BLOCK), lambda j: (0, j))] * RING
        + [pl.BlockSpec(memory_space=pl.ANY)],
        out_specs=pl.BlockSpec((shard_rows, BLOCK), lambda j: (0, skip + j)),
        scratch_shapes=[
            pltpu.VMEM((shard_rows, 128 * RING), jnp.bfloat16),
            pltpu.VMEM((128 * RING, 128), jnp.float32),
            pltpu.VMEM((128 * RING, BLOCK), jnp.bfloat16),
        ],
        input_output_aliases={3 + RING: 0},
        compiler_params=VMEM,
        cost_estimate=cost(shard_rows * 1024 * width, (shard_rows + 704) * width),
    )(z, target, scale, *parts, half_done)


def ring_shifted(parts):
    moved = [parts[0]]
    for k in range(1, RING):
        moved.append(lax.ppermute(parts[k], "dev_0", [(i, (i + k) % RING) for i in range(RING)]))
    return moved


def in_plane(parts):
    return lax.all_to_all(parts, PLANE, split_axis=0, concat_axis=0, tiled=True)


def by_device(table):
    rest = table.shape[1:]
    return table.reshape(4, 8, RING, *rest).swapaxes(1, 2).reshape(-1, *rest)


def by_column(table):
    rest = table.shape[1:]
    return table.reshape(4, RING, 8, *rest).swapaxes(1, 2).reshape(-1, *rest)


def count_earlier(key, counts):
    pos = jnp.arange(key.shape[0], dtype=jnp.int32)
    earlier = (pos[None, :] < pos[:, None]) & (key[None, :] == key[:, None]) & counts[None, :]
    return jnp.sum(earlier.astype(jnp.int32), axis=1)


def local(
    token_ids,
    sensitivity,
    last_hidden,
    lengths,
    norm_gain,
    reward_head,
    chosen_index,
    rejected_index,
    shard_owner,
):
    resp_local, block_len = token_ids.shape
    width = sensitivity.shape[2]
    second_width = width - FIRST
    tok_local = resp_local * block_len
    devices = shard_owner.shape[0]
    slots = devices * CAP
    shard_rows = VOCAB // devices
    responses = devices * resp_local
    cols = width // devices
    own_place = lax.axis_index(GRP_DEV)
    z = lax.axis_index("dev_0")[None]
    rows = sensitivity.reshape(tok_local, width)

    ids = token_ids.reshape(tok_local)
    shard_of = ids // shard_rows
    offset = ids - shard_of * shard_rows
    shard_hot = shard_of[:, None] == jnp.arange(devices, dtype=jnp.int32)[None, :]
    owner = jnp.sum(jnp.where(shard_hot, shard_owner[None, :], 0), axis=1)
    token_pos = jnp.arange(tok_local, dtype=jnp.int32)
    live = (jnp.arange(block_len, dtype=jnp.int32)[None, :] < lengths[:, None]).reshape(tok_local)
    rank = count_earlier(shard_of, jnp.ones_like(live))
    plane = (owner >> 3) & 7
    column = ((owner >> 6) << 3) + (owner & 7)
    place = count_earlier(plane, live)
    fits = live & (place < ROWS - 1)
    over_here = jnp.any(live & ~fits).astype(jnp.float32)
    ring = jnp.where(fits, (plane - z) & 7, -1)

    first = ring_packed(
        ring[None, :],
        place[None, :],
        (column * CAP + rank + 1).astype(jnp.float32)[None, :],
        rows,
        FIRST,
    )
    first, code, hidden = lax.optimization_barrier(
        (
            first,
            jnp.where(live, (offset + 1) * resp_local + token_pos // block_len, 0),
            last_hidden,
        )
    )
    first = ring_shifted(first)

    hidden = hidden.astype(jnp.float32)
    norm = jnp.sqrt(jnp.mean(hidden * hidden, axis=-1, keepdims=True) + 1e-05)
    own_reward = jnp.sum(hidden / norm * norm_gain * reward_head, axis=-1)
    slot_match = (owner * CAP + rank)[None, :] == jnp.arange(slots, dtype=jnp.int32)[:, None]
    codes = jnp.sum(jnp.where(slot_match, code[None, :], 0), axis=1).reshape(devices, CAP)
    owner_match = (owner[:, None] == jnp.arange(devices, dtype=jnp.int32)[None, :]) & live[:, None]
    counts = jnp.sum(owner_match.astype(jnp.float32), axis=0)
    own_facts = jnp.concatenate(
        [own_reward, norm[:, 0], over_here[None], jnp.zeros((51,), jnp.float32)]
    )
    message = jnp.concatenate(
        [
            codes.astype(jnp.float32),
            jnp.broadcast_to(own_facts[None, :], (devices, 60)),
            hidden.reshape(resp_local, devices, cols).swapaxes(0, 1).reshape(devices, -1),
            jnp.broadcast_to((counts[:128] * 8 + counts[128:])[None, :], (devices, 128)),
        ],
        axis=1,
    )
    message, first[1], first[7] = lax.optimization_barrier((message, first[1], first[7]))
    heard = lax.all_to_all(message, GRP_DEV, split_axis=0, concat_axis=0, tiled=True)

    second_slot = jnp.where(live, (column << 5) + (plane << 2) + rank, -1)
    second_slot, message, first[2], first[6] = lax.optimization_barrier(
        (second_slot, message, first[2], first[6])
    )
    second = packed_rows(second_slot[None, :], rows, slots, FIRST, second_width)
    second, heard = lax.optimization_barrier((second, heard))
    second = in_plane(second.reshape(COLUMNS, CAP * RING, second_width))
    heard = by_column(heard)

    arrived_code = heard[:, :CAP].astype(jnp.int32)
    reward = by_device(heard[:, 4:8]).reshape(responses)
    coded = heard[:, 128:]
    upper = jnp.floor(coded * 0.125)
    plane_counts = jnp.stack([upper, coded - 8 * upper]).reshape(2, COLUMNS, RING, 128).sum(axis=1)
    any_over = (jnp.max(heard[:, 12]) > 0) | (jnp.max(plane_counts) > ROWS - 1)
    margin = reward[chosen_index] - reward[rejected_index]
    push = -jax.nn.sigmoid(-margin)
    every = jnp.arange(responses, dtype=jnp.int32)
    sign_table = (chosen_index[None, :] == every[:, None]).astype(jnp.float32) - (
        rejected_index[None, :] == every[:, None]
    ).astype(jnp.float32)
    reward_grad = jnp.sum(sign_table * push[None, :], axis=1).reshape(devices, resp_local)
    reward_grad = by_column(reward_grad)
    own_gain = lax.dynamic_slice(norm_gain, (own_place * cols,), (cols,))
    head_grad = jnp.zeros((cols,), jnp.float32)
    for r in range(resp_local):
        normed = heard[:, 64 + r * cols : 64 + (r + 1) * cols] / heard[:, 8 + r : 9 + r] * own_gain
        head_grad += jnp.sum(reward_grad[:, r : r + 1] * normed, axis=0)

    response_in = arrived_code % resp_local
    scale = jnp.zeros(arrived_code.shape, jnp.float32)
    for r in range(resp_local):
        scale = jnp.where(response_in == r, reward_grad[:, r : r + 1], scale)
    target = arrived_code // resp_local - 1
    scale = jnp.where(target >= 0, scale, 0.0)
    target, scale, head_grad, first = lax.optimization_barrier((target, scale, head_grad, first))
    first = ring_spread(z, first)
    first, second = lax.optimization_barrier((first, second))
    first = in_plane(first)
    second = ring_shifted(ring_repacked(z, second))

    half_done = placed_rows(
        target.reshape(1, slots),
        scale.reshape(slots, 1),
        first.reshape(slots, FIRST),
        shard_rows,
        width,
    )

    def by_plane(table):
        return table.reshape(COLUMNS, RING, CAP).swapaxes(0, 1).reshape(RING, -1)

    def by_ring():
        return ring_placed(z, by_plane(target), by_plane(scale), second, half_done)

    def direct():
        sent = packed_rows(
            jnp.where(live, owner * CAP + rank, -1)[None, :], rows, slots, 0, width
        ).reshape(devices, CAP, width)
        arrived = lax.all_to_all(sent, GRP_DEV, split_axis=0, concat_axis=0, tiled=True)
        return placed_rows(
            by_device(target).reshape(1, slots),
            by_device(scale).reshape(slots, 1),
            arrived.reshape(slots, width),
            shard_rows,
            width,
        )

    return (lax.cond(any_over, direct, by_ring), head_grad)


def solution(mesh):
    torus = Mesh(
        mesh.devices.reshape(mesh.shape["grp"], 8, 4, 2), ("grp", "dev_0", "dev_1", "dev_2")
    )
    placed_as = (
        P(GRP_DEV, None),
        P(GRP_DEV, None, None),
        P(GRP_DEV, None),
        P(GRP_DEV),
        P(),
        P(),
        P(),
        P(),
        P(),
    )
    return jax.shard_map(
        local,
        mesh=torus,
        in_specs=placed_as,
        out_specs=(P(GRP_DEV, None), P(GRP_DEV)),
        check_vma=False,
    )
```

```python
import functools

import jax
import jax.numpy as jnp
from jax import lax
from jax.experimental import pallas as pl
from jax.experimental.pallas import tpu as pltpu
from jax.sharding import Mesh
from jax.sharding import PartitionSpec as P

VOCAB = 128256
CAP = 4
GRP_DEV = ("grp", "dev_0", "dev_1", "dev_2")
PLANE = ("grp", "dev_1", "dev_2")
RING = 8
COLUMNS = 32
ROWS = 88
BLOCK = 512
VMEM = pltpu.CompilerParams(vmem_limit_bytes=62 << 20)
NT = (((1,), (1,)), ((), ()))


def cost(contractions, elements):
    return pl.CostEstimate(flops=2 * contractions, bytes_accessed=2 * elements, transcendentals=0)


def rows_of(shape):
    return lax.broadcasted_iota(jnp.int32, shape, 0)


def whole(shape):
    return pl.BlockSpec(shape, lambda j: (0,) * len(shape))


def pack_kernel(slot_ref, rows_ref, out_ref, hot_ref):
    @pl.when(pl.program_id(0) == 0)
    def _():
        hot_ref[...] = (rows_of(hot_ref.shape) == slot_ref[...]).astype(jnp.bfloat16)

    out_ref[...] = jnp.dot(
        hot_ref[...], rows_ref[...], preferred_element_type=jnp.float32
    ).astype(jnp.bfloat16)


def packed_rows(slot, rows, slots, first, width):
    tokens = rows.shape[0]
    skip = first // BLOCK
    return pl.pallas_call(
        pack_kernel,
        out_shape=jax.ShapeDtypeStruct((slots, width), jnp.bfloat16),
        grid=(width // BLOCK,),
        in_specs=[
            whole((1, tokens)),
            pl.BlockSpec((tokens, BLOCK), lambda j: (0, skip + j)),
        ],
        out_specs=pl.BlockSpec((slots, BLOCK), lambda j: (0, j)),
        scratch_shapes=[pltpu.VMEM((slots, tokens), jnp.bfloat16)],
        compiler_params=VMEM,
        cost_estimate=cost(slots * tokens * width, (slots + tokens) * width),
    )(slot, rows)


def compact_tables(ring, place, code, hot_ref, note_ref):
    count = ring.shape[1]
    row = jnp.where(ring >= 0, ring * ROWS + place, -1)
    hot_ref[...] = (rows_of((RING * ROWS, count)) == row).astype(jnp.bfloat16)
    codes = jnp.broadcast_to(code, (8, count)).astype(jnp.bfloat16)
    for k in range(RING):
        mine = rows_of((128, count)) == jnp.where(ring == k, place, -1)
        note_ref[8 * k : 8 * k + 8, :] = lax.dot_general(
            codes, mine.astype(jnp.bfloat16), NT, preferred_element_type=jnp.float32
        )


def write_compact(rows, hot_ref, note_ref, out_refs):
    picked = jnp.dot(hot_ref[...], rows, preferred_element_type=jnp.float32)
    for k in range(RING):
        out_refs[k][...] = picked[k * ROWS : (k + 1) * ROWS].astype(jnp.bfloat16)

    @pl.when(pl.program_id(0) == 0)
    def _():
        for k in range(RING):
            tail = picked[(k + 1) * ROWS - 8 : (k + 1) * ROWS, :128]
            note = jnp.where(rows_of((8, 128)) == 7, note_ref[8 * k : 8 * k + 8, :], 0.0)
            out_refs[k][ROWS - 8 : ROWS, 0:128] = (tail + note).astype(jnp.bfloat16)


def ring_pack_kernel(ring_ref, place_ref, code_ref, rows_ref, *refs):
    outs, (hot_ref, note_ref) = refs[:RING], refs[RING:]

    @pl.when(pl.program_id(0) == 0)
    def _():
        compact_tables(ring_ref[...], place_ref[...], code_ref[...], hot_ref, note_ref)

    write_compact(rows_ref[...], hot_ref, note_ref, outs)


def ring_packed(ring, place, code, rows, width):
    tokens = rows.shape[0]
    return pl.pallas_call(
        ring_pack_kernel,
        out_shape=[jax.ShapeDtypeStruct((ROWS, width), jnp.bfloat16)] * RING,
        grid=(width // BLOCK,),
        in_specs=[whole((1, tokens))] * 3 + [pl.BlockSpec((tokens, BLOCK), lambda j: (0, j))],
        out_specs=[pl.BlockSpec((ROWS, BLOCK), lambda j: (0, j))] * RING,
        scratch_shapes=[
            pltpu.VMEM((RING * ROWS, tokens), jnp.bfloat16),
            pltpu.VMEM((8 * RING, 128), jnp.float32),
        ],
        compiler_params=VMEM,
        cost_estimate=cost(RING * ROWS * tokens * width, (RING * ROWS + tokens) * width),
    )(ring, place, code, rows)


def ring_repack_kernel(z_ref, rows_ref, *refs):
    outs, flag_ref = refs[:RING], refs[RING]
    hot_ref, note_ref, place_ref, held_ref, sent_ref = refs[RING + 1 :]
    width = rows_ref.shape[2]
    step = pl.program_id(0)

    @pl.when(step == 0)
    def _():
        lane = lax.broadcasted_iota(jnp.int32, (8, 256), 1)
        before = rows_of((256, 256))
        slot = lax.broadcasted_iota(jnp.int32, (256, 256), 1)
        ahead = ((before < slot) & (((before ^ slot) & 4) == 0)).astype(jnp.bfloat16)
        over = jnp.zeros((8, 256), jnp.float32)
        for q in range(RING // 2):
            total = jnp.zeros((COLUMNS, 8, 128), jnp.float32)
            for c in range(0, width, 128):
                total += jnp.abs(
                    rows_ref[:, 8 * q : 8 * q + 8, c : c + 128].astype(jnp.float32)
                )
            filled = (total.reshape(256, 128) > 0).astype(jnp.bfloat16)
            seen = lax.dot_general(
                jnp.ones((8, 128), jnp.bfloat16), filled, NT, preferred_element_type=jnp.float32
            )
            used = seen > 0
            place = jnp.dot(
                used.astype(jnp.bfloat16), ahead, preferred_element_type=jnp.float32
            )
            over = jnp.maximum(over, jnp.where(used & (place >= ROWS - 1), 1.0, 0.0))
            place_ref[8 * q : 8 * q + 8, :] = jnp.where(
                used & (place < ROWS - 1), place, -1.0
            ).astype(jnp.int32)
        flag_ref[...] = jnp.broadcast_to(jnp.max(over, axis=1, keepdims=True), (8, 128))
        codes = (((lane >> 3) << 2) + (lane & 3) + 1).astype(jnp.float32).astype(jnp.bfloat16)
        for k in range(RING):
            plane = (z_ref[0] + k) & 7
            start = pl.multiple_of((plane >> 1) * 8, 8)
            mine = ((lane >> 2) & 1) == (plane & 1)
            place = jnp.where(mine, place_ref[pl.ds(start, 8), :], -1)[0:1, :]
            hot_ref[plane] = (rows_of((ROWS, 256)) == place).astype(jnp.bfloat16)
            note_ref[8 * k : 8 * k + 8, :] = lax.dot_general(
                codes,
                (rows_of((128, 256)) == place).astype(jnp.bfloat16),
                NT,
                preferred_element_type=jnp.float32,
            )

    first = pl.multiple_of(step * BLOCK, BLOCK)
    for q in range(RING // 2):
        rows = rows_ref[:, 8 * q : 8 * q + 8, pl.ds(first, BLOCK)].astype(jnp.float32)
        held_ref[256 * q : 256 * q + 256, :] = rows.reshape(256, BLOCK).astype(jnp.bfloat16)
    for q in range(RING // 2):
        hot = jnp.concatenate([hot_ref[2 * q], hot_ref[2 * q + 1]], axis=0)
        picked = jnp.dot(
            hot, held_ref[256 * q : 256 * q + 256, :], preferred_element_type=jnp.float32
        )
        for half in (0, 1):
            k = (2 * q + half - z_ref[0]) & 7
            sent_ref[k] = picked[half * ROWS : (half + 1) * ROWS].astype(jnp.bfloat16)
    for k in range(RING):
        outs[k][...] = sent_ref[k]

    @pl.when(step == 0)
    def _():
        for k in range(RING):
            tail = sent_ref[k, ROWS - 8 : ROWS, 0:128].astype(jnp.float32)
            note = jnp.where(rows_of((8, 128)) == 7, note_ref[8 * k : 8 * k + 8, :], 0.0)
            outs[k][ROWS - 8 : ROWS, 0:128] = (tail + note).astype(jnp.bfloat16)


def ring_repacked(z, rows):
    width = rows.shape[2]
    out = pl.pallas_call(
        ring_repack_kernel,
        out_shape=[jax.ShapeDtypeStruct((ROWS, width), jnp.bfloat16)] * RING
        + [jax.ShapeDtypeStruct((8, 128), jnp.float32)],
        grid=(width // BLOCK,),
        in_specs=[pl.BlockSpec(memory_space=pltpu.SMEM), whole(rows.shape)],
        out_specs=[pl.BlockSpec((ROWS, BLOCK), lambda j: (0, j))] * RING + [whole((8, 128))],
        scratch_shapes=[
            pltpu.VMEM((RING, ROWS, 256), jnp.bfloat16),
            pltpu.VMEM((8 * RING, 128), jnp.float32),
            pltpu.VMEM((4 * RING, 256), jnp.int32),
            pltpu.VMEM((128 * RING, BLOCK), jnp.bfloat16),
            pltpu.VMEM((RING, ROWS, BLOCK), jnp.bfloat16),
        ],
        compiler_params=VMEM,
        cost_estimate=cost(RING * ROWS * 1024 * width, (RING * ROWS + 1024) * width),
    )(z, rows)
    return out[:RING], out[RING]


def ring_spread_kernel(z_ref, *refs):
    ins, (out_ref, hot_ref, held_ref) = refs[:RING], refs[RING:]

    @pl.when(pl.program_id(0) == 0)
    def _():
        held_ref[...] = jnp.zeros_like(held_ref)
        for k in range(RING):
            code = ins[k][ROWS - 8 : ROWS, 0:128].astype(jnp.float32)[7:8, :].astype(jnp.int32)
            where = code - 1
            plane = (z_ref[0] - k) & 7
            slot = ((where >> 2) << 3) + ((plane & 1) << 2) + (where & 3)
            hot_ref[plane] = (rows_of((256, 128)) == jnp.where(code > 0, slot, -1)).astype(
                jnp.bfloat16
            )

    for k in range(RING):
        start = pl.multiple_of(((z_ref[0] - k) & 7) * 128, 128)
        held_ref[pl.ds(start, ROWS), :] = ins[k][...]
    for q in range(RING // 2):
        hot = jnp.concatenate([hot_ref[2 * q], hot_ref[2 * q + 1]], axis=1)
        picked = jnp.dot(
            hot, held_ref[256 * q : 256 * q + 256, :], preferred_element_type=jnp.float32
        )
        out_ref[:, 8 * q : 8 * q + 8, :] = picked.reshape(COLUMNS, 8, BLOCK).astype(jnp.bfloat16)


def ring_spread(z, parts):
    width = parts[0].shape[1]
    return pl.pallas_call(
        ring_spread_kernel,
        out_shape=jax.ShapeDtypeStruct((COLUMNS, CAP * RING, width), jnp.bfloat16),
        grid=(width // BLOCK,),
        in_specs=[pl.BlockSpec(memory_space=pltpu.SMEM)]
        + [pl.BlockSpec((ROWS, BLOCK), lambda j: (0, j))] * RING,
        out_specs=pl.BlockSpec((COLUMNS, CAP * RING, BLOCK), lambda j: (0, 0, j)),
        scratch_shapes=[
            pltpu.VMEM((RING, 256, 128), jnp.bfloat16),
            pltpu.VMEM((128 * RING, BLOCK), jnp.bfloat16),
        ],
        compiler_params=VMEM,
        cost_estimate=cost(1024 * 1024 * width, (1024 + ROWS * RING) * width),
    )(z, *parts)


def place_kernel(target_ref, scale_ref, rows_ref, out_ref, hot_ref, held_ref):
    @pl.when(pl.program_id(0) == 0)
    def _():
        hot_ref[...] = (rows_of(hot_ref.shape) == target_ref[...]).astype(jnp.bfloat16)
        held_ref[...] = jnp.broadcast_to(scale_ref[...], held_ref.shape)

    scale = jnp.concatenate([held_ref[...]] * (BLOCK // 128), axis=1)
    scaled = (scale * rows_ref[...].astype(jnp.float32)).astype(jnp.bfloat16)
    out_ref[...] = jnp.dot(
        hot_ref[...], scaled, preferred_element_type=jnp.float32
    ).astype(jnp.bfloat16)


def placed_rows(target, scale, rows, shard_rows, out_width):
    slots, width = rows.shape
    return pl.pallas_call(
        place_kernel,
        out_shape=jax.ShapeDtypeStruct((shard_rows, out_width), jnp.bfloat16),
        grid=(width // BLOCK,),
        in_specs=[
            whole((1, slots)),
            whole((slots, 1)),
            pl.BlockSpec((slots, BLOCK), lambda j: (0, j)),
        ],
        out_specs=pl.BlockSpec((shard_rows, BLOCK), lambda j: (0, j)),
        scratch_shapes=[
            pltpu.VMEM((shard_rows, slots), jnp.bfloat16),
            pltpu.VMEM((slots, 128), jnp.float32),
        ],
        compiler_params=VMEM,
        cost_estimate=cost(shard_rows * slots * width, (shard_rows + slots) * width),
    )(target, scale, rows)


def rounded(x):
    return x.astype(jnp.bfloat16).astype(jnp.float32)


def ring_place_kernel(z_ref, target_ref, scale_ref, *refs):
    ins, (_, out_ref, hot_ref, held_ref, scaled_ref) = refs[:RING], refs[RING:]

    @pl.when(pl.program_id(0) == 0)
    def _():
        scaled_ref[...] = jnp.zeros_like(scaled_ref)
        row = rows_of((8, 128))
        for k in range(RING):
            code = ins[k][ROWS - 8 : ROWS, 0:128].astype(jnp.float32)[7:8, :].astype(jnp.int32)
            plane = (z_ref[0] - k) & 7
            listed = (rows_of((128, 128)) == code - 1).astype(jnp.bfloat16)
            target = target_ref[pl.ds(plane, 1), :] + 1
            scale = scale_ref[pl.ds(plane, 1), :]
            high = rounded(scale)
            middle = rounded(scale - high)
            low = scale - high - middle
            parts = [(target >> 4).astype(jnp.float32), (target & 15).astype(jnp.float32)]
            parts += [high, middle, low]
            table = jnp.zeros((8, 128), jnp.float32)
            for r, part in enumerate(parts):
                table = jnp.where(row == r, part, table)
            found = jnp.dot(
                table.astype(jnp.bfloat16), listed, preferred_element_type=jnp.float32
            )
            place = (found[0:1, :] * 16 + found[1:2, :]).astype(jnp.int32) - 1
            hot_ref[:, 128 * k : 128 * k + 128] = (
                rows_of((out_ref.shape[0], 128)) == place
            ).astype(jnp.bfloat16)
            weight = found[2:3, :] + found[3:4, :] + found[4:5, :]
            held_ref[128 * k : 128 * k + 128, :] = jnp.broadcast_to(weight, (128, 128)).T

    for k in range(RING):
        scale = held_ref[128 * k : 128 * k + ROWS, :]
        for c in range(0, BLOCK, 128):
            rows = ins[k][:, c : c + 128].astype(jnp.float32)
            scaled_ref[128 * k : 128 * k + ROWS, c : c + 128] = (scale * rows).astype(jnp.bfloat16)
    out_ref[...] = jnp.dot(
        hot_ref[...], scaled_ref[...], preferred_element_type=jnp.float32
    ).astype(jnp.bfloat16)


def ring_placed(z, target, scale, parts, half_done):
    shard_rows, out_width = half_done.shape
    width = parts[0].shape[1]
    skip = (out_width - width) // BLOCK
    return pl.pallas_call(
        ring_place_kernel,
        out_shape=jax.ShapeDtypeStruct(half_done.shape, jnp.bfloat16),
        grid=(width // BLOCK,),
        in_specs=[pl.BlockSpec(memory_space=pltpu.SMEM)]
        + [whole((RING, 128))] * 2
        + [pl.BlockSpec((ROWS, BLOCK), lambda j: (0, j))] * RING
        + [pl.BlockSpec(memory_space=pl.ANY)],
        out_specs=pl.BlockSpec((shard_rows, BLOCK), lambda j: (0, skip + j)),
        scratch_shapes=[
            pltpu.VMEM((shard_rows, 128 * RING), jnp.bfloat16),
            pltpu.VMEM((128 * RING, 128), jnp.float32),
            pltpu.VMEM((128 * RING, BLOCK), jnp.bfloat16),
        ],
        input_output_aliases={3 + RING: 0},
        compiler_params=VMEM,
        cost_estimate=cost(shard_rows * 1024 * width, (shard_rows + 704) * width),
    )(z, target, scale, *parts, half_done)


def ring_shifted(parts):
    moved = [parts[0]]
    for k in range(1, RING):
        moved.append(lax.ppermute(parts[k], "dev_0", [(i, (i + k) % RING) for i in range(RING)]))
    return moved


def in_plane(parts):
    return lax.all_to_all(parts, PLANE, split_axis=0, concat_axis=0, tiled=True)


def by_device(table):
    rest = table.shape[1:]
    return table.reshape(4, 8, RING, *rest).swapaxes(1, 2).reshape(-1, *rest)


def by_column(table):
    rest = table.shape[1:]
    return table.reshape(4, RING, 8, *rest).swapaxes(1, 2).reshape(-1, *rest)


def count_earlier(key, counts):
    pos = jnp.arange(key.shape[0], dtype=jnp.int32)
    earlier = (pos[None, :] < pos[:, None]) & (key[None, :] == key[:, None]) & counts[None, :]
    return jnp.sum(earlier.astype(jnp.int32), axis=1)


def local(
    token_ids,
    sensitivity,
    last_hidden,
    lengths,
    norm_gain,
    reward_head,
    chosen_index,
    rejected_index,
    shard_owner,
):
    resp_local, block_len = token_ids.shape
    width = sensitivity.shape[2]
    half = width // 2
    tok_local = resp_local * block_len
    devices = shard_owner.shape[0]
    slots = devices * CAP
    shard_rows = VOCAB // devices
    responses = devices * resp_local
    cols = width // devices
    own_place = lax.axis_index(GRP_DEV)
    z = lax.axis_index("dev_0")[None]
    rows = sensitivity.reshape(tok_local, width)

    ids = token_ids.reshape(tok_local)
    shard_of = ids // shard_rows
    offset = ids - shard_of * shard_rows
    shard_hot = shard_of[:, None] == jnp.arange(devices, dtype=jnp.int32)[None, :]
    owner = jnp.sum(jnp.where(shard_hot, shard_owner[None, :], 0), axis=1)
    token_pos = jnp.arange(tok_local, dtype=jnp.int32)
    live = (jnp.arange(block_len, dtype=jnp.int32)[None, :] < lengths[:, None]).reshape(tok_local)
    rank = count_earlier(shard_of, jnp.ones_like(live))
    plane = (owner >> 3) & 7
    column = ((owner >> 6) << 3) + (owner & 7)
    place = count_earlier(plane, live)
    fits = live & (place < ROWS - 1)
    over_here = jnp.any(live & ~fits).astype(jnp.float32)
    ring = jnp.where(fits, (plane - z) & 7, -1)

    first = ring_packed(
        ring[None, :],
        place[None, :],
        (column * CAP + rank + 1).astype(jnp.float32)[None, :],
        rows,
        half,
    )
    first = ring_shifted(first)
    second_slot = jnp.where(live, (column << 5) + (plane << 2) + rank, -1)
    second = packed_rows(second_slot[None, :], rows, slots, half, half)
    second = in_plane(second.reshape(COLUMNS, CAP * RING, half))
    first[1], first[2], second = lax.optimization_barrier((first[1], first[2], second))
    second, over_there = ring_repacked(z, second)
    second = ring_shifted(second)

    code = jnp.where(live, (offset + 1) * resp_local + token_pos // block_len, 0)
    note_slot = owner * CAP + rank
    hidden = last_hidden.astype(jnp.float32)
    norm = jnp.sqrt(jnp.mean(hidden * hidden, axis=-1, keepdims=True) + 1e-05)
    own_reward = jnp.sum(hidden / norm * norm_gain * reward_head, axis=-1)
    slot_match = note_slot[None, :] == jnp.arange(slots, dtype=jnp.int32)[:, None]
    codes = jnp.sum(jnp.where(slot_match, code[None, :], 0), axis=1).reshape(devices, CAP)
    hidden_cols = hidden.reshape(resp_local, devices, cols).swapaxes(0, 1)
    own_facts = jnp.concatenate([own_reward, norm[:, 0], over_here[None]])
    ready = jnp.concatenate(
        [
            codes.astype(jnp.float32),
            jnp.broadcast_to(own_facts[None, :], (devices, 9)),
            jnp.zeros((devices, 51), jnp.float32),
            hidden_cols.reshape(devices, resp_local * cols),
        ],
        axis=1,
    )
    lane = jnp.arange(128, dtype=jnp.int32)
    message = jnp.where(lane[None, :] == 13, over_there[0, 0], ready)
    heard = lax.all_to_all(message, GRP_DEV, split_axis=0, concat_axis=0, tiled=True)
    heard = by_column(heard)

    first = ring_spread(z, first)
    first, second[1], second[7] = lax.optimization_barrier((first, second[1], second[7]))
    first = in_plane(first)

    arrived_code = heard[:, :CAP].astype(jnp.int32)
    reward = by_device(heard[:, 4:8]).reshape(responses)
    any_over = jnp.max(heard[:, 12:14]) > 0
    margin = reward[chosen_index] - reward[rejected_index]
    push = -jax.nn.sigmoid(-margin)
    every = jnp.arange(responses, dtype=jnp.int32)
    sign_table = (chosen_index[None, :] == every[:, None]).astype(jnp.float32) - (
        rejected_index[None, :] == every[:, None]
    ).astype(jnp.float32)
    reward_grad = jnp.sum(sign_table * push[None, :], axis=1).reshape(devices, resp_local)
    reward_grad = by_column(reward_grad)
    own_gain = lax.dynamic_slice(norm_gain, (own_place * cols,), (cols,))
    head_grad = jnp.zeros((cols,), jnp.float32)
    for r in range(resp_local):
        normed = heard[:, 64 + r * cols : 64 + (r + 1) * cols] / heard[:, 8 + r : 9 + r] * own_gain
        head_grad += jnp.sum(reward_grad[:, r : r + 1] * normed, axis=0)

    response_in = arrived_code % resp_local
    scale = jnp.zeros(arrived_code.shape, jnp.float32)
    for r in range(resp_local):
        scale = jnp.where(response_in == r, reward_grad[:, r : r + 1], scale)
    target = arrived_code // resp_local - 1
    scale = jnp.where(target >= 0, scale, 0.0)
    half_done = placed_rows(
        target.reshape(1, slots),
        scale.reshape(slots, 1),
        first.reshape(slots, half),
        shard_rows,
        width,
    )

    def by_plane(table):
        return table.reshape(COLUMNS, RING, CAP).swapaxes(0, 1).reshape(RING, -1)

    def by_ring():
        return ring_placed(z, by_plane(target), by_plane(scale), second, half_done)

    def direct():
        sent = packed_rows(
            jnp.where(live, owner * CAP + rank, -1)[None, :], rows, slots, 0, width
        ).reshape(devices, CAP, width)
        arrived = lax.all_to_all(sent, GRP_DEV, split_axis=0, concat_axis=0, tiled=True)
        return placed_rows(
            by_device(target).reshape(1, slots),
            by_device(scale).reshape(slots, 1),
            arrived.reshape(slots, width),
            shard_rows,
            width,
        )

    return (lax.cond(any_over, direct, by_ring), head_grad)


def solution(mesh):
    torus = Mesh(
        mesh.devices.reshape(mesh.shape["grp"], 8, 4, 2), ("grp", "dev_0", "dev_1", "dev_2")
    )
    placed_as = (
        P(GRP_DEV, None),
        P(GRP_DEV, None, None),
        P(GRP_DEV, None),
        P(GRP_DEV),
        P(),
        P(),
        P(),
        P(),
        P(),
    )
    return jax.shard_map(
        local,
        mesh=torus,
        in_specs=placed_as,
        out_specs=(P(GRP_DEV, None), P(GRP_DEV)),
        check_vma=False,
    )
```

```python
import functools

import jax
import jax.numpy as jnp
from jax import lax
from jax.experimental import pallas as pl
from jax.experimental.pallas import tpu as pltpu
from jax.sharding import Mesh
from jax.sharding import PartitionSpec as P

VOCAB = 128256
CAP = 4
GRP_DEV = ("grp", "dev_0", "dev_1", "dev_2")
PLANE = ("grp", "dev_1", "dev_2")
RING = 8
COLUMNS = 32
ROWS = 88
BLOCK = 512
VMEM = pltpu.CompilerParams(vmem_limit_bytes=48 << 20)
NT = (((1,), (1,)), ((), ()))


def cost(contractions, elements):
    return pl.CostEstimate(flops=2 * contractions, bytes_accessed=2 * elements, transcendentals=0)


def rows_of(shape):
    return lax.broadcasted_iota(jnp.int32, shape, 0)


def whole(shape):
    return pl.BlockSpec(shape, lambda j: (0,) * len(shape))


def pack_kernel(slot_ref, rows_ref, out_ref, hot_ref):
    @pl.when(pl.program_id(0) == 0)
    def _():
        hot_ref[...] = (rows_of(hot_ref.shape) == slot_ref[...]).astype(jnp.bfloat16)

    out_ref[...] = jnp.dot(
        hot_ref[...], rows_ref[...], preferred_element_type=jnp.float32
    ).astype(jnp.bfloat16)


def packed_rows(slot, rows, slots, first, width):
    tokens = rows.shape[0]
    skip = first // BLOCK
    return pl.pallas_call(
        pack_kernel,
        out_shape=jax.ShapeDtypeStruct((slots, width), jnp.bfloat16),
        grid=(width // BLOCK,),
        in_specs=[
            whole((1, tokens)),
            pl.BlockSpec((tokens, BLOCK), lambda j: (0, skip + j)),
        ],
        out_specs=pl.BlockSpec((slots, BLOCK), lambda j: (0, j)),
        scratch_shapes=[pltpu.VMEM((slots, tokens), jnp.bfloat16)],
        compiler_params=VMEM,
        cost_estimate=cost(slots * tokens * width, (slots + tokens) * width),
    )(slot, rows)


def compact_tables(ring, place, code, hot_ref, note_ref):
    count = ring.shape[1]
    row = jnp.where(ring >= 0, ring * ROWS + place, -1)
    hot_ref[...] = (rows_of((RING * ROWS, count)) == row).astype(jnp.bfloat16)
    codes = jnp.broadcast_to(code, (8, count)).astype(jnp.bfloat16)
    for k in range(RING):
        mine = rows_of((128, count)) == jnp.where(ring == k, place, -1)
        note_ref[8 * k : 8 * k + 8, :] = lax.dot_general(
            codes, mine.astype(jnp.bfloat16), NT, preferred_element_type=jnp.float32
        )


def write_compact(rows, hot_ref, note_ref, out_refs):
    picked = jnp.dot(hot_ref[...], rows, preferred_element_type=jnp.float32)
    for k in range(RING):
        out_refs[k][...] = picked[k * ROWS : (k + 1) * ROWS].astype(jnp.bfloat16)

    @pl.when(pl.program_id(0) == 0)
    def _():
        for k in range(RING):
            tail = picked[(k + 1) * ROWS - 8 : (k + 1) * ROWS, :128]
            note = jnp.where(rows_of((8, 128)) == 7, note_ref[8 * k : 8 * k + 8, :], 0.0)
            out_refs[k][ROWS - 8 : ROWS, 0:128] = (tail + note).astype(jnp.bfloat16)


def ring_pack_kernel(ring_ref, place_ref, code_ref, rows_ref, *refs):
    outs, (hot_ref, note_ref) = refs[:RING], refs[RING:]

    @pl.when(pl.program_id(0) == 0)
    def _():
        compact_tables(ring_ref[...], place_ref[...], code_ref[...], hot_ref, note_ref)

    write_compact(rows_ref[...], hot_ref, note_ref, outs)


def ring_packed(ring, place, code, rows, width):
    tokens = rows.shape[0]
    return pl.pallas_call(
        ring_pack_kernel,
        out_shape=[jax.ShapeDtypeStruct((ROWS, width), jnp.bfloat16)] * RING,
        grid=(width // BLOCK,),
        in_specs=[whole((1, tokens))] * 3 + [pl.BlockSpec((tokens, BLOCK), lambda j: (0, j))],
        out_specs=[pl.BlockSpec((ROWS, BLOCK), lambda j: (0, j))] * RING,
        scratch_shapes=[
            pltpu.VMEM((RING * ROWS, tokens), jnp.bfloat16),
            pltpu.VMEM((8 * RING, 128), jnp.float32),
        ],
        compiler_params=VMEM,
        cost_estimate=cost(RING * ROWS * tokens * width, (RING * ROWS + tokens) * width),
    )(ring, place, code, rows)


def ring_repack_kernel(z_ref, rows_ref, *refs):
    outs, flag_ref = refs[:RING], refs[RING]
    hot_ref, note_ref, place_ref, held_ref, sent_ref = refs[RING + 1 :]
    width = rows_ref.shape[2]
    step = pl.program_id(0)

    @pl.when(step == 0)
    def _():
        lane = lax.broadcasted_iota(jnp.int32, (8, 256), 1)
        before = rows_of((256, 256))
        slot = lax.broadcasted_iota(jnp.int32, (256, 256), 1)
        ahead = ((before < slot) & (((before ^ slot) & 4) == 0)).astype(jnp.bfloat16)
        over = jnp.zeros((8, 256), jnp.float32)
        for q in range(RING // 2):
            total = jnp.zeros((COLUMNS, 8, 128), jnp.float32)
            for c in range(0, width, 128):
                total += jnp.abs(
                    rows_ref[:, 8 * q : 8 * q + 8, c : c + 128].astype(jnp.float32)
                )
            filled = (total.reshape(256, 128) > 0).astype(jnp.bfloat16)
            seen = lax.dot_general(
                jnp.ones((8, 128), jnp.bfloat16), filled, NT, preferred_element_type=jnp.float32
            )
            used = seen > 0
            place = jnp.dot(
                used.astype(jnp.bfloat16), ahead, preferred_element_type=jnp.float32
            )
            over = jnp.maximum(over, jnp.where(used & (place >= ROWS - 1), 1.0, 0.0))
            place_ref[8 * q : 8 * q + 8, :] = jnp.where(
                used & (place < ROWS - 1), place, -1.0
            ).astype(jnp.int32)
        flag_ref[...] = jnp.broadcast_to(jnp.max(over, axis=1, keepdims=True), (8, 128))
        codes = (((lane >> 3) << 2) + (lane & 3) + 1).astype(jnp.float32).astype(jnp.bfloat16)
        for k in range(RING):
            plane = (z_ref[0] + k) & 7
            start = pl.multiple_of((plane >> 1) * 8, 8)
            mine = ((lane >> 2) & 1) == (plane & 1)
            place = jnp.where(mine, place_ref[pl.ds(start, 8), :], -1)[0:1, :]
            hot_ref[plane] = (rows_of((ROWS, 256)) == place).astype(jnp.bfloat16)
            note_ref[8 * k : 8 * k + 8, :] = lax.dot_general(
                codes,
                (rows_of((128, 256)) == place).astype(jnp.bfloat16),
                NT,
                preferred_element_type=jnp.float32,
            )

    first = pl.multiple_of(step * BLOCK, BLOCK)
    for q in range(RING // 2):
        rows = rows_ref[:, 8 * q : 8 * q + 8, pl.ds(first, BLOCK)].astype(jnp.float32)
        held_ref[256 * q : 256 * q + 256, :] = rows.reshape(256, BLOCK).astype(jnp.bfloat16)
    for q in range(RING // 2):
        hot = jnp.concatenate([hot_ref[2 * q], hot_ref[2 * q + 1]], axis=0)
        picked = jnp.dot(
            hot, held_ref[256 * q : 256 * q + 256, :], preferred_element_type=jnp.float32
        )
        for half in (0, 1):
            k = (2 * q + half - z_ref[0]) & 7
            sent_ref[k] = picked[half * ROWS : (half + 1) * ROWS].astype(jnp.bfloat16)
    for k in range(RING):
        outs[k][...] = sent_ref[k]

    @pl.when(step == 0)
    def _():
        for k in range(RING):
            tail = sent_ref[k, ROWS - 8 : ROWS, 0:128].astype(jnp.float32)
            note = jnp.where(rows_of((8, 128)) == 7, note_ref[8 * k : 8 * k + 8, :], 0.0)
            outs[k][ROWS - 8 : ROWS, 0:128] = (tail + note).astype(jnp.bfloat16)


def ring_repacked(z, rows):
    width = rows.shape[2]
    out = pl.pallas_call(
        ring_repack_kernel,
        out_shape=[jax.ShapeDtypeStruct((ROWS, width), jnp.bfloat16)] * RING
        + [jax.ShapeDtypeStruct((8, 128), jnp.float32)],
        grid=(width // BLOCK,),
        in_specs=[pl.BlockSpec(memory_space=pltpu.SMEM), whole(rows.shape)],
        out_specs=[pl.BlockSpec((ROWS, BLOCK), lambda j: (0, j))] * RING + [whole((8, 128))],
        scratch_shapes=[
            pltpu.VMEM((RING, ROWS, 256), jnp.bfloat16),
            pltpu.VMEM((8 * RING, 128), jnp.float32),
            pltpu.VMEM((4 * RING, 256), jnp.int32),
            pltpu.VMEM((128 * RING, BLOCK), jnp.bfloat16),
            pltpu.VMEM((RING, ROWS, BLOCK), jnp.bfloat16),
        ],
        compiler_params=VMEM,
        cost_estimate=cost(RING * ROWS * 1024 * width, (RING * ROWS + 1024) * width),
    )(z, rows)
    return out[:RING], out[RING]


def ring_spread_kernel(z_ref, *refs):
    ins, (out_ref, hot_ref, held_ref) = refs[:RING], refs[RING:]

    @pl.when(pl.program_id(0) == 0)
    def _():
        held_ref[...] = jnp.zeros_like(held_ref)
        for k in range(RING):
            code = ins[k][ROWS - 8 : ROWS, 0:128].astype(jnp.float32)[7:8, :].astype(jnp.int32)
            where = code - 1
            plane = (z_ref[0] - k) & 7
            slot = ((where >> 2) << 3) + ((plane & 1) << 2) + (where & 3)
            hot_ref[plane] = (rows_of((256, 128)) == jnp.where(code > 0, slot, -1)).astype(
                jnp.bfloat16
            )

    for k in range(RING):
        start = pl.multiple_of(((z_ref[0] - k) & 7) * 128, 128)
        held_ref[pl.ds(start, ROWS), :] = ins[k][...]
    for q in range(RING // 2):
        hot = jnp.concatenate([hot_ref[2 * q], hot_ref[2 * q + 1]], axis=1)
        picked = jnp.dot(
            hot, held_ref[256 * q : 256 * q + 256, :], preferred_element_type=jnp.float32
        )
        out_ref[:, 8 * q : 8 * q + 8, :] = picked.reshape(COLUMNS, 8, BLOCK).astype(jnp.bfloat16)


def ring_spread(z, parts):
    width = parts[0].shape[1]
    return pl.pallas_call(
        ring_spread_kernel,
        out_shape=jax.ShapeDtypeStruct((COLUMNS, CAP * RING, width), jnp.bfloat16),
        grid=(width // BLOCK,),
        in_specs=[pl.BlockSpec(memory_space=pltpu.SMEM)]
        + [pl.BlockSpec((ROWS, BLOCK), lambda j: (0, j))] * RING,
        out_specs=pl.BlockSpec((COLUMNS, CAP * RING, BLOCK), lambda j: (0, 0, j)),
        scratch_shapes=[
            pltpu.VMEM((RING, 256, 128), jnp.bfloat16),
            pltpu.VMEM((128 * RING, BLOCK), jnp.bfloat16),
        ],
        compiler_params=VMEM,
        cost_estimate=cost(1024 * 1024 * width, (1024 + ROWS * RING) * width),
    )(z, *parts)


def place_kernel(target_ref, scale_ref, rows_ref, out_ref, hot_ref, held_ref):
    @pl.when(pl.program_id(0) == 0)
    def _():
        hot_ref[...] = (rows_of(hot_ref.shape) == target_ref[...]).astype(jnp.bfloat16)
        held_ref[...] = jnp.broadcast_to(scale_ref[...], held_ref.shape)

    scale = jnp.concatenate([held_ref[...]] * (BLOCK // 128), axis=1)
    scaled = (scale * rows_ref[...].astype(jnp.float32)).astype(jnp.bfloat16)
    out_ref[...] = jnp.dot(
        hot_ref[...], scaled, preferred_element_type=jnp.float32
    ).astype(jnp.bfloat16)


def placed_rows(target, scale, rows, shard_rows, out_width):
    slots, width = rows.shape
    return pl.pallas_call(
        place_kernel,
        out_shape=jax.ShapeDtypeStruct((shard_rows, out_width), jnp.bfloat16),
        grid=(width // BLOCK,),
        in_specs=[
            whole((1, slots)),
            whole((slots, 1)),
            pl.BlockSpec((slots, BLOCK), lambda j: (0, j)),
        ],
        out_specs=pl.BlockSpec((shard_rows, BLOCK), lambda j: (0, j)),
        scratch_shapes=[
            pltpu.VMEM((shard_rows, slots), jnp.bfloat16),
            pltpu.VMEM((slots, 128), jnp.float32),
        ],
        compiler_params=VMEM,
        cost_estimate=cost(shard_rows * slots * width, (shard_rows + slots) * width),
    )(target, scale, rows)


def rounded(x):
    return x.astype(jnp.bfloat16).astype(jnp.float32)


def ring_place_kernel(z_ref, table_ref, *refs):
    ins, (_, out_ref, hot_ref, held_ref, scaled_ref) = refs[:RING], refs[RING:]

    @pl.when(pl.program_id(0) == 0)
    def _():
        scaled_ref[...] = jnp.zeros_like(scaled_ref)
        row = rows_of((8, 128))
        for k in range(RING):
            code = ins[k][ROWS - 8 : ROWS, 0:128].astype(jnp.float32)[7:8, :].astype(jnp.int32)
            plane = (z_ref[0] - k) & 7
            listed = (rows_of((128, 128)) == code - 1).astype(jnp.bfloat16)
            target = table_ref[pl.ds(plane, 1), :].astype(jnp.int32) + 1
            scale = table_ref[pl.ds(plane + RING, 1), :]
            high = rounded(scale)
            middle = rounded(scale - high)
            low = scale - high - middle
            parts = [(target >> 4).astype(jnp.float32), (target & 15).astype(jnp.float32)]
            parts += [high, middle, low]
            table = jnp.zeros((8, 128), jnp.float32)
            for r, part in enumerate(parts):
                table = jnp.where(row == r, part, table)
            found = jnp.dot(
                table.astype(jnp.bfloat16), listed, preferred_element_type=jnp.float32
            )
            place = (found[0:1, :] * 16 + found[1:2, :]).astype(jnp.int32) - 1
            hot_ref[:, 128 * k : 128 * k + 128] = (
                rows_of((out_ref.shape[0], 128)) == place
            ).astype(jnp.bfloat16)
            weight = found[2:3, :] + found[3:4, :] + found[4:5, :]
            held_ref[128 * k : 128 * k + 128, :] = jnp.broadcast_to(weight, (128, 128)).T

    for k in range(RING):
        scale = held_ref[128 * k : 128 * k + ROWS, :]
        for c in range(0, BLOCK, 128):
            rows = ins[k][:, c : c + 128].astype(jnp.float32)
            scaled_ref[128 * k : 128 * k + ROWS, c : c + 128] = (scale * rows).astype(jnp.bfloat16)
    out_ref[...] = jnp.dot(
        hot_ref[...], scaled_ref[...], preferred_element_type=jnp.float32
    ).astype(jnp.bfloat16)


def ring_placed(z, tables, parts, half_done):
    shard_rows, out_width = half_done.shape
    width = parts[0].shape[1]
    skip = (out_width - width) // BLOCK
    return pl.pallas_call(
        ring_place_kernel,
        out_shape=jax.ShapeDtypeStruct(half_done.shape, jnp.bfloat16),
        grid=(width // BLOCK,),
        in_specs=[pl.BlockSpec(memory_space=pltpu.SMEM)]
        + [whole((2 * RING, 128))]
        + [pl.BlockSpec((ROWS, BLOCK), lambda j: (0, j))] * RING
        + [pl.BlockSpec(memory_space=pl.ANY)],
        out_specs=pl.BlockSpec((shard_rows, BLOCK), lambda j: (0, skip + j)),
        scratch_shapes=[
            pltpu.VMEM((shard_rows, 128 * RING), jnp.bfloat16),
            pltpu.VMEM((128 * RING, 128), jnp.float32),
            pltpu.VMEM((128 * RING, BLOCK), jnp.bfloat16),
        ],
        input_output_aliases={2 + RING: 0},
        compiler_params=VMEM,
        cost_estimate=cost(shard_rows * 1024 * width, (shard_rows + 704) * width),
    )(z, tables, *parts, half_done)


def ring_shifted(parts):
    moved = [parts[0]]
    for k in range(1, RING):
        moved.append(lax.ppermute(parts[k], "dev_0", [(i, (i + k) % RING) for i in range(RING)]))
    return moved


def in_plane(parts):
    return lax.all_to_all(parts, PLANE, split_axis=0, concat_axis=0, tiled=True)


def by_device(table):
    rest = table.shape[1:]
    return table.reshape(4, 8, RING, *rest).swapaxes(1, 2).reshape(-1, *rest)


def by_column(table):
    rest = table.shape[1:]
    return table.reshape(4, RING, 8, *rest).swapaxes(1, 2).reshape(-1, *rest)


def count_earlier(key, counts):
    pos = jnp.arange(key.shape[0], dtype=jnp.int32)
    earlier = (pos[None, :] < pos[:, None]) & (key[None, :] == key[:, None]) & counts[None, :]
    return jnp.sum(earlier.astype(jnp.int32), axis=1)


def local(
    token_ids,
    sensitivity,
    last_hidden,
    lengths,
    norm_gain,
    reward_head,
    chosen_index,
    rejected_index,
    shard_owner,
):
    resp_local, block_len = token_ids.shape
    width = sensitivity.shape[2]
    half = width // 2
    tok_local = resp_local * block_len
    devices = shard_owner.shape[0]
    slots = devices * CAP
    shard_rows = VOCAB // devices
    responses = devices * resp_local
    cols = width // devices
    own_place = lax.axis_index(GRP_DEV)
    z = lax.axis_index("dev_0")[None]
    rows = sensitivity.reshape(tok_local, width)

    ids = token_ids.reshape(tok_local)
    shard_of = ids // shard_rows
    offset = ids - shard_of * shard_rows
    shard_hot = shard_of[:, None] == jnp.arange(devices, dtype=jnp.int32)[None, :]
    owner = jnp.sum(jnp.where(shard_hot, shard_owner[None, :], 0), axis=1)
    token_pos = jnp.arange(tok_local, dtype=jnp.int32)
    live = (jnp.arange(block_len, dtype=jnp.int32)[None, :] < lengths[:, None]).reshape(tok_local)
    rank = count_earlier(shard_of, jnp.ones_like(live))
    plane = (owner >> 3) & 7
    column = ((owner >> 6) << 3) + (owner & 7)
    place = count_earlier(plane, live)
    fits = live & (place < ROWS - 1)
    over_here = jnp.any(live & ~fits).astype(jnp.float32)
    ring = jnp.where(fits, (plane - z) & 7, -1)

    first = ring_packed(
        ring[None, :],
        place[None, :],
        (column * CAP + rank + 1).astype(jnp.float32)[None, :],
        rows,
        half,
    )
    first = ring_shifted(first)
    second_slot = jnp.where(live, (column << 5) + (plane << 2) + rank, -1)
    second = packed_rows(second_slot[None, :], rows, slots, half, half)
    second = in_plane(second.reshape(COLUMNS, CAP * RING, half))
    first[1], first[7], second = lax.optimization_barrier((first[1], first[7], second))
    second, over_there = ring_repacked(z, second)
    second = ring_shifted(second)

    code = jnp.where(live, (offset + 1) * resp_local + token_pos // block_len, 0)
    note_slot = owner * CAP + rank
    hidden = last_hidden.astype(jnp.float32)
    norm = jnp.sqrt(jnp.mean(hidden * hidden, axis=-1, keepdims=True) + 1e-05)
    own_reward = jnp.sum(hidden / norm * norm_gain * reward_head, axis=-1)
    slot_match = note_slot[None, :] == jnp.arange(slots, dtype=jnp.int32)[:, None]
    codes = jnp.sum(jnp.where(slot_match, code[None, :], 0), axis=1).reshape(devices, CAP)
    hidden_cols = hidden.reshape(resp_local, devices, cols).swapaxes(0, 1)
    own_facts = jnp.concatenate([own_reward, norm[:, 0], over_here[None]])
    ready = jnp.concatenate(
        [
            codes.astype(jnp.float32),
            jnp.broadcast_to(own_facts[None, :], (devices, 9)),
            jnp.zeros((devices, 51), jnp.float32),
            hidden_cols.reshape(devices, resp_local * cols),
        ],
        axis=1,
    )
    lane = jnp.arange(128, dtype=jnp.int32)
    message = jnp.where(lane[None, :] == 13, over_there[0:1, :], ready)
    heard = lax.all_to_all(message, GRP_DEV, split_axis=0, concat_axis=0, tiled=True)
    heard = by_column(heard)

    first = ring_spread(z, first)
    first, second[1], second[7] = lax.optimization_barrier((first, second[1], second[7]))
    first = in_plane(first)

    arrived_code = heard[:, :CAP].astype(jnp.int32)
    reward = by_device(heard[:, 4:8]).reshape(responses)
    any_over = jnp.max(heard[:, 12:14]) > 0
    margin = reward[chosen_index] - reward[rejected_index]
    push = -jax.nn.sigmoid(-margin)
    every = jnp.arange(responses, dtype=jnp.int32)
    sign_table = (chosen_index[None, :] == every[:, None]).astype(jnp.float32) - (
        rejected_index[None, :] == every[:, None]
    ).astype(jnp.float32)
    reward_grad = jnp.sum(sign_table * push[None, :], axis=1).reshape(devices, resp_local)
    reward_grad = by_column(reward_grad)
    own_gain = lax.dynamic_slice(norm_gain, (own_place * cols,), (cols,))
    head_grad = jnp.zeros((cols,), jnp.float32)
    for r in range(resp_local):
        normed = heard[:, 64 + r * cols : 64 + (r + 1) * cols] / heard[:, 8 + r : 9 + r] * own_gain
        head_grad += jnp.sum(reward_grad[:, r : r + 1] * normed, axis=0)

    response_in = arrived_code % resp_local
    scale = jnp.zeros(arrived_code.shape, jnp.float32)
    for r in range(resp_local):
        scale = jnp.where(response_in == r, reward_grad[:, r : r + 1], scale)
    target = arrived_code // resp_local - 1
    scale = jnp.where(target >= 0, scale, 0.0)
    half_done = placed_rows(
        target.reshape(1, slots),
        scale.reshape(slots, 1),
        first.reshape(slots, half),
        shard_rows,
        width,
    )

    def by_plane(table):
        return table.reshape(COLUMNS, RING, CAP).swapaxes(0, 1).reshape(RING, -1)

    tail_table = jnp.concatenate([by_plane(target).astype(jnp.float32), by_plane(scale)])

    def by_ring():
        return ring_placed(z, tail_table, second, half_done)

    def direct():
        sent = packed_rows(
            jnp.where(live, owner * CAP + rank, -1)[None, :], rows, slots, 0, width
        ).reshape(devices, CAP, width)
        arrived = lax.all_to_all(sent, GRP_DEV, split_axis=0, concat_axis=0, tiled=True)
        return placed_rows(
            by_device(target).reshape(1, slots),
            by_device(scale).reshape(slots, 1),
            arrived.reshape(slots, width),
            shard_rows,
            width,
        )

    return (lax.cond(any_over, direct, by_ring), head_grad)


def solution(mesh):
    torus = Mesh(
        mesh.devices.reshape(mesh.shape["grp"], 8, 4, 2), ("grp", "dev_0", "dev_1", "dev_2")
    )
    placed_as = (
        P(GRP_DEV, None),
        P(GRP_DEV, None, None),
        P(GRP_DEV, None),
        P(GRP_DEV),
        P(),
        P(),
        P(),
        P(),
        P(),
    )
    return jax.shard_map(
        local,
        mesh=torus,
        in_specs=placed_as,
        out_specs=(P(GRP_DEV, None), P(GRP_DEV)),
        check_vma=False,
    )
```

```python
import functools

import jax
import jax.numpy as jnp
from jax import lax
from jax.experimental import pallas as pl
from jax.experimental.pallas import tpu as pltpu
from jax.sharding import Mesh
from jax.sharding import PartitionSpec as P

VOCAB = 128256
CAP = 4
GRP_DEV = ("grp", "dev_0", "dev_1", "dev_2")
PLANE = ("grp", "dev_1", "dev_2")
RING = 8
COLUMNS = 32
ROWS = 88
BLOCK = 1024
VMEM = pltpu.CompilerParams(vmem_limit_bytes=48 << 20)
NT = (((1,), (1,)), ((), ()))


def cost(contractions, elements):
    return pl.CostEstimate(flops=2 * contractions, bytes_accessed=2 * elements, transcendentals=0)


def rows_of(shape):
    return lax.broadcasted_iota(jnp.int32, shape, 0)


def whole(shape):
    return pl.BlockSpec(shape, lambda j: (0,) * len(shape))


def pack_kernel(slot_ref, rows_ref, out_ref, hot_ref):
    @pl.when(pl.program_id(0) == 0)
    def _():
        hot_ref[...] = (rows_of(hot_ref.shape) == slot_ref[...]).astype(jnp.bfloat16)

    out_ref[...] = jnp.dot(
        hot_ref[...], rows_ref[...], preferred_element_type=jnp.float32
    ).astype(jnp.bfloat16)


def packed_rows(slot, rows, slots, first, width):
    tokens = rows.shape[0]
    skip = first // BLOCK
    return pl.pallas_call(
        pack_kernel,
        out_shape=jax.ShapeDtypeStruct((slots, width), jnp.bfloat16),
        grid=(width // BLOCK,),
        in_specs=[
            whole((1, tokens)),
            pl.BlockSpec((tokens, BLOCK), lambda j: (0, skip + j)),
        ],
        out_specs=pl.BlockSpec((slots, BLOCK), lambda j: (0, j)),
        scratch_shapes=[pltpu.VMEM((slots, tokens), jnp.bfloat16)],
        compiler_params=VMEM,
        cost_estimate=cost(slots * tokens * width, (slots + tokens) * width),
    )(slot, rows)


def compact_tables(ring, place, code, hot_ref, note_ref):
    count = ring.shape[1]
    row = jnp.where(ring >= 0, ring * ROWS + place, -1)
    hot_ref[...] = (rows_of((RING * ROWS, count)) == row).astype(jnp.bfloat16)
    codes = jnp.broadcast_to(code, (8, count)).astype(jnp.bfloat16)
    for k in range(RING):
        mine = rows_of((128, count)) == jnp.where(ring == k, place, -1)
        note_ref[8 * k : 8 * k + 8, :] = lax.dot_general(
            codes, mine.astype(jnp.bfloat16), NT, preferred_element_type=jnp.float32
        )


def write_compact(rows, hot_ref, note_ref, out_refs):
    picked = jnp.dot(hot_ref[...], rows, preferred_element_type=jnp.float32)
    for k in range(RING):
        out_refs[k][...] = picked[k * ROWS : (k + 1) * ROWS].astype(jnp.bfloat16)

    @pl.when(pl.program_id(0) == 0)
    def _():
        for k in range(RING):
            tail = picked[(k + 1) * ROWS - 8 : (k + 1) * ROWS, :128]
            note = jnp.where(rows_of((8, 128)) == 7, note_ref[8 * k : 8 * k + 8, :], 0.0)
            out_refs[k][ROWS - 8 : ROWS, 0:128] = (tail + note).astype(jnp.bfloat16)


def ring_pack_kernel(ring_ref, place_ref, code_ref, rows_ref, *refs):
    outs, (hot_ref, note_ref) = refs[:RING], refs[RING:]

    @pl.when(pl.program_id(0) == 0)
    def _():
        compact_tables(ring_ref[...], place_ref[...], code_ref[...], hot_ref, note_ref)

    write_compact(rows_ref[...], hot_ref, note_ref, outs)


def ring_packed(ring, place, code, rows, width):
    tokens = rows.shape[0]
    return pl.pallas_call(
        ring_pack_kernel,
        out_shape=[jax.ShapeDtypeStruct((ROWS, width), jnp.bfloat16)] * RING,
        grid=(width // BLOCK,),
        in_specs=[whole((1, tokens))] * 3 + [pl.BlockSpec((tokens, BLOCK), lambda j: (0, j))],
        out_specs=[pl.BlockSpec((ROWS, BLOCK), lambda j: (0, j))] * RING,
        scratch_shapes=[
            pltpu.VMEM((RING * ROWS, tokens), jnp.bfloat16),
            pltpu.VMEM((8 * RING, 128), jnp.float32),
        ],
        compiler_params=VMEM,
        cost_estimate=cost(RING * ROWS * tokens * width, (RING * ROWS + tokens) * width),
    )(ring, place, code, rows)


def ring_repack_kernel(z_ref, rows_ref, *refs):
    outs, flag_ref = refs[:RING], refs[RING]
    hot_ref, note_ref, place_ref, held_ref, sent_ref = refs[RING + 1 :]
    width = rows_ref.shape[2]
    step = pl.program_id(0)

    @pl.when(step == 0)
    def _():
        lane = lax.broadcasted_iota(jnp.int32, (8, 256), 1)
        before = rows_of((256, 256))
        slot = lax.broadcasted_iota(jnp.int32, (256, 256), 1)
        ahead = ((before < slot) & (((before ^ slot) & 4) == 0)).astype(jnp.bfloat16)
        over = jnp.zeros((8, 256), jnp.float32)
        for q in range(RING // 2):
            total = jnp.zeros((COLUMNS, 8, 128), jnp.float32)
            for c in range(0, width, 128):
                total += jnp.abs(
                    rows_ref[:, 8 * q : 8 * q + 8, c : c + 128].astype(jnp.float32)
                )
            filled = (total.reshape(256, 128) > 0).astype(jnp.bfloat16)
            seen = lax.dot_general(
                jnp.ones((8, 128), jnp.bfloat16), filled, NT, preferred_element_type=jnp.float32
            )
            used = seen > 0
            place = jnp.dot(
                used.astype(jnp.bfloat16), ahead, preferred_element_type=jnp.float32
            )
            over = jnp.maximum(over, jnp.where(used & (place >= ROWS - 1), 1.0, 0.0))
            place_ref[8 * q : 8 * q + 8, :] = jnp.where(
                used & (place < ROWS - 1), place, -1.0
            ).astype(jnp.int32)
        flag_ref[...] = jnp.broadcast_to(jnp.max(over, axis=1, keepdims=True), (8, 128))
        codes = (((lane >> 3) << 2) + (lane & 3) + 1).astype(jnp.float32).astype(jnp.bfloat16)
        for k in range(RING):
            plane = (z_ref[0] + k) & 7
            start = pl.multiple_of((plane >> 1) * 8, 8)
            mine = ((lane >> 2) & 1) == (plane & 1)
            place = jnp.where(mine, place_ref[pl.ds(start, 8), :], -1)[0:1, :]
            hot_ref[plane] = (rows_of((ROWS, 256)) == place).astype(jnp.bfloat16)
            note_ref[8 * k : 8 * k + 8, :] = lax.dot_general(
                codes,
                (rows_of((128, 256)) == place).astype(jnp.bfloat16),
                NT,
                preferred_element_type=jnp.float32,
            )

    first = pl.multiple_of(step * BLOCK, BLOCK)
    for q in range(RING // 2):
        rows = rows_ref[:, 8 * q : 8 * q + 8, pl.ds(first, BLOCK)].astype(jnp.float32)
        held_ref[256 * q : 256 * q + 256, :] = rows.reshape(256, BLOCK).astype(jnp.bfloat16)
    for q in range(RING // 2):
        hot = jnp.concatenate([hot_ref[2 * q], hot_ref[2 * q + 1]], axis=0)
        picked = jnp.dot(
            hot, held_ref[256 * q : 256 * q + 256, :], preferred_element_type=jnp.float32
        )
        for half in (0, 1):
            k = (2 * q + half - z_ref[0]) & 7
            sent_ref[k] = picked[half * ROWS : (half + 1) * ROWS].astype(jnp.bfloat16)
    for k in range(RING):
        outs[k][...] = sent_ref[k]

    @pl.when(step == 0)
    def _():
        for k in range(RING):
            tail = sent_ref[k, ROWS - 8 : ROWS, 0:128].astype(jnp.float32)
            note = jnp.where(rows_of((8, 128)) == 7, note_ref[8 * k : 8 * k + 8, :], 0.0)
            outs[k][ROWS - 8 : ROWS, 0:128] = (tail + note).astype(jnp.bfloat16)


def ring_repacked(z, rows):
    width = rows.shape[2]
    out = pl.pallas_call(
        ring_repack_kernel,
        out_shape=[jax.ShapeDtypeStruct((ROWS, width), jnp.bfloat16)] * RING
        + [jax.ShapeDtypeStruct((8, 128), jnp.float32)],
        grid=(width // BLOCK,),
        in_specs=[pl.BlockSpec(memory_space=pltpu.SMEM), whole(rows.shape)],
        out_specs=[pl.BlockSpec((ROWS, BLOCK), lambda j: (0, j))] * RING + [whole((8, 128))],
        scratch_shapes=[
            pltpu.VMEM((RING, ROWS, 256), jnp.bfloat16),
            pltpu.VMEM((8 * RING, 128), jnp.float32),
            pltpu.VMEM((4 * RING, 256), jnp.int32),
            pltpu.VMEM((128 * RING, BLOCK), jnp.bfloat16),
            pltpu.VMEM((RING, ROWS, BLOCK), jnp.bfloat16),
        ],
        compiler_params=VMEM,
        cost_estimate=cost(RING * ROWS * 1024 * width, (RING * ROWS + 1024) * width),
    )(z, rows)
    return out[:RING], out[RING]


def ring_spread_kernel(z_ref, *refs):
    ins, (out_ref, hot_ref, held_ref) = refs[:RING], refs[RING:]

    @pl.when(pl.program_id(0) == 0)
    def _():
        held_ref[...] = jnp.zeros_like(held_ref)
        for k in range(RING):
            code = ins[k][ROWS - 8 : ROWS, 0:128].astype(jnp.float32)[7:8, :].astype(jnp.int32)
            where = code - 1
            plane = (z_ref[0] - k) & 7
            slot = ((where >> 2) << 3) + ((plane & 1) << 2) + (where & 3)
            hot_ref[plane] = (rows_of((256, 128)) == jnp.where(code > 0, slot, -1)).astype(
                jnp.bfloat16
            )

    for k in range(RING):
        start = pl.multiple_of(((z_ref[0] - k) & 7) * 128, 128)
        held_ref[pl.ds(start, ROWS), :] = ins[k][...]
    for q in range(RING // 2):
        hot = jnp.concatenate([hot_ref[2 * q], hot_ref[2 * q + 1]], axis=1)
        picked = jnp.dot(
            hot, held_ref[256 * q : 256 * q + 256, :], preferred_element_type=jnp.float32
        )
        out_ref[:, 8 * q : 8 * q + 8, :] = picked.reshape(COLUMNS, 8, BLOCK).astype(jnp.bfloat16)


def ring_spread(z, parts):
    width = parts[0].shape[1]
    return pl.pallas_call(
        ring_spread_kernel,
        out_shape=jax.ShapeDtypeStruct((COLUMNS, CAP * RING, width), jnp.bfloat16),
        grid=(width // BLOCK,),
        in_specs=[pl.BlockSpec(memory_space=pltpu.SMEM)]
        + [pl.BlockSpec((ROWS, BLOCK), lambda j: (0, j))] * RING,
        out_specs=pl.BlockSpec((COLUMNS, CAP * RING, BLOCK), lambda j: (0, 0, j)),
        scratch_shapes=[
            pltpu.VMEM((RING, 256, 128), jnp.bfloat16),
            pltpu.VMEM((128 * RING, BLOCK), jnp.bfloat16),
        ],
        compiler_params=VMEM,
        cost_estimate=cost(1024 * 1024 * width, (1024 + ROWS * RING) * width),
    )(z, *parts)


def place_kernel(target_ref, scale_ref, rows_ref, out_ref, hot_ref, held_ref):
    @pl.when(pl.program_id(0) == 0)
    def _():
        hot_ref[...] = (rows_of(hot_ref.shape) == target_ref[...]).astype(jnp.bfloat16)
        held_ref[...] = jnp.broadcast_to(scale_ref[...], held_ref.shape)

    scale = jnp.concatenate([held_ref[...]] * (BLOCK // 128), axis=1)
    scaled = (scale * rows_ref[...].astype(jnp.float32)).astype(jnp.bfloat16)
    out_ref[...] = jnp.dot(
        hot_ref[...], scaled, preferred_element_type=jnp.float32
    ).astype(jnp.bfloat16)


def placed_rows(target, scale, rows, shard_rows, out_width):
    slots, width = rows.shape
    return pl.pallas_call(
        place_kernel,
        out_shape=jax.ShapeDtypeStruct((shard_rows, out_width), jnp.bfloat16),
        grid=(width // BLOCK,),
        in_specs=[
            whole((1, slots)),
            whole((slots, 1)),
            pl.BlockSpec((slots, BLOCK), lambda j: (0, j)),
        ],
        out_specs=pl.BlockSpec((shard_rows, BLOCK), lambda j: (0, j)),
        scratch_shapes=[
            pltpu.VMEM((shard_rows, slots), jnp.bfloat16),
            pltpu.VMEM((slots, 128), jnp.float32),
        ],
        compiler_params=VMEM,
        cost_estimate=cost(shard_rows * slots * width, (shard_rows + slots) * width),
    )(target, scale, rows)


def rounded(x):
    return x.astype(jnp.bfloat16).astype(jnp.float32)


def ring_place_kernel(z_ref, table_ref, *refs):
    ins, (_, out_ref, hot_ref, held_ref, scaled_ref) = refs[:RING], refs[RING:]

    @pl.when(pl.program_id(0) == 0)
    def _():
        scaled_ref[...] = jnp.zeros_like(scaled_ref)
        row = rows_of((8, 128))
        for k in range(RING):
            code = ins[k][ROWS - 8 : ROWS, 0:128].astype(jnp.float32)[7:8, :].astype(jnp.int32)
            plane = (z_ref[0] - k) & 7
            listed = (rows_of((128, 128)) == code - 1).astype(jnp.bfloat16)
            target = table_ref[pl.ds(plane, 1), :].astype(jnp.int32) + 1
            scale = table_ref[pl.ds(plane + RING, 1), :]
            high = rounded(scale)
            middle = rounded(scale - high)
            low = scale - high - middle
            parts = [(target >> 4).astype(jnp.float32), (target & 15).astype(jnp.float32)]
            parts += [high, middle, low]
            table = jnp.zeros((8, 128), jnp.float32)
            for r, part in enumerate(parts):
                table = jnp.where(row == r, part, table)
            found = jnp.dot(
                table.astype(jnp.bfloat16), listed, preferred_element_type=jnp.float32
            )
            place = (found[0:1, :] * 16 + found[1:2, :]).astype(jnp.int32) - 1
            hot_ref[:, 128 * k : 128 * k + 128] = (
                rows_of((out_ref.shape[0], 128)) == place
            ).astype(jnp.bfloat16)
            weight = found[2:3, :] + found[3:4, :] + found[4:5, :]
            held_ref[128 * k : 128 * k + 128, :] = jnp.broadcast_to(weight, (128, 128)).T

    for k in range(RING):
        scale = held_ref[128 * k : 128 * k + ROWS, :]
        for c in range(0, BLOCK, 128):
            rows = ins[k][:, c : c + 128].astype(jnp.float32)
            scaled_ref[128 * k : 128 * k + ROWS, c : c + 128] = (scale * rows).astype(jnp.bfloat16)
    out_ref[...] = jnp.dot(
        hot_ref[...], scaled_ref[...], preferred_element_type=jnp.float32
    ).astype(jnp.bfloat16)


def ring_placed(z, tables, parts, half_done):
    shard_rows, out_width = half_done.shape
    width = parts[0].shape[1]
    skip = (out_width - width) // BLOCK
    return pl.pallas_call(
        ring_place_kernel,
        out_shape=jax.ShapeDtypeStruct(half_done.shape, jnp.bfloat16),
        grid=(width // BLOCK,),
        in_specs=[pl.BlockSpec(memory_space=pltpu.SMEM)]
        + [whole((2 * RING, 128))]
        + [pl.BlockSpec((ROWS, BLOCK), lambda j: (0, j))] * RING
        + [pl.BlockSpec(memory_space=pl.ANY)],
        out_specs=pl.BlockSpec((shard_rows, BLOCK), lambda j: (0, skip + j)),
        scratch_shapes=[
            pltpu.VMEM((shard_rows, 128 * RING), jnp.bfloat16),
            pltpu.VMEM((128 * RING, 128), jnp.float32),
            pltpu.VMEM((128 * RING, BLOCK), jnp.bfloat16),
        ],
        input_output_aliases={2 + RING: 0},
        compiler_params=VMEM,
        cost_estimate=cost(shard_rows * 1024 * width, (shard_rows + 704) * width),
    )(z, tables, *parts, half_done)


def ring_shifted(parts):
    moved = [parts[0]]
    for k in range(1, RING):
        moved.append(lax.ppermute(parts[k], "dev_0", [(i, (i + k) % RING) for i in range(RING)]))
    return moved


def in_plane(parts):
    return lax.all_to_all(parts, PLANE, split_axis=0, concat_axis=0, tiled=True)


def by_device(table):
    rest = table.shape[1:]
    return table.reshape(4, 8, RING, *rest).swapaxes(1, 2).reshape(-1, *rest)


def by_column(table):
    rest = table.shape[1:]
    return table.reshape(4, RING, 8, *rest).swapaxes(1, 2).reshape(-1, *rest)


def count_earlier(key, counts):
    pos = jnp.arange(key.shape[0], dtype=jnp.int32)
    earlier = (pos[None, :] < pos[:, None]) & (key[None, :] == key[:, None]) & counts[None, :]
    return jnp.sum(earlier.astype(jnp.int32), axis=1)


def local(
    token_ids,
    sensitivity,
    last_hidden,
    lengths,
    norm_gain,
    reward_head,
    chosen_index,
    rejected_index,
    shard_owner,
):
    resp_local, block_len = token_ids.shape
    width = sensitivity.shape[2]
    half = width // 2
    tok_local = resp_local * block_len
    devices = shard_owner.shape[0]
    slots = devices * CAP
    shard_rows = VOCAB // devices
    responses = devices * resp_local
    cols = width // devices
    own_place = lax.axis_index(GRP_DEV)
    z = lax.axis_index("dev_0")[None]
    rows = sensitivity.reshape(tok_local, width)

    ids = token_ids.reshape(tok_local)
    shard_of = ids // shard_rows
    offset = ids - shard_of * shard_rows
    shard_hot = shard_of[:, None] == jnp.arange(devices, dtype=jnp.int32)[None, :]
    owner = jnp.sum(jnp.where(shard_hot, shard_owner[None, :], 0), axis=1)
    token_pos = jnp.arange(tok_local, dtype=jnp.int32)
    live = (jnp.arange(block_len, dtype=jnp.int32)[None, :] < lengths[:, None]).reshape(tok_local)
    rank = count_earlier(shard_of, jnp.ones_like(live))
    plane = (owner >> 3) & 7
    column = ((owner >> 6) << 3) + (owner & 7)
    place = count_earlier(plane, live)
    fits = live & (place < ROWS - 1)
    over_here = jnp.any(live & ~fits).astype(jnp.float32)
    ring = jnp.where(fits, (plane - z) & 7, -1)

    first = ring_packed(
        ring[None, :],
        place[None, :],
        (column * CAP + rank + 1).astype(jnp.float32)[None, :],
        rows,
        half,
    )
    first = ring_shifted(first)
    second_slot = jnp.where(live, (column << 5) + (plane << 2) + rank, -1)
    second = packed_rows(second_slot[None, :], rows, slots, half, half)
    second = in_plane(second.reshape(COLUMNS, CAP * RING, half))
    first[1], first[7], second = lax.optimization_barrier((first[1], first[7], second))
    second, over_there = ring_repacked(z, second)
    second = ring_shifted(second)

    code = jnp.where(live, (offset + 1) * resp_local + token_pos // block_len, 0)
    note_slot = owner * CAP + rank
    hidden = last_hidden.astype(jnp.float32)
    norm = jnp.sqrt(jnp.mean(hidden * hidden, axis=-1, keepdims=True) + 1e-05)
    own_reward = jnp.sum(hidden / norm * norm_gain * reward_head, axis=-1)
    slot_match = note_slot[None, :] == jnp.arange(slots, dtype=jnp.int32)[:, None]
    codes = jnp.sum(jnp.where(slot_match, code[None, :], 0), axis=1).reshape(devices, CAP)
    hidden_cols = hidden.reshape(resp_local, devices, cols).swapaxes(0, 1)
    own_facts = jnp.concatenate([own_reward, norm[:, 0], over_here[None]])
    ready = jnp.concatenate(
        [
            codes.astype(jnp.float32),
            jnp.broadcast_to(own_facts[None, :], (devices, 9)),
            jnp.zeros((devices, 51), jnp.float32),
            hidden_cols.reshape(devices, resp_local * cols),
        ],
        axis=1,
    )
    lane = jnp.arange(128, dtype=jnp.int32)
    message = jnp.where(lane[None, :] == 13, over_there[0:1, :], ready)
    heard = lax.all_to_all(message, GRP_DEV, split_axis=0, concat_axis=0, tiled=True)
    heard = by_column(heard)

    first = ring_spread(z, first)
    first, second[1], second[7] = lax.optimization_barrier((first, second[1], second[7]))
    first = in_plane(first)

    arrived_code = heard[:, :CAP].astype(jnp.int32)
    reward = by_device(heard[:, 4:8]).reshape(responses)
    any_over = jnp.max(heard[:, 12:14]) > 0
    margin = reward[chosen_index] - reward[rejected_index]
    push = -jax.nn.sigmoid(-margin)
    every = jnp.arange(responses, dtype=jnp.int32)
    sign_table = (chosen_index[None, :] == every[:, None]).astype(jnp.float32) - (
        rejected_index[None, :] == every[:, None]
    ).astype(jnp.float32)
    reward_grad = jnp.sum(sign_table * push[None, :], axis=1).reshape(devices, resp_local)
    reward_grad = by_column(reward_grad)
    own_gain = lax.dynamic_slice(norm_gain, (own_place * cols,), (cols,))
    head_grad = jnp.zeros((cols,), jnp.float32)
    for r in range(resp_local):
        normed = heard[:, 64 + r * cols : 64 + (r + 1) * cols] / heard[:, 8 + r : 9 + r] * own_gain
        head_grad += jnp.sum(reward_grad[:, r : r + 1] * normed, axis=0)

    response_in = arrived_code % resp_local
    scale = jnp.zeros(arrived_code.shape, jnp.float32)
    for r in range(resp_local):
        scale = jnp.where(response_in == r, reward_grad[:, r : r + 1], scale)
    target = arrived_code // resp_local - 1
    scale = jnp.where(target >= 0, scale, 0.0)
    half_done = placed_rows(
        target.reshape(1, slots),
        scale.reshape(slots, 1),
        first.reshape(slots, half),
        shard_rows,
        width,
    )

    def by_plane(table):
        return table.reshape(COLUMNS, RING, CAP).swapaxes(0, 1).reshape(RING, -1)

    tail_table = jnp.concatenate([by_plane(target).astype(jnp.float32), by_plane(scale)])

    def by_ring():
        return ring_placed(z, tail_table, second, half_done)

    def direct():
        sent = packed_rows(
            jnp.where(live, owner * CAP + rank, -1)[None, :], rows, slots, 0, width
        ).reshape(devices, CAP, width)
        arrived = lax.all_to_all(sent, GRP_DEV, split_axis=0, concat_axis=0, tiled=True)
        return placed_rows(
            by_device(target).reshape(1, slots),
            by_device(scale).reshape(slots, 1),
            arrived.reshape(slots, width),
            shard_rows,
            width,
        )

    return (lax.cond(any_over, direct, by_ring), head_grad)


def solution(mesh):
    torus = Mesh(
        mesh.devices.reshape(mesh.shape["grp"], 8, 4, 2), ("grp", "dev_0", "dev_1", "dev_2")
    )
    placed_as = (
        P(GRP_DEV, None),
        P(GRP_DEV, None, None),
        P(GRP_DEV, None),
        P(GRP_DEV),
        P(),
        P(),
        P(),
        P(),
        P(),
    )
    return jax.shard_map(
        local,
        mesh=torus,
        in_specs=placed_as,
        out_specs=(P(GRP_DEV, None), P(GRP_DEV)),
        check_vma=False,
    )
```
